32 devices in a mesh: groups: 1, ctx: 32 (over z, y, x, core).
Axes of the slice: x: 2, y: 2, z: 4, core: 2. Of those that a mesh axis runs over, the one named last changes fastest.
Arguments:
- queries: bfloat16 [4096, 2048], P(('groups', 'ctx')), may hold values from -120 to 120
- self_keys: bfloat16 [4096, 2048], P(('groups', 'ctx')), may hold values from -6 to 6
- self_values: bfloat16 [4096, 2048], P(('groups', 'ctx')), may hold values from -6 to 6
- cross_queries: bfloat16 [4096, 2048], P(('groups', 'ctx')), may hold values from -6 to 6
- encoded: bfloat16 [4096, 896], P(('groups', 'ctx')), may hold values from -6 to 6
- neighbour_weight: bfloat16 [896, 4096], replicated, may hold values from -1 to 1
- counts: int32 [64], P(('groups', 'ctx')), may hold values from 0 to 2
- sources: int32 [64, 2], P(('groups', 'ctx')), may hold values from 0 to 61, as said below
Outputs:
- attended: bfloat16 [4096, 2048], P(('groups', 'ctx'))
The draws below stay inside these ranges and needn't reach their ends.
Inputs may be any that keep to these rules, and one draw needn't show every extreme that they name: sources[c, j] equals max(c - 1 - r, 0) for some r with 1 <= r <= 29.
All inputs are finite; a program needn't handle non-finite values.
Results may differ from the reference program's by a relative error of at most 0.0061.
Values may be sent and summed in bfloat16 or wider, within the bound.
No kernel may reach another device: no remote copies, remote signals or barrier semaphores. Data moves between devices by JAX's collectives and lax.ppermute only.
A program may use at most 128 MiB of HBM per device.

```python
import jax
import jax.numpy as jnp
from jax import lax

HEADS = 16
HEAD_DIM = 128
WIDTH = 2048
ENC = 896
SPAN = 64
WINDOW = 2048
CH_DEV = 2
TOK_DEV = 128
REACH = 16
TOKENS = 4096
SPANS = 64


def paired_rows(key):
    key_rows = jax.random.truncated_normal(jax.random.fold_in(key, 11), -6.0, 6.0, (TOKENS, WIDTH), jnp.float32)
    query_rows = jax.random.truncated_normal(jax.random.fold_in(key, 12), -6.0, 6.0, (TOKENS, WIDTH), jnp.float32)
    return (key_rows, query_rows)


def draw_queries(key, part):
    key_rows, query_rows = paired_rows(key)
    return query_rows.astype(jnp.bfloat16)


def draw_self_keys(key, part):
    key_rows, query_rows = paired_rows(key)
    return key_rows.astype(jnp.bfloat16)


def draw_neighbour_weight(key, part):
    base = jax.random.truncated_normal(jax.random.fold_in(key, 41), -4.0, 4.0, (ENC, 2 * WIDTH), jnp.float32) * ENC ** (-0.5)
    return base.astype(jnp.bfloat16)


def draw_encoded(key, part):
    rows = jax.random.truncated_normal(jax.random.fold_in(key, 21), -6.0, 6.0, (TOKENS, ENC), jnp.float32)
    return rows.astype(jnp.bfloat16)


def draw_cross_queries(key, part):
    rows = jax.random.truncated_normal(jax.random.fold_in(key, 31), -6.0, 6.0, (TOKENS, WIDTH), jnp.float32)
    return rows.astype(jnp.bfloat16)


def draw_sources(key, part):
    span_ids = jnp.arange(SPANS, dtype=jnp.int32)[:, None]
    backward = jax.random.randint(key, (SPANS, 2), 1, (REACH - 1) * CH_DEV, dtype=jnp.int32)
    row_ids = jnp.arange(SPANS, dtype=jnp.int32)[:, None]
    slot_ids = jnp.arange(2, dtype=jnp.int32)[None, :]
    nearest = (row_ids == SPANS - 1) & (slot_ids == 0)
    backward = jnp.where(nearest, 1, backward)
    return jnp.maximum(span_ids - 1 - backward, 0)


def touch_ends(drawn, rng, least, high):
    longest = drawn.shape.index(max(drawn.shape))
    spots = []
    for shift in (0, 1):
        where = [jax.random.randint(jax.random.fold_in(rng, axis), (), 0, length) for axis, length in enumerate(drawn.shape)]
        where[longest] = (where[longest] + shift) % drawn.shape[longest]
        spots.append(tuple(where))
    return drawn.at[spots[0]].set(least).at[spots[1]].set(high)


def shard_levels(stream_key, shape, cuts, smallest, top_value):
    factor_of, own = 1.0, jax.random.fold_in(stream_key, 6)
    for dim, parts in cuts:
        draws = jnp.exp(jax.random.uniform(jax.random.fold_in(own, dim), (parts,), jnp.float32, smallest / len(cuts), top_value / len(cuts)))
        factor_of = factor_of * jnp.repeat(draws, shape[dim] // parts).reshape([-1 if axis == dim else 1 for axis in range(len(shape))])
    return factor_of


def centred(stream_key, dims, scale, reach, cuts=(), held_as=jnp.bfloat16):
    loudness = shard_levels(stream_key, dims, cuts, -0.22, 0.18) if cuts else 1.0
    result = jax.random.normal(stream_key, dims, jnp.float32) * scale * loudness
    return jnp.minimum(jnp.maximum(result, -reach), reach).astype(held_as)


def setup_inputs(seed: int = 0, part: int = 0) -> dict:
    arg_keys = jax.random.split(jax.random.key(seed), 9)
    part_splits = jax.random.split(jax.random.fold_in(arg_keys[8], part), 9)
    queries = draw_queries(jax.random.fold_in(jax.random.fold_in(arg_keys[8], part), 71), part)
    self_keys = draw_self_keys(jax.random.fold_in(jax.random.fold_in(arg_keys[8], part), 71), part)
    self_values = centred(part_splits[2], (TOKENS, WIDTH), 1.0, 6.0, ((0, 32),))
    cross_queries = draw_cross_queries(jax.random.fold_in(jax.random.fold_in(arg_keys[8], part), 71), part)
    encoded = draw_encoded(jax.random.fold_in(jax.random.fold_in(arg_keys[8], part), 71), part)
    neighbour_weight = draw_neighbour_weight(jax.random.fold_in(arg_keys[8], 71), part)
    counts = touch_ends(jax.random.randint(part_splits[6], (SPANS,), 0, 3), jax.random.fold_in(part_splits[6], 1), 0, 2).astype(jnp.int32)
    sources = draw_sources(jax.random.fold_in(jax.random.fold_in(arg_keys[8], part), 71), part)
    return {"queries": queries, "self_keys": self_keys, "self_values": self_values, "cross_queries": cross_queries, "encoded": encoded, "neighbour_weight": neighbour_weight, "counts": counts, "sources": sources}


MASKED_SCORE = -1.0e30


def masked_weights(scores, valid_mask, extra_total):
    masked = jnp.where(valid_mask, scores, MASKED_SCORE)
    largest = jnp.max(masked, axis=-1, keepdims=True)
    exponent = jnp.where(valid_mask, jnp.exp(masked - largest), 0.0)
    totals = jnp.sum(exponent, axis=-1, keepdims=True)
    return (exponent / (totals + extra_total)).astype(jnp.bfloat16)


def reference(queries, self_keys, self_values, cross_queries, encoded, neighbour_weight, counts, sources):
    scale_factor = HEAD_DIM ** -0.5
    padding = jnp.zeros((WINDOW, WIDTH), jnp.bfloat16)
    keys_padded = jnp.concatenate([padding, self_keys], axis=0)
    values_padded = jnp.concatenate([padding, self_values], axis=0)
    query_index = jnp.arange(TOK_DEV, dtype=jnp.int32)[:, None]
    key_index = jnp.arange(WINDOW + TOK_DEV, dtype=jnp.int32)[None, :]

    def self_block(block_index):
        block_start = (block_index * TOK_DEV).astype(jnp.int32)
        query_block = lax.dynamic_slice_in_dim(queries, block_start, TOK_DEV, 0).reshape(TOK_DEV, HEADS, HEAD_DIM).astype(jnp.float32)
        key_block = lax.dynamic_slice_in_dim(keys_padded, block_start, WINDOW + TOK_DEV, 0).reshape(WINDOW + TOK_DEV, HEADS, HEAD_DIM).astype(jnp.float32)
        value_block = lax.dynamic_slice_in_dim(values_padded, block_start, WINDOW + TOK_DEV, 0).reshape(WINDOW + TOK_DEV, HEADS, HEAD_DIM).astype(jnp.float32)
        scores = jnp.einsum("rhd,ihd->hri", query_block, key_block) * scale_factor
        valid_mask = (key_index > query_index) & (key_index <= query_index + WINDOW) & (key_index >= WINDOW - block_start)
        weights = masked_weights(scores, valid_mask[None], 0.0)
        weights = lax.optimization_barrier(weights).astype(jnp.float32)
        return jnp.einsum("hri,ihd->rhd", weights, value_block).reshape(TOK_DEV, WIDTH)

    self_part = lax.map(self_block, jnp.arange(TOKENS // TOK_DEV, dtype=jnp.int32)).reshape(TOKENS, WIDTH)

    projected = jnp.dot(encoded, neighbour_weight, preferred_element_type=jnp.float32).astype(jnp.bfloat16)
    slot_index = jnp.arange(4 * SPAN, dtype=jnp.int32) // (2 * SPAN)

    def cross_span(span_index):
        previous = jnp.maximum(span_index - 1, 0).astype(jnp.int32)
        neighbour_count = jnp.where(span_index > 0, counts[previous], 0)
        span_sources = sources[previous]
        pieces = [lax.dynamic_slice_in_dim(projected, (span_sources[slot] * SPAN).astype(jnp.int32), 2 * SPAN, 0) for slot in range(2)]
        neighbour_rows = jnp.concatenate(pieces, axis=0)
        neighbour_keys = neighbour_rows[:, :WIDTH].reshape(4 * SPAN, HEADS, HEAD_DIM).astype(jnp.float32)
        neighbour_values = neighbour_rows[:, WIDTH:].reshape(4 * SPAN, HEADS, HEAD_DIM).astype(jnp.float32)
        query_block = lax.dynamic_slice_in_dim(cross_queries, (span_index * SPAN).astype(jnp.int32), SPAN, 0).reshape(SPAN, HEADS, HEAD_DIM).astype(jnp.float32)
        scores = jnp.einsum("qhd,khd->hqk", query_block, neighbour_keys) * scale_factor
        valid_mask = (slot_index < neighbour_count)[None, None, :]
        extra_total = jnp.where(neighbour_count > 0, 0.0, 1.0)
        weights = masked_weights(scores, valid_mask, extra_total)
        weights = lax.optimization_barrier(weights).astype(jnp.float32)
        return jnp.einsum("hqk,khd->qhd", weights, neighbour_values).reshape(SPAN, WIDTH)

    cross_part = lax.map(cross_span, jnp.arange(SPANS, dtype=jnp.int32)).reshape(TOKENS, WIDTH)
    return (self_part + cross_part).astype(jnp.bfloat16)
```

```python
import functools

import jax
import jax.numpy as jnp
from jax import lax
from jax.experimental import pallas as pl
from jax.experimental.pallas import tpu as pltpu
from jax.sharding import PartitionSpec as P

HEADS = 16
HEAD_DIM = 128
SPAN = 64
REACH = 16
PLANE = 8

MASKED_SCORE = -1e30
LOG2E = 1.4426950408889634


def shifted(value, axis, steps):
    count = lax.axis_size(axis)
    first, last = (max(0, -steps), min(count, count - steps))
    return lax.ppermute(value, axis, [(source, source + steps) for source in range(first, last)])


def swapped(value, axis, bit):
    count = lax.axis_size(axis)
    return lax.ppermute(value, axis, [(source, source ^ bit) for source in range(count)])


def pack_kernel(q_ref, k_ref, v_ref, out_ref):
    rows = q_ref.shape[0]
    for head in range(q_ref.shape[1] // HEAD_DIM):
        columns = slice(head * HEAD_DIM, (head + 1) * HEAD_DIM)
        out_ref[head, 0:rows, :] = q_ref[:, columns]
        out_ref[head, rows : 2 * rows, :] = k_ref[:, columns]
        out_ref[head, 2 * rows : 3 * rows, :] = v_ref[:, columns]


def packed(queries, keys, values):
    rows, width = queries.shape
    return pl.pallas_call(
        pack_kernel,
        out_shape=jax.ShapeDtypeStruct((width // HEAD_DIM, 3 * rows, HEAD_DIM), queries.dtype),
        name="pack",
    )(queries, keys, values)


def scores_of(q, k):
    return lax.dot_general(q, k, (((1,), (1,)), ((), ())), preferred_element_type=jnp.float32)


def softmax_parts(q, pieces, scale):
    scores = []
    for k, _, mask in pieces:
        s = scores_of(q, k)
        scores.append(s if mask is None else jnp.where(mask, s, MASKED_SCORE))
    largest = functools.reduce(
        jnp.maximum, [jnp.max(s, axis=1, keepdims=True) for s in scores]
    )
    total, out = None, None
    for s, (_, v, _) in zip(scores, pieces):
        p = jnp.exp2((s - largest) * scale)
        t = jnp.sum(p, axis=1, keepdims=True)
        o = jnp.dot(p.astype(jnp.bfloat16), v, preferred_element_type=jnp.float32)
        total = t if total is None else total + t
        out = o if out is None else out + o
    return out, largest, total


def with_stats(largest, total, rows):
    lane = lax.broadcasted_iota(jnp.int32, (rows, 128), 1)
    return jnp.where(lane < 64, largest, total)


def own_kernel(scale, x_ref, out_ref, stat_ref):
    blocks, triple, dim = x_ref.shape
    rows = triple // 3
    size = 2 * rows
    row = lax.broadcasted_iota(jnp.int32, (size, size), 0)
    column = lax.broadcasted_iota(jnp.int32, (size, size), 1)
    causal = column <= row

    def take(first, count, which):
        return x_ref[first : first + count, which * rows : (which + 1) * rows, :].reshape(
            count * rows, dim
        )

    for i in range(blocks // 2):
        q = take(2 * i, 2, 0)
        pieces = [(take(2 * i, 2, 1), take(2 * i, 2, 2), causal)]
        if i:
            pieces.append((take(0, 2 * i, 1), take(0, 2 * i, 2), None))
        out, largest, total = softmax_parts(q, pieces, scale)
        out_ref[2 * i : 2 * i + 2] = out.reshape(2, rows, dim)
        stat_ref[2 * i : 2 * i + 2] = with_stats(largest, total, size).reshape(2, rows, 128)


def previous_kernel(scale, flag_ref, x_ref, kv_ref, out1_ref, stat_ref, out_ref):
    blocks, triple, dim = x_ref.shape
    rows = triple // 3
    size = 2 * rows
    row = lax.broadcasted_iota(jnp.int32, (size, size), 0)
    column = lax.broadcasted_iota(jnp.int32, (size, size), 1)
    later = column > row

    def take(first, count, which):
        return kv_ref[first : first + count, which * rows : (which + 1) * rows, :].reshape(
            count * rows, dim
        )

    @pl.when(flag_ref[0] > 0)
    def _():
        for i in range(blocks // 2):
            q = x_ref[2 * i : 2 * i + 2, 0:rows, :].reshape(size, dim)
            pieces = [(take(2 * i, 2, 0), take(2 * i, 2, 1), later)]
            rest = blocks - 2 * i - 2
            if rest:
                pieces.append((take(2 * i + 2, rest, 0), take(2 * i + 2, rest, 1), None))
            out, largest, total = softmax_parts(q, pieces, scale)
            stat = stat_ref[2 * i : 2 * i + 2].reshape(size, 128)
            largest1, total1 = stat[:, 0:1], stat[:, 64:65]
            out1 = out1_ref[2 * i : 2 * i + 2].reshape(size, dim)
            top = jnp.maximum(largest, largest1)
            a, b = jnp.exp2((largest - top) * scale), jnp.exp2((largest1 - top) * scale)
            merged = (out * a + out1 * b) / (total * a + total1 * b)
            out_ref[2 * i : 2 * i + 2] = merged.reshape(2, rows, dim).astype(out_ref.dtype)

    @pl.when(flag_ref[0] == 0)
    def _():
        for i in range(blocks // 2):
            stat = stat_ref[2 * i : 2 * i + 2].reshape(size, 128)
            out1 = out1_ref[2 * i : 2 * i + 2].reshape(size, dim)
            merged = out1 / stat[:, 64:65]
            out_ref[2 * i : 2 * i + 2] = merged.reshape(2, rows, dim).astype(out_ref.dtype)


def self_attention(queries, keys, values, chunk, groups):
    rows, width = queries.shape
    heads = width // HEAD_DIM
    scale = HEAD_DIM ** (-0.5) * LOG2E
    x = lax.all_to_all(
        packed(queries, keys, values), "ctx", 0, 0, axis_index_groups=groups, tiled=True
    )
    arriving = shifted(x[:, rows:, :], "ctx", heads)
    area = (heads * rows) ** 2 // 2
    cost = pl.CostEstimate(
        flops=4 * HEAD_DIM * area, bytes_accessed=4 * x.size, transcendentals=area
    )
    out1, stat = pl.pallas_call(
        functools.partial(own_kernel, scale),
        out_shape=(
            jax.ShapeDtypeStruct((heads, rows, HEAD_DIM), jnp.float32),
            jax.ShapeDtypeStruct((heads, rows, 128), jnp.float32),
        ),
        cost_estimate=cost,
        name="own",
    )(x)
    vmem = pl.BlockSpec(memory_space=pltpu.VMEM)
    return pl.pallas_call(
        functools.partial(previous_kernel, scale),
        out_shape=jax.ShapeDtypeStruct((heads, rows, HEAD_DIM), jnp.bfloat16),
        in_specs=[pl.BlockSpec(memory_space=pltpu.SMEM), vmem, vmem, vmem, vmem],
        cost_estimate=cost,
        name="previous",
    )(chunk.reshape(1), x, arriving, out1, stat)


def cross_kernel(
    scale,
    span_count,
    piece_ref,
    count_ref,
    window_ref,
    q_ref,
    wk_ref,
    wv_ref,
    out_ref,
    rows_ref,
):
    span = q_ref.shape[0] // span_count
    keys_of_span = rows_ref.shape[0] // span_count
    pieces = rows_ref.shape[0] // span

    @pl.when(pl.program_id(0) == 0)
    def _():
        for n in range(pieces):
            start = pl.multiple_of(piece_ref[n], span)
            rows_ref[n * span : (n + 1) * span, :] = window_ref[pl.ds(start, span), :]

    rows = rows_ref[...]
    keys = jnp.dot(rows, wk_ref[...], preferred_element_type=jnp.float32).astype(jnp.bfloat16)
    values = jnp.dot(rows, wv_ref[...], preferred_element_type=jnp.float32).astype(jnp.bfloat16)
    slot = lax.broadcasted_iota(jnp.int32, (span, keys_of_span), 1) // (2 * span)
    for c in range(span_count):
        valid = slot < count_ref[c]
        none = jnp.where(count_ref[c] > 0, 0.0, 1.0)
        here = slice(c * keys_of_span, (c + 1) * keys_of_span)
        for h in range(q_ref.shape[1] // HEAD_DIM):
            lanes = slice(h * HEAD_DIM, (h + 1) * HEAD_DIM)
            s = scores_of(q_ref[c * span : (c + 1) * span, lanes], keys[here, lanes])
            s = jnp.where(valid, s, MASKED_SCORE)
            largest = jnp.max(s, axis=1, keepdims=True)
            p = jnp.where(valid, jnp.exp2((s - largest) * scale), 0.0)
            total = jnp.sum(p, axis=1, keepdims=True) + none
            o = jnp.dot(
                (p / total).astype(jnp.bfloat16),
                values[here, lanes],
                preferred_element_type=jnp.float32,
            )
            out_ref[c * span : (c + 1) * span, lanes] = o


def cross_attention(cross_queries, encoded, weight, counts, sources, position):
    rows, width = cross_queries.shape
    span_count = counts.shape[0]
    depth = encoded.shape[1]
    core, place = position % 2, position % PLANE
    one_back = shifted(encoded, "ctx", PLANE)
    two_back = shifted(one_back, "ctx", PLANE)

    def pick(bit):
        other = jnp.where(place < (place ^ bit), encoded, two_back)
        return jnp.concatenate([one_back, other], axis=0)

    near = [swapped(pick(bit), "ctx", bit) for bit in (2, 4, 6)]
    far = swapped(jnp.concatenate([pick(1)] + near, axis=0), "ctx", 1)
    own = jnp.concatenate([one_back, jnp.where(position < 2 * PLANE, encoded, two_back)], axis=0)
    window = jnp.concatenate([own] + near + [far], axis=0)

    index = jnp.concatenate([counts[-1:], sources[-1]])
    before = shifted(index, "ctx", 1)
    count_rows = jnp.concatenate([before[:1], counts[:-1]])
    source_rows = jnp.concatenate([before[1:][None], sources[:-1]], axis=0)
    spans = (source_rows[:, :, None] + jnp.arange(2, dtype=jnp.int32)).reshape(-1)
    block, half = spans // span_count, spans % span_count
    relative = (block % PLANE) ^ place
    column = (relative % 2) * (PLANE // 2) + relative // 2
    which = jnp.where(block // PLANE == position // PLANE - 1, 0, 1)
    pieces = (column * 2 + which) * rows + half * SPAN

    pair = 2 * HEAD_DIM
    steps = width // pair
    picked = span_count * 4 * SPAN
    cost = pl.CostEstimate(
        flops=2 * picked * depth * 2 * width,
        bytes_accessed=weight.size * 2 + window.size * 2,
        transcendentals=picked * SPAN * HEADS,
    )
    return pl.pallas_call(
        functools.partial(cross_kernel, HEAD_DIM ** (-0.5) * LOG2E, span_count),
        out_shape=jax.ShapeDtypeStruct((rows, width), jnp.float32),
        grid_spec=pltpu.PrefetchScalarGridSpec(
            num_scalar_prefetch=2,
            grid=(steps,),
            in_specs=[
                pl.BlockSpec(window.shape, lambda g, *_: (0, 0), pipeline_mode=pl.Buffered(1)),
                pl.BlockSpec((rows, pair), lambda g, *_: (0, g)),
                pl.BlockSpec((depth, pair), lambda g, *_: (0, g)),
                pl.BlockSpec((depth, pair), lambda g, *_: (0, g + steps)),
            ],
            out_specs=pl.BlockSpec((rows, pair), lambda g, *_: (0, g)),
            scratch_shapes=[pltpu.VMEM((picked, depth), encoded.dtype)],
        ),
        cost_estimate=cost,
        name="cross",
    )(pieces, count_rows, window, cross_queries, weight, weight)


def sum_kernel(self_ref, cross_ref, out_ref):
    for head in range(self_ref.shape[0]):
        lanes = slice(head * HEAD_DIM, (head + 1) * HEAD_DIM)
        out_ref[:, lanes] = (self_ref[head].astype(jnp.float32) + cross_ref[:, lanes]).astype(
            out_ref.dtype
        )


def per_device(
    queries, self_keys, self_values, cross_queries, encoded, neighbour_weight, counts, sources
):
    position = lax.axis_index("ctx")
    count = lax.axis_size("ctx")
    groups = [list(range(first, first + HEADS)) for first in range(0, count, HEADS)]
    cross_part = cross_attention(
        cross_queries, encoded, neighbour_weight, counts, sources, position
    )
    by_head = self_attention(queries, self_keys, self_values, position // HEADS, groups)
    self_part = lax.all_to_all(by_head, "ctx", 0, 0, axis_index_groups=groups, tiled=True)
    return pl.pallas_call(
        sum_kernel,
        out_shape=jax.ShapeDtypeStruct(queries.shape, jnp.bfloat16),
        name="total",
    )(self_part, cross_part)


def solution(mesh):
    return jax.shard_map(
        per_device,
        mesh=mesh,
        in_specs=(
            P(("groups", "ctx"), None),
            P(("groups", "ctx"), None),
            P(("groups", "ctx"), None),
            P(("groups", "ctx"), None),
            P(("groups", "ctx"), None),
            P(),
            P(("groups", "ctx")),
            P(("groups", "ctx"), None),
        ),
        out_specs=P(("groups", "ctx"), None),
        check_vma=False,
    )
```

```python
import functools

import jax
import jax.numpy as jnp
from jax import lax
from jax.experimental import pallas as pl
from jax.experimental.pallas import tpu as pltpu
from jax.sharding import PartitionSpec as P


HEADS = 16
HEAD_DIM = 128
SPAN = 64
PLANE = 8
LEFT = 6

MASKED_SCORE = -1e30
LOG2E = 1.4426950408889634


def shifted(value, axis, steps):
    count = lax.axis_size(axis)
    first, last = (max(0, -steps), min(count, count - steps))
    return lax.ppermute(value, axis, [(source, source + steps) for source in range(first, last)])


def swapped(value, axis, bit):
    count = lax.axis_size(axis)
    return lax.ppermute(value, axis, [(source, source ^ bit) for source in range(count)])


def pack_kernel(*refs):
    *in_refs, out_ref = refs
    rows = in_refs[0].shape[0]
    for head in range(out_ref.shape[0]):
        columns = slice(head * HEAD_DIM, (head + 1) * HEAD_DIM)
        for n, ref in enumerate(in_refs):
            out_ref[head, n * rows : (n + 1) * rows, :] = ref[:, columns]


def packed(*arrays):
    rows, width = arrays[0].shape
    return pl.pallas_call(
        pack_kernel,
        out_shape=jax.ShapeDtypeStruct(
            (width // HEAD_DIM, len(arrays) * rows, HEAD_DIM), arrays[0].dtype
        ),
        cost_estimate=pl.CostEstimate(
            flops=0, bytes_accessed=4 * len(arrays) * rows * width, transcendentals=0
        ),
        name="pack",
    )(*arrays)


def scores_of(q, k):
    return lax.dot_general(q, k, (((1,), (1,)), ((), ())), preferred_element_type=jnp.float32)


def softmax_parts(q, pieces, scale):
    scores = []
    for k, _, mask in pieces:
        s = scores_of(q, k)
        scores.append(s if mask is None else jnp.where(mask, s, MASKED_SCORE))
    largest = functools.reduce(
        jnp.maximum, [jnp.max(s, axis=1, keepdims=True) for s in scores]
    )
    total, out = None, None
    for s, (_, v, _) in zip(scores, pieces):
        p = jnp.exp2((s - largest) * scale)
        t = jnp.sum(p, axis=1, keepdims=True)
        o = jnp.dot(p.astype(jnp.bfloat16), v, preferred_element_type=jnp.float32)
        total = t if total is None else total + t
        out = o if out is None else out + o
    return out, largest, total


def with_stats(largest, total):
    lane = lax.broadcasted_iota(jnp.int32, (largest.shape[0], 128), 1)
    return jnp.where(lane < 64, largest, total)


def halves(stat):
    return stat[:, 0:1], stat[:, 64:65]


def thirds(x):
    high = x.astype(jnp.bfloat16)
    rest = x - high.astype(jnp.float32)
    middle = rest.astype(jnp.bfloat16)
    low = (rest - middle.astype(jnp.float32)).astype(jnp.bfloat16)
    return high, middle, low


def taken(ref, first, count, start, rows):
    return ref[first : first + count, start : start + rows, :].reshape(count * rows, ref.shape[2])


def triangle(size, keep):
    row = lax.broadcasted_iota(jnp.int32, (size, size), 0)
    column = lax.broadcasted_iota(jnp.int32, (size, size), 1)
    return keep(column, row)


def own_kernel(scale, q_ref, kv_ref, out_ref, stat_ref):
    blocks, rows, dim = q_ref.shape
    causal = triangle(2 * rows, lambda column, row: column <= row)
    for i in range(0, blocks, 2):
        pieces = [(taken(kv_ref, i, 2, 0, rows), taken(kv_ref, i, 2, rows, rows), causal)]
        if i:
            pieces.append((taken(kv_ref, 0, i, 0, rows), taken(kv_ref, 0, i, rows, rows), None))
        out, largest, total = softmax_parts(taken(q_ref, i, 2, 0, rows), pieces, scale)
        out_ref[i : i + 2] = out.reshape(2, rows, dim)
        stat_ref[i : i + 2] = with_stats(largest, total).reshape(2, rows, 128)


def later_kernel(scale, q_ref, kv_ref, out_ref):
    blocks, rows, dim = q_ref.shape
    later = triangle(2 * rows, lambda column, row: column > row)
    out_ref[blocks] = jnp.zeros((rows, dim), out_ref.dtype)
    for i in range(0, blocks, 2):
        pieces = [(taken(kv_ref, i, 2, 0, rows), taken(kv_ref, i, 2, rows, rows), later)]
        rest = blocks - i - 2
        if rest:
            pieces.append(
                (taken(kv_ref, i + 2, rest, 0, rows), taken(kv_ref, i + 2, rest, rows, rows), None)
            )
        out, largest, total = softmax_parts(taken(q_ref, i, 2, 0, rows), pieces, scale)
        out_ref[i : i + 2] = out.reshape(2, rows, dim).astype(out_ref.dtype)
        stat = with_stats(largest, total)
        for n in range(2):
            turned = stat[n * rows : (n + 1) * rows].T
            for m, row in enumerate((turned[0:1], turned[64:65])):
                for k, part in enumerate(thirds(row)):
                    place = ((i + n) * 2 + m) * 3 + k
                    out_ref[blocks, place : place + 1, :] = part


def sent_stats(ref, block, rows):
    values = []
    for m in range(2):
        place = (block * 2 + m) * 3
        three = ref[ref.shape[0] - 1, place : place + 3, :].astype(jnp.float32)
        values.append(three[0:1] + three[1:2] + three[2:3])
    sublane = lax.broadcasted_iota(jnp.int32, (rows, 128), 0)
    return jnp.where(sublane < 64, values[0], values[1]).T


def previous_kernel(scale, flag_ref, q_ref, kv_ref, back_ref, out1_ref, stat_ref, out_ref):
    blocks, rows, dim = q_ref.shape
    sent = back_ref.shape[0] - 1
    later = triangle(2 * rows, lambda column, row: column > row)

    def store(i, parts):
        top = functools.reduce(jnp.maximum, [largest for _, largest, _ in parts])
        weights = [jnp.exp2((largest - top) * scale) for _, largest, _ in parts]
        inverse = 1.0 / sum(w * total for w, (_, _, total) in zip(weights, parts))
        merged = sum((w * inverse) * out for w, (out, _, _) in zip(weights, parts))
        out_ref[i : i + 2] = merged.reshape(2, rows, dim).astype(out_ref.dtype)

    def own_part(i):
        stat = stat_ref[i : i + 2].reshape(2 * rows, 128)
        return (out1_ref[i : i + 2].reshape(2 * rows, dim), *halves(stat))

    @pl.when(flag_ref[0] > 0)
    def _():
        for i in range(0, blocks, 2):
            pieces = []
            first = max(i - sent, 0)
            if i >= sent:
                pieces.append(
                    (taken(kv_ref, first, 2, 0, rows), taken(kv_ref, first, 2, rows, rows), later)
                )
                first += 2
            rest = kv_ref.shape[0] - first
            if rest:
                pieces.append(
                    (
                        taken(kv_ref, first, rest, 0, rows),
                        taken(kv_ref, first, rest, rows, rows),
                        None,
                    )
                )
            parts = [softmax_parts(taken(q_ref, i, 2, 0, rows), pieces, scale), own_part(i)]
            if i < sent:
                stat = jnp.concatenate([sent_stats(back_ref, i + n, rows) for n in range(2)], axis=0)
                parts.append((taken(back_ref, i, 2, 0, rows).astype(jnp.float32), *halves(stat)))
            store(i, parts)

    @pl.when(flag_ref[0] == 0)
    def _():
        for i in range(0, blocks, 2):
            store(i, [own_part(i)])


def estimate(area, arrays):
    return pl.CostEstimate(
        flops=4 * HEAD_DIM * area,
        bytes_accessed=sum(2 * a.size for a in arrays),
        transcendentals=area,
    )


def self_attention(queries, keys, values, chunk, groups):
    rows, width = queries.shape
    heads = width // HEAD_DIM
    scale = HEAD_DIM ** (-0.5) * LOG2E
    kv = lax.all_to_all(
        packed(keys, values), "ctx", 0, 0, axis_index_groups=groups, tiled=True
    )
    q = lax.all_to_all(packed(queries), "ctx", 0, 0, axis_index_groups=groups, tiled=True)
    arriving = shifted(kv[LEFT:], "ctx", heads)
    asked = shifted(q[:LEFT], "ctx", -heads)
    area = (heads * rows) ** 2 // 2
    small = (LEFT * rows) ** 2 // 2
    out1, stat = pl.pallas_call(
        functools.partial(own_kernel, scale),
        out_shape=(
            jax.ShapeDtypeStruct((heads, rows, HEAD_DIM), jnp.float32),
            jax.ShapeDtypeStruct((heads, rows, 128), jnp.float32),
        ),
        cost_estimate=estimate(area, (q, kv)),
        name="own",
    )(q, kv)
    answer = pl.pallas_call(
        functools.partial(later_kernel, scale),
        out_shape=jax.ShapeDtypeStruct((LEFT + 1, rows, HEAD_DIM), jnp.bfloat16),
        cost_estimate=estimate(small, (asked,)),
        name="later",
    )(asked, kv[:LEFT])
    back = shifted(answer, "ctx", heads)
    vmem = pl.BlockSpec(memory_space=pltpu.VMEM)
    return pl.pallas_call(
        functools.partial(previous_kernel, scale),
        out_shape=jax.ShapeDtypeStruct((heads, rows, HEAD_DIM), jnp.bfloat16),
        in_specs=[pl.BlockSpec(memory_space=pltpu.SMEM)] + [vmem] * 5,
        cost_estimate=estimate(area - small, (q, kv, out1, stat)),
        name="previous",
    )(chunk.reshape(1), q, arriving, back, out1, stat)


def gather_kernel(mine_ref, theirs_ref, *refs):
    *in_refs, mine_out, theirs_out, window_ref = refs
    start = 0
    for ref in in_refs:
        window_ref[start : start + ref.shape[0], :] = ref[...]
        start += ref.shape[0]
    for piece_ref, out_ref in ((mine_ref, mine_out), (theirs_ref, theirs_out)):
        pieces = piece_ref.shape[0]
        size = out_ref.shape[0] // pieces
        for n in range(pieces):
            place = pl.multiple_of(piece_ref[n], size)
            out_ref[n * size : (n + 1) * size, :] = window_ref[pl.ds(place, size), :]


def cross_kernel(
    scale, span_count, here_ref, count_ref, mine_ref, theirs_ref, q_ref, wk_ref, wv_ref, out_ref, rows_ref
):
    span = q_ref.shape[0] // span_count
    keys_of_span = rows_ref.shape[0] // span_count
    pieces = rows_ref.shape[0] // span

    @pl.when(pl.program_id(0) == 0)
    def _():
        for n in range(pieces):
            place = slice(n * span, (n + 1) * span)

            @pl.when(here_ref[n] > 0)
            def _():
                rows_ref[place, :] = mine_ref[place, :]

            @pl.when(here_ref[n] == 0)
            def _():
                rows_ref[place, :] = theirs_ref[place, :]

    rows = rows_ref[...]
    keys = jnp.dot(rows, wk_ref[...], preferred_element_type=jnp.float32).astype(jnp.bfloat16)
    values = jnp.dot(rows, wv_ref[...], preferred_element_type=jnp.float32).astype(jnp.bfloat16)
    slot = lax.broadcasted_iota(jnp.int32, (span, keys_of_span), 1) // (2 * span)
    for c in range(span_count):
        valid = slot < count_ref[c]
        none = jnp.where(count_ref[c] > 0, 0.0, 1.0)
        here = slice(c * keys_of_span, (c + 1) * keys_of_span)
        for h in range(q_ref.shape[1] // HEAD_DIM):
            lanes = slice(h * HEAD_DIM, (h + 1) * HEAD_DIM)
            s = scores_of(q_ref[c * span : (c + 1) * span, lanes], keys[here, lanes])
            s = jnp.where(valid, s, MASKED_SCORE)
            largest = jnp.max(s, axis=1, keepdims=True)
            p = jnp.where(valid, jnp.exp2((s - largest) * scale), 0.0)
            total = jnp.sum(p, axis=1, keepdims=True) + none
            o = jnp.dot(
                p.astype(jnp.bfloat16), values[here, lanes], preferred_element_type=jnp.float32
            )
            out_ref[c * span : (c + 1) * span, lanes] = o * (1.0 / total)


def cross_attention(cross_queries, encoded, weight, counts, sources, position):
    rows, width = cross_queries.shape
    span_count = counts.shape[0]
    depth = encoded.shape[1]
    place, plane = position % PLANE, position // PLANE
    one_back = shifted(encoded, "ctx", PLANE)
    before = shifted(jnp.concatenate([counts[-1:], sources[-1]]), "ctx", 1)
    count_rows = jnp.concatenate([before[:1], counts[:-1]])
    source_rows = jnp.concatenate([before[1:][None], sources[:-1]], axis=0)
    spans = (source_rows[:, :, None] + jnp.arange(2, dtype=jnp.int32)).reshape(-1)
    their_spans = swapped(spans, "ctx", 1)
    two_back = shifted(one_back, "ctx", PLANE)

    near = []
    for bit in (2, 4, 6):
        other = jnp.where(place < (place ^ bit), encoded, two_back)
        near.append(swapped(jnp.concatenate([one_back, other], axis=0), "ctx", bit))

    def places(wanted):
        block, half = wanted // span_count, wanted % span_count
        relative = (block % PLANE) ^ place
        away = plane - block // PLANE
        column = relative // 2
        slot = jnp.where(column == 0, away, 1 + 2 * column + jnp.where(away == 1, 0, 1))
        start = jnp.where(relative % 2 == 0, slot * rows + half * SPAN, 0)
        return jnp.clip(start, 0, 9 * rows - SPAN), (relative % 2 == 0).astype(jnp.int32)

    my_places, here = places(spans)
    picked = span_count * 4 * SPAN
    smem, vmem = (pl.BlockSpec(memory_space=m) for m in (pltpu.SMEM, pltpu.VMEM))
    mine, theirs = pl.pallas_call(
        gather_kernel,
        out_shape=(jax.ShapeDtypeStruct((picked, depth), encoded.dtype),) * 2,
        in_specs=[smem] * 2 + [vmem] * 6,
        scratch_shapes=[pltpu.VMEM((9 * rows, depth), encoded.dtype)],
        cost_estimate=pl.CostEstimate(
            flops=0, bytes_accessed=8 * picked * depth, transcendentals=0
        ),
        name="gather",
    )(my_places, places(their_spans)[0], encoded, one_back, two_back, *near)
    theirs = swapped(theirs, "ctx", 1)

    block = 4 * HEAD_DIM
    steps = width // block
    cost = pl.CostEstimate(
        flops=2 * picked * depth * 2 * width,
        bytes_accessed=weight.size * 2 + picked * depth * 4,
        transcendentals=picked * SPAN * HEADS,
    )
    return pl.pallas_call(
        functools.partial(cross_kernel, HEAD_DIM ** (-0.5) * LOG2E, span_count),
        out_shape=jax.ShapeDtypeStruct((rows, width), jnp.float32),
        grid_spec=pltpu.PrefetchScalarGridSpec(
            num_scalar_prefetch=2,
            grid=(steps,),
            in_specs=[
                pl.BlockSpec((picked, depth), lambda g, *_: (0, 0), pipeline_mode=pl.Buffered(1)),
                pl.BlockSpec((picked, depth), lambda g, *_: (0, 0), pipeline_mode=pl.Buffered(1)),
                pl.BlockSpec((rows, block), lambda g, *_: (0, g)),
                pl.BlockSpec((depth, block), lambda g, *_: (0, g)),
                pl.BlockSpec((depth, block), lambda g, *_: (0, g + steps)),
            ],
            out_specs=pl.BlockSpec((rows, block), lambda g, *_: (0, g)),
            scratch_shapes=[pltpu.VMEM((picked, depth), encoded.dtype)],
        ),
        cost_estimate=cost,
        name="cross",
    )(here, count_rows, mine, theirs, cross_queries, weight, weight)


def sum_kernel(self_ref, cross_ref, out_ref):
    for head in range(self_ref.shape[0]):
        lanes = slice(head * HEAD_DIM, (head + 1) * HEAD_DIM)
        out_ref[:, lanes] = (self_ref[head].astype(jnp.float32) + cross_ref[:, lanes]).astype(
            out_ref.dtype
        )


def per_device(
    queries, self_keys, self_values, cross_queries, encoded, neighbour_weight, counts, sources
):
    position = lax.axis_index("ctx")
    count = lax.axis_size("ctx")
    groups = [list(range(first, first + HEADS)) for first in range(0, count, HEADS)]
    cross_part = cross_attention(
        cross_queries, encoded, neighbour_weight, counts, sources, position
    )
    by_head = self_attention(queries, self_keys, self_values, position // HEADS, groups)
    self_part = lax.all_to_all(by_head, "ctx", 0, 0, axis_index_groups=groups, tiled=True)
    return pl.pallas_call(
        sum_kernel,
        out_shape=jax.ShapeDtypeStruct(queries.shape, jnp.bfloat16),
        name="total",
    )(self_part, cross_part)


def solution(mesh):
    return jax.shard_map(
        per_device,
        mesh=mesh,
        in_specs=(
            P(("groups", "ctx"), None),
            P(("groups", "ctx"), None),
            P(("groups", "ctx"), None),
            P(("groups", "ctx"), None),
            P(("groups", "ctx"), None),
            P(),
            P(("groups", "ctx")),
            P(("groups", "ctx"), None),
        ),
        out_specs=P(("groups", "ctx"), None),
        check_vma=False,
    )
```

```python
import functools

import jax
import jax.numpy as jnp
from jax import lax
from jax.experimental import pallas as pl
from jax.experimental.pallas import tpu as pltpu
from jax.sharding import PartitionSpec as P


HEADS = 16
HEAD_DIM = 128
SPAN = 64
PLANE = 8
LEFT = 8

MASKED_SCORE = -1e30
LOG2E = 1.4426950408889634


def shifted(value, axis, steps):
    count = lax.axis_size(axis)
    first, last = (max(0, -steps), min(count, count - steps))
    return lax.ppermute(value, axis, [(source, source + steps) for source in range(first, last)])


def swapped(value, axis, bit):
    count = lax.axis_size(axis)
    return lax.ppermute(value, axis, [(source, source ^ bit) for source in range(count)])


def pack_kernel(*refs):
    *in_refs, out_ref = refs
    rows = in_refs[0].shape[0]
    for head in range(out_ref.shape[0]):
        columns = slice(head * HEAD_DIM, (head + 1) * HEAD_DIM)
        for n, ref in enumerate(in_refs):
            out_ref[head, n * rows : (n + 1) * rows, :] = ref[:, columns]


def packed(*arrays):
    rows, width = arrays[0].shape
    return pl.pallas_call(
        pack_kernel,
        out_shape=jax.ShapeDtypeStruct(
            (width // HEAD_DIM, len(arrays) * rows, HEAD_DIM), arrays[0].dtype
        ),
        cost_estimate=pl.CostEstimate(
            flops=0, bytes_accessed=4 * len(arrays) * rows * width, transcendentals=0
        ),
        name="pack",
    )(*arrays)


def scores_of(q, k):
    return lax.dot_general(q, k, (((1,), (1,)), ((), ())), preferred_element_type=jnp.float32)


def softmax_parts(q, pieces, scale):
    scores = []
    for k, _, mask in pieces:
        s = scores_of(q, k)
        scores.append(s if mask is None else jnp.where(mask, s, MASKED_SCORE))
    largest = functools.reduce(
        jnp.maximum, [jnp.max(s, axis=1, keepdims=True) for s in scores]
    )
    total, out = None, None
    for s, (_, v, _) in zip(scores, pieces):
        p = jnp.exp2((s - largest) * scale)
        t = jnp.sum(p, axis=1, keepdims=True)
        o = jnp.dot(p.astype(jnp.bfloat16), v, preferred_element_type=jnp.float32)
        total = t if total is None else total + t
        out = o if out is None else out + o
    return out, largest, total


def with_stats(largest, total):
    lane = lax.broadcasted_iota(jnp.int32, (largest.shape[0], 128), 1)
    return jnp.where(lane < 64, largest, total)


def halves(stat):
    return stat[:, 0:1], stat[:, 64:65]


def thirds(x):
    high = x.astype(jnp.bfloat16)
    rest = x - high.astype(jnp.float32)
    middle = rest.astype(jnp.bfloat16)
    low = (rest - middle.astype(jnp.float32)).astype(jnp.bfloat16)
    return high, middle, low


def taken(ref, first, count, start, rows):
    return ref[first : first + count, start : start + rows, :].reshape(count * rows, ref.shape[2])


def triangle(size, keep):
    row = lax.broadcasted_iota(jnp.int32, (size, size), 0)
    column = lax.broadcasted_iota(jnp.int32, (size, size), 1)
    return keep(column, row)


def own_kernel(scale, q_ref, kv_ref, out_ref, stat_ref):
    blocks, rows, dim = q_ref.shape
    causal = triangle(2 * rows, lambda column, row: column <= row)
    for i in range(0, blocks, 2):
        pieces = [(taken(kv_ref, i, 2, 0, rows), taken(kv_ref, i, 2, rows, rows), causal)]
        if i:
            pieces.append((taken(kv_ref, 0, i, 0, rows), taken(kv_ref, 0, i, rows, rows), None))
        out, largest, total = softmax_parts(taken(q_ref, i, 2, 0, rows), pieces, scale)
        out_ref[i : i + 2] = out.reshape(2, rows, dim)
        stat_ref[i : i + 2] = with_stats(largest, total).reshape(2, rows, 128)


def later_kernel(scale, q_ref, kv_ref, out_ref):
    blocks, rows, dim = q_ref.shape
    later = triangle(2 * rows, lambda column, row: column > row)
    out_ref[blocks] = jnp.zeros((rows, dim), out_ref.dtype)
    for i in range(0, blocks, 2):
        pieces = [(taken(kv_ref, i, 2, 0, rows), taken(kv_ref, i, 2, rows, rows), later)]
        rest = blocks - i - 2
        if rest:
            pieces.append(
                (taken(kv_ref, i + 2, rest, 0, rows), taken(kv_ref, i + 2, rest, rows, rows), None)
            )
        out, largest, total = softmax_parts(taken(q_ref, i, 2, 0, rows), pieces, scale)
        out_ref[i : i + 2] = out.reshape(2, rows, dim).astype(out_ref.dtype)
        stat = with_stats(largest, total)
        for n in range(2):
            turned = stat[n * rows : (n + 1) * rows].T
            for m, row in enumerate((turned[0:1], turned[64:65])):
                for k, part in enumerate(thirds(row)):
                    place = ((i + n) * 2 + m) * 3 + k
                    out_ref[blocks, place : place + 1, :] = part


def sent_stats(ref, block, rows):
    values = []
    for m in range(2):
        place = (block * 2 + m) * 3
        three = ref[ref.shape[0] - 1, place : place + 3, :].astype(jnp.float32)
        values.append(three[0:1] + three[1:2] + three[2:3])
    sublane = lax.broadcasted_iota(jnp.int32, (rows, 128), 0)
    return jnp.where(sublane < 64, values[0], values[1]).T


def previous_kernel(scale, flag_ref, q_ref, kv_ref, back_ref, out1_ref, stat_ref, out_ref):
    blocks, rows, dim = q_ref.shape
    sent = back_ref.shape[0] - 1
    later = triangle(2 * rows, lambda column, row: column > row)

    def store(i, parts):
        top = functools.reduce(jnp.maximum, [largest for _, largest, _ in parts])
        weights = [jnp.exp2((largest - top) * scale) for _, largest, _ in parts]
        inverse = 1.0 / sum(w * total for w, (_, _, total) in zip(weights, parts))
        merged = sum((w * inverse) * out for w, (out, _, _) in zip(weights, parts))
        out_ref[i : i + 2] = merged.reshape(2, rows, dim).astype(out_ref.dtype)

    def own_part(i):
        stat = stat_ref[i : i + 2].reshape(2 * rows, 128)
        return (out1_ref[i : i + 2].reshape(2 * rows, dim), *halves(stat))

    @pl.when(flag_ref[0] > 0)
    def _():
        for i in range(0, blocks, 2):
            pieces = []
            first = max(i - sent, 0)
            if i >= sent:
                pieces.append(
                    (taken(kv_ref, first, 2, 0, rows), taken(kv_ref, first, 2, rows, rows), later)
                )
                first += 2
            rest = kv_ref.shape[0] - first
            if rest:
                pieces.append(
                    (
                        taken(kv_ref, first, rest, 0, rows),
                        taken(kv_ref, first, rest, rows, rows),
                        None,
                    )
                )
            parts = [softmax_parts(taken(q_ref, i, 2, 0, rows), pieces, scale), own_part(i)]
            if i < sent:
                stat = jnp.concatenate([sent_stats(back_ref, i + n, rows) for n in range(2)], axis=0)
                parts.append((taken(back_ref, i, 2, 0, rows).astype(jnp.float32), *halves(stat)))
            store(i, parts)

    @pl.when(flag_ref[0] == 0)
    def _():
        for i in range(0, blocks, 2):
            store(i, [own_part(i)])


def estimate(area, arrays):
    return pl.CostEstimate(
        flops=4 * HEAD_DIM * area,
        bytes_accessed=sum(2 * a.size for a in arrays),
        transcendentals=area,
    )


def self_attention(queries, keys, values, chunk, groups):
    rows, width = queries.shape
    heads = width // HEAD_DIM
    scale = HEAD_DIM ** (-0.5) * LOG2E
    kv = lax.all_to_all(
        packed(keys, values), "ctx", 0, 0, axis_index_groups=groups, tiled=True
    )
    q = lax.all_to_all(packed(queries), "ctx", 0, 0, axis_index_groups=groups, tiled=True)
    arriving = shifted(kv[LEFT:], "ctx", heads)
    asked = shifted(q[:LEFT], "ctx", -heads)
    area = (heads * rows) ** 2 // 2
    small = (LEFT * rows) ** 2 // 2
    out1, stat = pl.pallas_call(
        functools.partial(own_kernel, scale),
        out_shape=(
            jax.ShapeDtypeStruct((heads, rows, HEAD_DIM), jnp.float32),
            jax.ShapeDtypeStruct((heads, rows, 128), jnp.float32),
        ),
        cost_estimate=estimate(area, (q, kv)),
        name="own",
    )(q, kv)
    answer = pl.pallas_call(
        functools.partial(later_kernel, scale),
        out_shape=jax.ShapeDtypeStruct((LEFT + 1, rows, HEAD_DIM), jnp.bfloat16),
        cost_estimate=estimate(small, (asked,)),
        name="later",
    )(asked, kv)
    back = shifted(answer, "ctx", heads)
    vmem = pl.BlockSpec(memory_space=pltpu.VMEM)
    return pl.pallas_call(
        functools.partial(previous_kernel, scale),
        out_shape=jax.ShapeDtypeStruct((heads, rows, HEAD_DIM), jnp.bfloat16),
        in_specs=[pl.BlockSpec(memory_space=pltpu.SMEM)] + [vmem] * 5,
        cost_estimate=estimate(area - small, (q, kv, out1, stat)),
        name="previous",
    )(chunk.reshape(1), q, arriving, back, out1, stat)


def wanted_pieces(table_ref, position, span_count):
    pieces = []
    place, plane = position % PLANE, position // PLANE
    for c in range(span_count):
        for slot in range(2):
            source = table_ref[c, slot] // 4
            for later in range(2):
                block = (source + later) // span_count
                relative = (block % PLANE) ^ place
                away = plane - block // PLANE
                column = relative // 2
                index = jnp.where(
                    column == 0, away, 1 + 2 * column + jnp.where(away == 1, 0, 1)
                )
                pieces.append((relative % 2 == 0, index, (source + later) % span_count))
    return pieces


def fetch(refs, rows, index, half, target, sem):
    size = target.shape[0]
    first = 0
    for ref in refs:
        count = ref.shape[0] // rows

        @pl.when((index >= first) & (index < first + count))
        def _(ref=ref, first=first):
            start = pl.multiple_of((index - first) * rows + half * size, size)
            pltpu.make_async_copy(ref.at[pl.ds(start, size), :], target, sem).start()

        first += count


def gather_kernel(span_count, position_ref, theirs_ref, *refs):
    *in_refs, out_ref, sems = refs
    rows = in_refs[0].shape[0]
    pieces = wanted_pieces(theirs_ref, position_ref[0], span_count)
    size = out_ref.shape[0] // len(pieces)
    targets = [out_ref.at[n * size : (n + 1) * size, :] for n in range(len(pieces))]
    for n, (here, index, half) in enumerate(pieces):
        fetch(in_refs, rows, jnp.where(here, index, -1), half, targets[n], sems.at[n])
    for n, (here, _, _) in enumerate(pieces):

        @pl.when(here)
        def _(n=n):
            pltpu.make_async_copy(in_refs[0].at[0:size, :], targets[n], sems.at[n]).wait()


def cross_kernel(scale, span_count, position_ref, table_ref, *refs):
    *in_refs, theirs_ref, q_ref, weight_ref, out_ref, rows_ref, weights_ref, sems, weight_sems = refs
    rows, width = q_ref.shape
    span = rows // span_count
    steps, _, _, block = weights_ref.shape
    weight_copies = [
        [
            pltpu.make_async_copy(
                weight_ref.at[:, n * width + g * block : n * width + (g + 1) * block],
                weights_ref.at[g, n],
                weight_sems.at[g, n],
            )
            for n in range(2)
        ]
        for g in range(steps)
    ]
    pieces = wanted_pieces(table_ref, position_ref[0], span_count)
    targets = [rows_ref.at[n * span : (n + 1) * span, :] for n in range(len(pieces))]
    held = sum(ref.shape[0] for ref in in_refs) // rows
    for n, (here, index, half) in enumerate(pieces):
        fetch(in_refs, rows, jnp.where(here, index, held), half, targets[n], sems.at[n])

        @pl.when(jnp.logical_not(here))
        def _(n=n):
            source = theirs_ref.at[n * span : (n + 1) * span, :]
            pltpu.make_async_copy(source, targets[n], sems.at[n]).start()

    for g in range(steps):
        for copy in weight_copies[g]:
            copy.start()
    for n in range(len(pieces)):
        pltpu.make_async_copy(theirs_ref.at[0:span, :], targets[n], sems.at[n]).wait()

    keys_of_span = rows_ref.shape[0] // span_count
    slot = lax.broadcasted_iota(jnp.int32, (span, keys_of_span), 1) // (2 * span)
    counts = [table_ref[c, 0] % 4 for c in range(span_count)]
    valid = [slot < count for count in counts]
    none = [jnp.where(count > 0, 0.0, 1.0) for count in counts]

    def attend(g, keys, values):
        for h in range(block // HEAD_DIM):
            inner = slice(h * HEAD_DIM, (h + 1) * HEAD_DIM)
            lanes = slice(g * block + h * HEAD_DIM, g * block + (h + 1) * HEAD_DIM)
            for c in range(span_count):
                here = slice(c * keys_of_span, (c + 1) * keys_of_span)
                mine = slice(c * span, (c + 1) * span)
                s = jnp.where(valid[c], scores_of(q_ref[mine, lanes], keys[here, inner]), MASKED_SCORE)
                largest = jnp.max(s, axis=1, keepdims=True)
                p = jnp.where(valid[c], jnp.exp2((s - largest) * scale), 0.0)
                total = jnp.sum(p, axis=1, keepdims=True) + none[c]
                o = jnp.dot(
                    p.astype(jnp.bfloat16), values[here, inner], preferred_element_type=jnp.float32
                )
                out_ref[mine, lanes] = o * (1.0 / total)

    waiting = None
    for g in range(steps):
        for copy in weight_copies[g]:
            copy.wait()
        projected = [
            jnp.dot(
                rows_ref[...], weights_ref[g, n], preferred_element_type=jnp.float32
            ).astype(jnp.bfloat16)
            for n in range(2)
        ]
        if waiting is not None:
            attend(*waiting)
        waiting = (g, *projected)
    attend(*waiting)


def cross_attention(cross_queries, encoded, weight, counts, sources, position):
    rows, width = cross_queries.shape
    span_count = counts.shape[0]
    depth = encoded.shape[1]
    place = position % PLANE
    one_back = shifted(encoded, "ctx", PLANE)
    table = sources * 4 + counts[:, None]
    before = shifted(table, "ctx", 1)
    table = jnp.concatenate([before[-1:], table[:-1]], axis=0)
    their_table = swapped(table, "ctx", 1)
    two_back = shifted(one_back, "ctx", PLANE)

    near = []
    for bit in (2, 4, 6):
        other = jnp.where(place < (place ^ bit), encoded, two_back)
        near.append(swapped(jnp.concatenate([one_back, other], axis=0), "ctx", bit))

    held = [encoded, one_back, two_back, *near]
    where = position.reshape(1)
    picked = span_count * 4 * SPAN
    pieces = picked // SPAN
    smem, anywhere = (pl.BlockSpec(memory_space=m) for m in (pltpu.SMEM, pl.ANY))
    vmem = pl.BlockSpec(memory_space=pltpu.VMEM)
    theirs = pl.pallas_call(
        functools.partial(gather_kernel, span_count),
        out_shape=jax.ShapeDtypeStruct((picked, depth), encoded.dtype),
        in_specs=[smem] * 2 + [anywhere] * len(held),
        out_specs=vmem,
        scratch_shapes=[pltpu.SemaphoreType.DMA((pieces,))],
        cost_estimate=pl.CostEstimate(
            flops=0, bytes_accessed=8 * picked * depth, transcendentals=0
        ),
        name="gather",
    )(where, their_table, *held)
    theirs = swapped(theirs, "ctx", 1)

    block = 4 * HEAD_DIM
    steps = width // block
    cost = pl.CostEstimate(
        flops=2 * picked * depth * 2 * width,
        bytes_accessed=weight.size * 2 + picked * depth * 4,
        transcendentals=picked * SPAN * HEADS,
    )
    return pl.pallas_call(
        functools.partial(cross_kernel, HEAD_DIM ** (-0.5) * LOG2E, span_count),
        out_shape=jax.ShapeDtypeStruct((rows, width), jnp.float32),
        in_specs=[smem] * 2 + [anywhere] * (len(held) + 1) + [vmem, anywhere],
        out_specs=vmem,
        scratch_shapes=[
            pltpu.VMEM((picked, depth), encoded.dtype),
            pltpu.VMEM((steps, 2, depth, block), weight.dtype),
            pltpu.SemaphoreType.DMA((pieces,)),
            pltpu.SemaphoreType.DMA((steps, 2)),
        ],
        cost_estimate=cost,
        name="cross",
    )(where, table, *held, theirs, cross_queries, weight)


def sum_kernel(self_ref, cross_ref, out_ref):
    for head in range(self_ref.shape[0]):
        lanes = slice(head * HEAD_DIM, (head + 1) * HEAD_DIM)
        out_ref[:, lanes] = (self_ref[head].astype(jnp.float32) + cross_ref[:, lanes]).astype(
            out_ref.dtype
        )


def per_device(
    queries, self_keys, self_values, cross_queries, encoded, neighbour_weight, counts, sources
):
    position = lax.axis_index("ctx")
    count = lax.axis_size("ctx")
    groups = [list(range(first, first + HEADS)) for first in range(0, count, HEADS)]
    cross_part = cross_attention(
        cross_queries, encoded, neighbour_weight, counts, sources, position
    )
    by_head = self_attention(queries, self_keys, self_values, position // HEADS, groups)
    self_part = lax.all_to_all(by_head, "ctx", 0, 0, axis_index_groups=groups, tiled=True)
    return pl.pallas_call(
        sum_kernel,
        out_shape=jax.ShapeDtypeStruct(queries.shape, jnp.bfloat16),
        name="total",
    )(self_part, cross_part)


def solution(mesh):
    return jax.shard_map(
        per_device,
        mesh=mesh,
        in_specs=(
            P(("groups", "ctx"), None),
            P(("groups", "ctx"), None),
            P(("groups", "ctx"), None),
            P(("groups", "ctx"), None),
            P(("groups", "ctx"), None),
            P(),
            P(("groups", "ctx")),
            P(("groups", "ctx"), None),
        ),
        out_specs=P(("groups", "ctx"), None),
        check_vma=False,
    )
```

```python
import functools

import jax
import jax.numpy as jnp
from jax import lax
from jax.experimental import pallas as pl
from jax.experimental.pallas import tpu as pltpu
from jax.sharding import PartitionSpec as P


HEADS = 16
HEAD_DIM = 128
SPAN = 64
PLANE = 8
LEFT = 12

MASKED_SCORE = -1e30
LOG2E = 1.4426950408889634


def shifted(value, axis, steps):
    count = lax.axis_size(axis)
    first, last = (max(0, -steps), min(count, count - steps))
    return lax.ppermute(value, axis, [(source, source + steps) for source in range(first, last)])


def swapped(value, axis, bit):
    count = lax.axis_size(axis)
    return lax.ppermute(value, axis, [(source, source ^ bit) for source in range(count)])


def pack_kernel(*refs):
    *in_refs, out_ref = refs
    rows = in_refs[0].shape[0]
    for head in range(out_ref.shape[0]):
        columns = slice(head * HEAD_DIM, (head + 1) * HEAD_DIM)
        for n, ref in enumerate(in_refs):
            out_ref[head, n * rows : (n + 1) * rows, :] = ref[:, columns]


def packed(*arrays):
    rows, width = arrays[0].shape
    return pl.pallas_call(
        pack_kernel,
        out_shape=jax.ShapeDtypeStruct(
            (width // HEAD_DIM, len(arrays) * rows, HEAD_DIM), arrays[0].dtype
        ),
        cost_estimate=pl.CostEstimate(
            flops=0, bytes_accessed=4 * len(arrays) * rows * width, transcendentals=0
        ),
        name="pack",
    )(*arrays)


def scores_of(q, k):
    return lax.dot_general(q, k, (((1,), (1,)), ((), ())), preferred_element_type=jnp.float32)


def softmax_parts(q, pieces, scale):
    scores = []
    for k, _, mask in pieces:
        s = scores_of(q, k)
        scores.append(s if mask is None else jnp.where(mask, s, MASKED_SCORE))
    largest = functools.reduce(
        jnp.maximum, [jnp.max(s, axis=1, keepdims=True) for s in scores]
    )
    total, out = None, None
    for s, (_, v, _) in zip(scores, pieces):
        p = jnp.exp2((s - largest) * scale)
        t = jnp.sum(p, axis=1, keepdims=True)
        o = jnp.dot(p.astype(jnp.bfloat16), v, preferred_element_type=jnp.float32)
        total = t if total is None else total + t
        out = o if out is None else out + o
    return out, largest, total


def with_stats(largest, total):
    lane = lax.broadcasted_iota(jnp.int32, (largest.shape[0], 128), 1)
    return jnp.where(lane < 64, largest, total)


def halves(stat):
    return stat[:, 0:1], stat[:, 64:65]


def thirds(x):
    high = x.astype(jnp.bfloat16)
    rest = x - high.astype(jnp.float32)
    middle = rest.astype(jnp.bfloat16)
    low = (rest - middle.astype(jnp.float32)).astype(jnp.bfloat16)
    return high, middle, low


def taken(ref, first, count, start, rows):
    return ref[first : first + count, start : start + rows, :].reshape(count * rows, ref.shape[2])


def triangle(size, keep):
    row = lax.broadcasted_iota(jnp.int32, (size, size), 0)
    column = lax.broadcasted_iota(jnp.int32, (size, size), 1)
    return keep(column, row)


def own_kernel(scale, q_ref, kv_ref, out_ref, stat_ref):
    blocks, rows, dim = q_ref.shape
    causal = triangle(2 * rows, lambda column, row: column <= row)
    for i in range(0, blocks, 2):
        pieces = [(taken(kv_ref, i, 2, 0, rows), taken(kv_ref, i, 2, rows, rows), causal)]
        if i:
            pieces.append((taken(kv_ref, 0, i, 0, rows), taken(kv_ref, 0, i, rows, rows), None))
        out, largest, total = softmax_parts(taken(q_ref, i, 2, 0, rows), pieces, scale)
        out_ref[i : i + 2] = out.reshape(2, rows, dim)
        stat_ref[i : i + 2] = with_stats(largest, total).reshape(2, rows, 128)


def later_kernel(scale, q_ref, kv_ref, out_ref):
    blocks, rows, dim = q_ref.shape
    later = triangle(2 * rows, lambda column, row: column > row)
    out_ref[blocks] = jnp.zeros((rows, dim), out_ref.dtype)
    for i in range(0, blocks, 2):
        pieces = [(taken(kv_ref, i, 2, 0, rows), taken(kv_ref, i, 2, rows, rows), later)]
        rest = blocks - i - 2
        if rest:
            pieces.append(
                (taken(kv_ref, i + 2, rest, 0, rows), taken(kv_ref, i + 2, rest, rows, rows), None)
            )
        out, largest, total = softmax_parts(taken(q_ref, i, 2, 0, rows), pieces, scale)
        out_ref[i : i + 2] = out.reshape(2, rows, dim).astype(out_ref.dtype)
        stat = with_stats(largest, total)
        for n in range(2):
            turned = stat[n * rows : (n + 1) * rows].T
            for m, row in enumerate((turned[0:1], turned[64:65])):
                for k, part in enumerate(thirds(row)):
                    place = ((i + n) * 2 + m) * 3 + k
                    out_ref[blocks, place : place + 1, :] = part


def sent_stats(ref, block, rows):
    values = []
    for m in range(2):
        place = (block * 2 + m) * 3
        three = ref[ref.shape[0] - 1, place : place + 3, :].astype(jnp.float32)
        values.append(three[0:1] + three[1:2] + three[2:3])
    sublane = lax.broadcasted_iota(jnp.int32, (rows, 128), 0)
    return jnp.where(sublane < 64, values[0], values[1]).T


def previous_kernel(scale, flag_ref, q_ref, kv_ref, back_ref, out1_ref, stat_ref, out_ref):
    blocks, rows, dim = q_ref.shape
    sent = back_ref.shape[0] - 1
    later = triangle(2 * rows, lambda column, row: column > row)

    def store(i, parts):
        top = functools.reduce(jnp.maximum, [largest for _, largest, _ in parts])
        weights = [jnp.exp2((largest - top) * scale) for _, largest, _ in parts]
        inverse = 1.0 / sum(w * total for w, (_, _, total) in zip(weights, parts))
        merged = sum((w * inverse) * out for w, (out, _, _) in zip(weights, parts))
        out_ref[i : i + 2] = merged.reshape(2, rows, dim).astype(out_ref.dtype)

    def own_part(i):
        stat = stat_ref[i : i + 2].reshape(2 * rows, 128)
        return (out1_ref[i : i + 2].reshape(2 * rows, dim), *halves(stat))

    @pl.when(flag_ref[0] > 0)
    def _():
        for i in range(0, blocks, 2):
            pieces = []
            first = max(i - sent, 0)
            if i >= sent:
                pieces.append(
                    (taken(kv_ref, first, 2, 0, rows), taken(kv_ref, first, 2, rows, rows), later)
                )
                first += 2
            rest = kv_ref.shape[0] - first
            if rest:
                pieces.append(
                    (
                        taken(kv_ref, first, rest, 0, rows),
                        taken(kv_ref, first, rest, rows, rows),
                        None,
                    )
                )
            parts = [softmax_parts(taken(q_ref, i, 2, 0, rows), pieces, scale), own_part(i)]
            if i < sent:
                stat = jnp.concatenate([sent_stats(back_ref, i + n, rows) for n in range(2)], axis=0)
                parts.append((taken(back_ref, i, 2, 0, rows).astype(jnp.float32), *halves(stat)))
            store(i, parts)

    @pl.when(flag_ref[0] == 0)
    def _():
        for i in range(0, blocks, 2):
            store(i, [own_part(i)])


def estimate(area, arrays):
    return pl.CostEstimate(
        flops=4 * HEAD_DIM * area,
        bytes_accessed=sum(2 * a.size for a in arrays),
        transcendentals=area,
    )


def self_attention(queries, keys, values, chunk, groups):
    rows, width = queries.shape
    heads = width // HEAD_DIM
    scale = HEAD_DIM ** (-0.5) * LOG2E
    kv = lax.all_to_all(
        packed(keys, values), "ctx", 0, 0, axis_index_groups=groups, tiled=True
    )
    q = lax.all_to_all(packed(queries), "ctx", 0, 0, axis_index_groups=groups, tiled=True)
    arriving = shifted(kv[LEFT:], "ctx", heads)
    asked = shifted(q[:LEFT], "ctx", -heads)
    area = (heads * rows) ** 2 // 2
    small = (LEFT * rows) ** 2 // 2
    out1, stat = pl.pallas_call(
        functools.partial(own_kernel, scale),
        out_shape=(
            jax.ShapeDtypeStruct((heads, rows, HEAD_DIM), jnp.float32),
            jax.ShapeDtypeStruct((heads, rows, 128), jnp.float32),
        ),
        cost_estimate=estimate(area, (q, kv)),
        name="own",
    )(q, kv)
    answer = pl.pallas_call(
        functools.partial(later_kernel, scale),
        out_shape=jax.ShapeDtypeStruct((LEFT + 1, rows, HEAD_DIM), jnp.bfloat16),
        cost_estimate=estimate(small, (asked,)),
        name="later",
    )(asked, kv)
    back = shifted(answer, "ctx", heads)
    vmem = pl.BlockSpec(memory_space=pltpu.VMEM)
    return pl.pallas_call(
        functools.partial(previous_kernel, scale),
        out_shape=jax.ShapeDtypeStruct((heads, rows, HEAD_DIM), jnp.bfloat16),
        in_specs=[pl.BlockSpec(memory_space=pltpu.SMEM)] + [vmem] * 5,
        cost_estimate=estimate(area - small, (q, kv, out1, stat)),
        name="previous",
    )(chunk.reshape(1), q, arriving, back, out1, stat)


def wanted_pieces(table_ref, position, span_count):
    pieces = []
    place, plane = position % PLANE, position // PLANE
    for c in range(span_count):
        for slot in range(2):
            source = table_ref[c, slot] // 4
            for later in range(2):
                block = (source + later) // span_count
                relative = (block % PLANE) ^ place
                away = plane - block // PLANE
                column = relative // 2
                index = jnp.where(
                    column == 0, away, 1 + 2 * column + jnp.where(away == 1, 0, 1)
                )
                pieces.append((relative % 2 == 0, index, (source + later) % span_count))
    return pieces


def fetch(refs, rows, index, half, target, sem):
    size = target.shape[0]
    first = 0
    for ref in refs:
        count = ref.shape[0] // rows

        @pl.when((index >= first) & (index < first + count))
        def _(ref=ref, first=first):
            start = pl.multiple_of((index - first) * rows + half * size, size)
            pltpu.make_async_copy(ref.at[pl.ds(start, size), :], target, sem).start()

        first += count


def gather_kernel(span_count, position_ref, theirs_ref, *refs):
    *in_refs, out_ref, sems = refs
    rows = in_refs[0].shape[0]
    pieces = wanted_pieces(theirs_ref, position_ref[0], span_count)
    size = out_ref.shape[0] // len(pieces)
    targets = [out_ref.at[n * size : (n + 1) * size, :] for n in range(len(pieces))]
    for n, (here, index, half) in enumerate(pieces):
        fetch(in_refs, rows, jnp.where(here, index, -1), half, targets[n], sems.at[n])
    for n, (here, _, _) in enumerate(pieces):

        @pl.when(here)
        def _(n=n):
            pltpu.make_async_copy(in_refs[0].at[0:size, :], targets[n], sems.at[n]).wait()


def absorb_kernel(q_ref, weight_ref, out_ref, weights_ref, sems):
    rows, width = q_ref.shape
    span_count = out_ref.shape[0]
    span = rows // span_count
    steps, _, block = weights_ref.shape
    copies = [
        pltpu.make_async_copy(
            weight_ref.at[:, g * block : (g + 1) * block], weights_ref.at[g], sems.at[g]
        )
        for g in range(steps)
    ]
    for copy in copies:
        copy.start()
    for head in range(width // HEAD_DIM):
        g, first = divmod(head * HEAD_DIM, block)
        if first == 0:
            copies[g].wait()
        lanes = slice(head * HEAD_DIM, (head + 1) * HEAD_DIM)
        product = scores_of(q_ref[:, lanes], weights_ref[g, :, first : first + HEAD_DIM])
        product = product.astype(out_ref.dtype)
        for c in range(span_count):
            out_ref[c, head * span : (head + 1) * span, :] = product[c * span : (c + 1) * span]


def cross_kernel(scale, position_ref, table_ref, *refs):
    *in_refs, theirs_ref, asks_ref, weight_ref, out_ref = refs[:-6]
    rows_ref, all_asks_ref, weights_ref, sems, ask_sems, weight_sems = refs[-6:]
    rows, width = out_ref.shape
    steps, span_count, asked, _ = all_asks_ref.shape
    span = rows // span_count
    block = weights_ref.shape[2]
    pieces = wanted_pieces(table_ref, position_ref[0], span_count)
    targets = [rows_ref.at[n * span : (n + 1) * span, :] for n in range(len(pieces))]
    held = sum(ref.shape[0] for ref in in_refs) // rows
    for n, (here, index, half) in enumerate(pieces):
        fetch(in_refs, rows, jnp.where(here, index, held), half, targets[n], sems.at[n])

        @pl.when(jnp.logical_not(here))
        def _(n=n):
            source = theirs_ref.at[n * span : (n + 1) * span, :]
            pltpu.make_async_copy(source, targets[n], sems.at[n]).start()

    ask_copies = [
        pltpu.make_async_copy(
            asks_ref.at[:, g * asked : (g + 1) * asked, :], all_asks_ref.at[g], ask_sems.at[g]
        )
        for g in range(steps)
    ]
    weight_copies = [
        pltpu.make_async_copy(
            weight_ref.at[:, width + g * block : width + (g + 1) * block],
            weights_ref.at[g],
            weight_sems.at[g],
        )
        for g in range(steps)
    ]
    for g in range(steps):
        ask_copies[g].start()
        weight_copies[g].start()
    for n in range(len(pieces)):
        pltpu.make_async_copy(theirs_ref.at[0:span, :], targets[n], sems.at[n]).wait()

    keys_of_span = rows_ref.shape[0] // span_count
    slot = lax.broadcasted_iota(jnp.int32, (asked, keys_of_span), 1) // (2 * span)
    counts = [table_ref[c, 0] % 4 for c in range(span_count)]
    for g in range(steps):
        ask_copies[g].wait()
        means = []
        for c in range(span_count):
            keys = rows_ref[c * keys_of_span : (c + 1) * keys_of_span, :]
            s = jnp.where(slot < counts[c], scores_of(all_asks_ref[g, c], keys), MASKED_SCORE)
            p = jnp.exp2((s - jnp.max(s, axis=1, keepdims=True)) * scale)
            inverse = jnp.where(counts[c] > 0, 1.0 / jnp.sum(p, axis=1, keepdims=True), 0.0)
            mean = jnp.dot(p.astype(jnp.bfloat16), keys, preferred_element_type=jnp.float32)
            means.append((mean * inverse).astype(jnp.bfloat16))
        weight_copies[g].wait()
        for h in range(block // HEAD_DIM):
            mean = jnp.concatenate([m[h * span : (h + 1) * span] for m in means], axis=0)
            inner = slice(h * HEAD_DIM, (h + 1) * HEAD_DIM)
            lanes = slice(g * block + h * HEAD_DIM, g * block + (h + 1) * HEAD_DIM)
            out_ref[:, lanes] = jnp.dot(
                mean, weights_ref[g, :, inner], preferred_element_type=jnp.float32
            )


def cross_attention(cross_queries, encoded, weight, counts, sources, position):
    rows, width = cross_queries.shape
    span_count = counts.shape[0]
    depth = encoded.shape[1]
    place = position % PLANE
    one_back = shifted(encoded, "ctx", PLANE)
    table = sources * 4 + counts[:, None]
    before = shifted(table, "ctx", 1)
    table = jnp.concatenate([before[-1:], table[:-1]], axis=0)
    their_table = swapped(table, "ctx", 1)
    two_back = shifted(one_back, "ctx", PLANE)

    near = []
    for bit in (2, 4, 6):
        other = jnp.where(place < (place ^ bit), encoded, two_back)
        near.append(swapped(jnp.concatenate([one_back, other], axis=0), "ctx", bit))

    held = [encoded, one_back, two_back, *near]
    where = position.reshape(1)
    picked = span_count * 4 * SPAN
    pieces = picked // SPAN
    smem, anywhere = (pl.BlockSpec(memory_space=m) for m in (pltpu.SMEM, pl.ANY))
    vmem = pl.BlockSpec(memory_space=pltpu.VMEM)
    theirs = pl.pallas_call(
        functools.partial(gather_kernel, span_count),
        out_shape=jax.ShapeDtypeStruct((picked, depth), encoded.dtype),
        in_specs=[smem] * 2 + [anywhere] * len(held),
        out_specs=vmem,
        scratch_shapes=[pltpu.SemaphoreType.DMA((pieces,))],
        cost_estimate=pl.CostEstimate(
            flops=0, bytes_accessed=8 * picked * depth, transcendentals=0
        ),
        name="gather",
    )(where, their_table, *held)
    theirs = swapped(theirs, "ctx", 1)

    heads = width // HEAD_DIM
    block = 4 * HEAD_DIM
    steps = width // block
    asks = pl.pallas_call(
        absorb_kernel,
        out_shape=jax.ShapeDtypeStruct((span_count, heads * SPAN, depth), jnp.bfloat16),
        in_specs=[vmem, anywhere],
        out_specs=vmem,
        scratch_shapes=[
            pltpu.VMEM((steps, depth, block), weight.dtype),
            pltpu.SemaphoreType.DMA((steps,)),
        ],
        cost_estimate=pl.CostEstimate(
            flops=2 * rows * depth * width, bytes_accessed=2 * weight.size, transcendentals=0
        ),
        name="absorb",
    )(cross_queries, weight)
    block = 8 * HEAD_DIM
    steps = width // block
    cost = pl.CostEstimate(
        flops=4 * picked * depth * heads * SPAN + 2 * rows * depth * width,
        bytes_accessed=weight.size + asks.size * 2 + picked * depth * 4,
        transcendentals=picked * SPAN * heads,
    )
    return pl.pallas_call(
        functools.partial(cross_kernel, HEAD_DIM ** (-0.5) * LOG2E),
        out_shape=jax.ShapeDtypeStruct((rows, width), jnp.float32),
        in_specs=[smem] * 2 + [anywhere] * (len(held) + 3),
        out_specs=vmem,
        scratch_shapes=[
            pltpu.VMEM((picked, depth), encoded.dtype),
            pltpu.VMEM((steps, span_count, heads * SPAN // steps, depth), asks.dtype),
            pltpu.VMEM((steps, depth, block), weight.dtype),
            pltpu.SemaphoreType.DMA((pieces,)),
            pltpu.SemaphoreType.DMA((steps,)),
            pltpu.SemaphoreType.DMA((steps,)),
        ],
        cost_estimate=cost,
        name="cross",
    )(where, table, *held, theirs, asks, weight)


def sum_kernel(self_ref, cross_ref, out_ref):
    for head in range(self_ref.shape[0]):
        lanes = slice(head * HEAD_DIM, (head + 1) * HEAD_DIM)
        out_ref[:, lanes] = (self_ref[head].astype(jnp.float32) + cross_ref[:, lanes]).astype(
            out_ref.dtype
        )


def per_device(
    queries, self_keys, self_values, cross_queries, encoded, neighbour_weight, counts, sources
):
    position = lax.axis_index("ctx")
    count = lax.axis_size("ctx")
    groups = [list(range(first, first + HEADS)) for first in range(0, count, HEADS)]
    cross_part = cross_attention(
        cross_queries, encoded, neighbour_weight, counts, sources, position
    )
    by_head = self_attention(queries, self_keys, self_values, position // HEADS, groups)
    self_part = lax.all_to_all(by_head, "ctx", 0, 0, axis_index_groups=groups, tiled=True)
    return pl.pallas_call(
        sum_kernel,
        out_shape=jax.ShapeDtypeStruct(queries.shape, jnp.bfloat16),
        name="total",
    )(self_part, cross_part)


def solution(mesh):
    return jax.shard_map(
        per_device,
        mesh=mesh,
        in_specs=(
            P(("groups", "ctx"), None),
            P(("groups", "ctx"), None),
            P(("groups", "ctx"), None),
            P(("groups", "ctx"), None),
            P(("groups", "ctx"), None),
            P(),
            P(("groups", "ctx")),
            P(("groups", "ctx"), None),
        ),
        out_specs=P(("groups", "ctx"), None),
        check_vma=False,
    )
```

```python
import functools

import jax
import jax.numpy as jnp
from jax import lax
from jax.experimental import pallas as pl
from jax.experimental.pallas import tpu as pltpu
from jax.sharding import PartitionSpec as P


HEADS = 16
HEAD_DIM = 128
SPAN = 64
PLANE = 8
LEFT = 8

MASKED_SCORE = -1e30
LOG2E = 1.4426950408889634


def shifted(value, axis, steps):
    count = lax.axis_size(axis)
    first, last = (max(0, -steps), min(count, count - steps))
    return lax.ppermute(value, axis, [(source, source + steps) for source in range(first, last)])


def swapped(value, axis, bit):
    count = lax.axis_size(axis)
    return lax.ppermute(value, axis, [(source, source ^ bit) for source in range(count)])


def pack_kernel(*refs):
    *in_refs, out_ref = refs
    rows = in_refs[0].shape[0]
    for head in range(out_ref.shape[0]):
        columns = slice(head * HEAD_DIM, (head + 1) * HEAD_DIM)
        for n, ref in enumerate(in_refs):
            out_ref[head, n * rows : (n + 1) * rows, :] = ref[:, columns]


def packed(*arrays):
    rows, width = arrays[0].shape
    return pl.pallas_call(
        pack_kernel,
        out_shape=jax.ShapeDtypeStruct(
            (width // HEAD_DIM, len(arrays) * rows, HEAD_DIM), arrays[0].dtype
        ),
        cost_estimate=pl.CostEstimate(
            flops=0, bytes_accessed=4 * len(arrays) * rows * width, transcendentals=0
        ),
        name="pack",
    )(*arrays)


def scores_of(q, k):
    return lax.dot_general(q, k, (((1,), (1,)), ((), ())), preferred_element_type=jnp.float32)


def softmax_parts(q, pieces, scale):
    scores = []
    for k, _, mask in pieces:
        s = scores_of(q, k)
        scores.append(s if mask is None else jnp.where(mask, s, MASKED_SCORE))
    largest = functools.reduce(
        jnp.maximum, [jnp.max(s, axis=1, keepdims=True) for s in scores]
    )
    total, out = None, None
    for s, (_, v, _) in zip(scores, pieces):
        p = jnp.exp2((s - largest) * scale)
        t = jnp.sum(p, axis=1, keepdims=True)
        o = jnp.dot(p.astype(jnp.bfloat16), v, preferred_element_type=jnp.float32)
        total = t if total is None else total + t
        out = o if out is None else out + o
    return out, largest, total


def with_stats(largest, total):
    lane = lax.broadcasted_iota(jnp.int32, (largest.shape[0], 128), 1)
    return jnp.where(lane < 64, largest, total)


def halves(stat):
    return stat[:, 0:1], stat[:, 64:65]


def thirds(x):
    high = x.astype(jnp.bfloat16)
    rest = x - high.astype(jnp.float32)
    middle = rest.astype(jnp.bfloat16)
    low = (rest - middle.astype(jnp.float32)).astype(jnp.bfloat16)
    return high, middle, low


def taken(ref, first, count, start, rows):
    return ref[first : first + count, start : start + rows, :].reshape(count * rows, ref.shape[2])


def triangle(size, keep):
    row = lax.broadcasted_iota(jnp.int32, (size, size), 0)
    column = lax.broadcasted_iota(jnp.int32, (size, size), 1)
    return keep(column, row)


def own_kernel(scale, x_ref, out_ref, stat_ref):
    blocks, triple, dim = x_ref.shape
    rows = triple // 3
    causal = triangle(2 * rows, lambda column, row: column <= row)
    for i in range(0, blocks, 2):
        spans = [(i, 2, causal)] + ([(0, i, None)] if i else [])
        pieces = [
            (taken(x_ref, f, n, rows, rows), taken(x_ref, f, n, 2 * rows, rows), mask)
            for f, n, mask in spans
        ]
        out, largest, total = softmax_parts(taken(x_ref, i, 2, 0, rows), pieces, scale)
        out_ref[i : i + 2] = out.reshape(2, rows, dim)
        stat_ref[i : i + 2] = with_stats(largest, total).reshape(2, rows, 128)


def later_kernel(scale, q_ref, x_ref, out_ref):
    blocks, rows, dim = q_ref.shape
    later = triangle(2 * rows, lambda column, row: column > row)
    out_ref[blocks] = jnp.zeros((rows, dim), out_ref.dtype)
    for i in range(0, blocks, 2):
        spans = [(i, 2, later)] + ([(i + 2, blocks - i - 2, None)] if i + 2 < blocks else [])
        pieces = [
            (taken(x_ref, f, n, rows, rows), taken(x_ref, f, n, 2 * rows, rows), mask)
            for f, n, mask in spans
        ]
        out, largest, total = softmax_parts(taken(q_ref, i, 2, 0, rows), pieces, scale)
        out_ref[i : i + 2] = out.reshape(2, rows, dim).astype(out_ref.dtype)
        stat = with_stats(largest, total)
        for n in range(2):
            turned = stat[n * rows : (n + 1) * rows].T
            for m, row in enumerate((turned[0:1], turned[64:65])):
                for k, part in enumerate(thirds(row)):
                    place = ((i + n) * 2 + m) * 3 + k
                    out_ref[blocks, place : place + 1, :] = part


def sent_stats(ref, block, rows):
    values = []
    for m in range(2):
        place = (block * 2 + m) * 3
        three = ref[ref.shape[0] - 1, place : place + 3, :].astype(jnp.float32)
        values.append(three[0:1] + three[1:2] + three[2:3])
    sublane = lax.broadcasted_iota(jnp.int32, (rows, 128), 0)
    return jnp.where(sublane < 64, values[0], values[1]).T


def previous_kernel(scale, flag_ref, *refs):
    in_refs, out_ref = refs[:5], refs[5]
    q_ref, kv_ref, back_ref, out1_ref, stat_ref = bufs = refs[6:11]
    sems = refs[11]
    blocks, rows, dim = q_ref.shape
    sent = back_ref.shape[0] - 1
    later = triangle(2 * rows, lambda column, row: column > row)

    def copy(n, i):
        if i is None:
            return pltpu.make_async_copy(in_refs[n], bufs[n], sems.at[n, 0])
        source = in_refs[n].at[i : i + 2, 0 : bufs[n].shape[1], :]
        return pltpu.make_async_copy(source, bufs[n].at[i : i + 2], sems.at[n, i // 2])

    whole = [copy(n, None) for n in (1, 2)]
    paired = {i: [copy(n, i) for n in (0, 3, 4)] for i in range(0, blocks, 2)}
    order = list(range(0, blocks, 2))[::-1]
    whole[0].start()
    for i in order:
        for c in paired[i]:
            c.start()
        if i == order[0]:
            whole[1].start()

    def store(i, parts):
        top = functools.reduce(jnp.maximum, [largest for _, largest, _ in parts])
        weights = [jnp.exp2((largest - top) * scale) for _, largest, _ in parts]
        inverse = 1.0 / sum(w * total for w, (_, _, total) in zip(weights, parts))
        merged = sum((w * inverse) * out for w, (out, _, _) in zip(weights, parts))
        out_ref[i : i + 2] = merged.reshape(2, rows, dim).astype(out_ref.dtype)

    def own_part(i):
        stat = stat_ref[i : i + 2].reshape(2 * rows, 128)
        return (out1_ref[i : i + 2].reshape(2 * rows, dim), *halves(stat))

    @pl.when(flag_ref[0] > 0)
    def _():
        whole[0].wait()
        for i in order:
            for c in paired[i]:
                c.wait()
            first = max(i - sent, 0)
            spans = [(first, 2, later)] if i >= sent else []
            first += 2 * len(spans)
            if first < kv_ref.shape[0]:
                spans.append((first, kv_ref.shape[0] - first, None))
            pieces = [
                (taken(kv_ref, f, n, 0, rows), taken(kv_ref, f, n, rows, rows), mask)
                for f, n, mask in spans
            ]
            parts = [softmax_parts(taken(q_ref, i, 2, 0, rows), pieces, scale), own_part(i)]
            if i < sent:
                if i == sent - 2:
                    whole[1].wait()
                stat = jnp.concatenate([sent_stats(back_ref, i + n, rows) for n in range(2)], axis=0)
                parts.append((taken(back_ref, i, 2, 0, rows).astype(jnp.float32), *halves(stat)))
            store(i, parts)

    @pl.when(flag_ref[0] == 0)
    def _():
        for c in whole:
            c.wait()
        for i in order:
            for c in paired[i]:
                c.wait()
            store(i, [own_part(i)])


def estimate(area, arrays):
    return pl.CostEstimate(
        flops=4 * HEAD_DIM * area,
        bytes_accessed=sum(2 * a.size for a in arrays),
        transcendentals=area,
    )


def self_attention(queries, keys, values, chunk, groups):
    rows, width = queries.shape
    heads = width // HEAD_DIM
    scale = HEAD_DIM ** (-0.5) * LOG2E
    x = lax.all_to_all(
        packed(queries, keys, values), "ctx", 0, 0, axis_index_groups=groups, tiled=True
    )
    arriving = shifted(x[LEFT:, rows:], "ctx", heads)
    asked = shifted(x[:LEFT, :rows], "ctx", -heads)
    area = (heads * rows) ** 2 // 2
    small = (LEFT * rows) ** 2 // 2
    out1, stat = pl.pallas_call(
        functools.partial(own_kernel, scale),
        out_shape=(
            jax.ShapeDtypeStruct((heads, rows, HEAD_DIM), jnp.float32),
            jax.ShapeDtypeStruct((heads, rows, 128), jnp.float32),
        ),
        cost_estimate=estimate(area, (x,)),
        name="own",
    )(x)
    answer = pl.pallas_call(
        functools.partial(later_kernel, scale),
        out_shape=jax.ShapeDtypeStruct((LEFT + 1, rows, HEAD_DIM), jnp.bfloat16),
        cost_estimate=estimate(small, (asked,)),
        name="later",
    )(asked, x)
    back = shifted(answer, "ctx", heads)
    return pl.pallas_call(
        functools.partial(previous_kernel, scale),
        out_shape=jax.ShapeDtypeStruct((heads, rows, HEAD_DIM), jnp.bfloat16),
        in_specs=[pl.BlockSpec(memory_space=pltpu.SMEM)]
        + [pl.BlockSpec(memory_space=pl.ANY)] * 5,
        out_specs=pl.BlockSpec(memory_space=pltpu.VMEM),
        scratch_shapes=[
            pltpu.VMEM((heads, rows, HEAD_DIM), x.dtype),
            pltpu.VMEM(arriving.shape, arriving.dtype),
            pltpu.VMEM(back.shape, back.dtype),
            pltpu.VMEM(out1.shape, out1.dtype),
            pltpu.VMEM(stat.shape, stat.dtype),
            pltpu.SemaphoreType.DMA((5, heads // 2)),
        ],
        cost_estimate=estimate(area - small, (x, out1, stat)),
        name="previous",
    )(chunk.reshape(1), x, arriving, back, out1, stat)


def wanted_pieces(table_ref, position, span_count):
    pieces = []
    place, plane = position % PLANE, position // PLANE
    for c in range(span_count):
        for slot in range(2):
            source = table_ref[c, slot] // 4
            for later in range(2):
                block = (source + later) // span_count
                relative = (block % PLANE) ^ place
                away = plane - block // PLANE
                column = relative // 2
                index = jnp.where(
                    column == 0, away, 1 + 2 * column + jnp.where(away == 1, 0, 1)
                )
                pieces.append((relative % 2 == 0, index, (source + later) % span_count))
    return pieces


def fetch(refs, rows, index, half, target, sem):
    size = target.shape[0]
    first = 0
    for ref in refs:
        count = ref.shape[0] // rows

        @pl.when((index >= first) & (index < first + count))
        def _(ref=ref, first=first):
            start = pl.multiple_of((index - first) * rows + half * size, size)
            pltpu.make_async_copy(ref.at[pl.ds(start, size), :], target, sem).start()

        first += count


def gather_kernel(span_count, position_ref, theirs_ref, *refs):
    *in_refs, out_ref, sems = refs
    rows = in_refs[0].shape[0]
    pieces = wanted_pieces(theirs_ref, position_ref[0], span_count)
    size = out_ref.shape[0] // len(pieces)
    targets = [out_ref.at[n * size : (n + 1) * size, :] for n in range(len(pieces))]
    for n, (here, index, half) in enumerate(pieces):
        fetch(in_refs, rows, jnp.where(here, index, -1), half, targets[n], sems.at[n])
    for n, (here, _, _) in enumerate(pieces):

        @pl.when(here)
        def _(n=n):
            pltpu.make_async_copy(in_refs[0].at[0:size, :], targets[n], sems.at[n]).wait()


def absorb_kernel(q_ref, weight_ref, out_ref, weights_ref, sems):
    rows, width = q_ref.shape
    span_count = out_ref.shape[0]
    span = rows // span_count
    steps, _, block = weights_ref.shape
    copies = [
        pltpu.make_async_copy(
            weight_ref.at[:, g * block : (g + 1) * block], weights_ref.at[g], sems.at[g]
        )
        for g in range(steps)
    ]
    for copy in copies:
        copy.start()
    for head in range(width // HEAD_DIM):
        g, first = divmod(head * HEAD_DIM, block)
        if first == 0:
            copies[g].wait()
        lanes = slice(head * HEAD_DIM, (head + 1) * HEAD_DIM)
        product = scores_of(q_ref[:, lanes], weights_ref[g, :, first : first + HEAD_DIM])
        product = product.astype(out_ref.dtype)
        for c in range(span_count):
            out_ref[c, head * span : (head + 1) * span, :] = product[c * span : (c + 1) * span]


def cross_kernel(scale, position_ref, table_ref, *refs):
    *in_refs, theirs_ref, asks_ref, weight_ref, out_ref = refs[:-6]
    rows_ref, all_asks_ref, weights_ref, sems, ask_sems, weight_sems = refs[-6:]
    rows, width = out_ref.shape
    steps, span_count, asked, _ = all_asks_ref.shape
    span = rows // span_count
    block = weights_ref.shape[2]
    pieces = wanted_pieces(table_ref, position_ref[0], span_count)
    targets = [rows_ref.at[n * span : (n + 1) * span, :] for n in range(len(pieces))]
    held = sum(ref.shape[0] for ref in in_refs) // rows
    for n, (here, index, half) in enumerate(pieces):
        fetch(in_refs, rows, jnp.where(here, index, held), half, targets[n], sems.at[n])

        @pl.when(jnp.logical_not(here))
        def _(n=n):
            source = theirs_ref.at[n * span : (n + 1) * span, :]
            pltpu.make_async_copy(source, targets[n], sems.at[n]).start()

    ask_copies = [
        pltpu.make_async_copy(
            asks_ref.at[:, g * asked : (g + 1) * asked, :], all_asks_ref.at[g], ask_sems.at[g]
        )
        for g in range(steps)
    ]
    weight_copies = [
        pltpu.make_async_copy(
            weight_ref.at[:, width + g * block : width + (g + 1) * block],
            weights_ref.at[g],
            weight_sems.at[g],
        )
        for g in range(steps)
    ]
    for g in range(steps):
        ask_copies[g].start()
        weight_copies[g].start()
    for n in range(len(pieces)):
        pltpu.make_async_copy(theirs_ref.at[0:span, :], targets[n], sems.at[n]).wait()

    keys_of_span = rows_ref.shape[0] // span_count
    slot = lax.broadcasted_iota(jnp.int32, (asked, keys_of_span), 1) // (2 * span)
    counts = [table_ref[c, 0] % 4 for c in range(span_count)]
    for g in range(steps):
        ask_copies[g].wait()
        means = []
        for c in range(span_count):
            keys = rows_ref[c * keys_of_span : (c + 1) * keys_of_span, :]
            s = jnp.where(slot < counts[c], scores_of(all_asks_ref[g, c], keys), MASKED_SCORE)
            p = jnp.exp2((s - jnp.max(s, axis=1, keepdims=True)) * scale)
            inverse = jnp.where(counts[c] > 0, 1.0 / jnp.sum(p, axis=1, keepdims=True), 0.0)
            mean = jnp.dot(p.astype(jnp.bfloat16), keys, preferred_element_type=jnp.float32)
            means.append((mean * inverse).astype(jnp.bfloat16))
        weight_copies[g].wait()
        for h in range(block // HEAD_DIM):
            mean = jnp.concatenate([m[h * span : (h + 1) * span] for m in means], axis=0)
            inner = slice(h * HEAD_DIM, (h + 1) * HEAD_DIM)
            lanes = slice(g * block + h * HEAD_DIM, g * block + (h + 1) * HEAD_DIM)
            out_ref[:, lanes] = jnp.dot(
                mean, weights_ref[g, :, inner], preferred_element_type=jnp.float32
            )


def cross_attention(cross_queries, encoded, weight, counts, sources, position):
    rows, width = cross_queries.shape
    span_count = counts.shape[0]
    depth = encoded.shape[1]
    place = position % PLANE
    one_back = shifted(encoded, "ctx", PLANE)
    table = sources * 4 + counts[:, None]
    before = shifted(table, "ctx", 1)
    table = jnp.concatenate([before[-1:], table[:-1]], axis=0)
    their_table = swapped(table, "ctx", 1)
    two_back = shifted(one_back, "ctx", PLANE)

    near = []
    for bit in (2, 4, 6):
        other = jnp.where(place < (place ^ bit), encoded, two_back)
        near.append(swapped(jnp.concatenate([one_back, other], axis=0), "ctx", bit))

    held = [encoded, one_back, two_back, *near]
    where = position.reshape(1)
    picked = span_count * 4 * SPAN
    pieces = picked // SPAN
    smem, anywhere = (pl.BlockSpec(memory_space=m) for m in (pltpu.SMEM, pl.ANY))
    vmem = pl.BlockSpec(memory_space=pltpu.VMEM)
    theirs = pl.pallas_call(
        functools.partial(gather_kernel, span_count),
        out_shape=jax.ShapeDtypeStruct((picked, depth), encoded.dtype),
        in_specs=[smem] * 2 + [anywhere] * len(held),
        out_specs=vmem,
        scratch_shapes=[pltpu.SemaphoreType.DMA((pieces,))],
        cost_estimate=pl.CostEstimate(
            flops=0, bytes_accessed=8 * picked * depth, transcendentals=0
        ),
        name="gather",
    )(where, their_table, *held)
    theirs = swapped(theirs, "ctx", 1)

    heads = width // HEAD_DIM
    block = 4 * HEAD_DIM
    steps = width // block
    asks = pl.pallas_call(
        absorb_kernel,
        out_shape=jax.ShapeDtypeStruct((span_count, heads * SPAN, depth), jnp.bfloat16),
        in_specs=[vmem, anywhere],
        out_specs=vmem,
        scratch_shapes=[
            pltpu.VMEM((steps, depth, block), weight.dtype),
            pltpu.SemaphoreType.DMA((steps,)),
        ],
        cost_estimate=pl.CostEstimate(
            flops=2 * rows * depth * width, bytes_accessed=2 * weight.size, transcendentals=0
        ),
        name="absorb",
    )(cross_queries, weight)
    block = 8 * HEAD_DIM
    steps = width // block
    cost = pl.CostEstimate(
        flops=4 * picked * depth * heads * SPAN + 2 * rows * depth * width,
        bytes_accessed=weight.size + asks.size * 2 + picked * depth * 4,
        transcendentals=picked * SPAN * heads,
    )
    return pl.pallas_call(
        functools.partial(cross_kernel, HEAD_DIM ** (-0.5) * LOG2E),
        out_shape=jax.ShapeDtypeStruct((rows, width), jnp.float32),
        in_specs=[smem] * 2 + [anywhere] * (len(held) + 3),
        out_specs=vmem,
        scratch_shapes=[
            pltpu.VMEM((picked, depth), encoded.dtype),
            pltpu.VMEM((steps, span_count, heads * SPAN // steps, depth), asks.dtype),
            pltpu.VMEM((steps, depth, block), weight.dtype),
            pltpu.SemaphoreType.DMA((pieces,)),
            pltpu.SemaphoreType.DMA((steps,)),
            pltpu.SemaphoreType.DMA((steps,)),
        ],
        cost_estimate=cost,
        name="cross",
    )(where, table, *held, theirs, asks, weight)


def sum_kernel(self_ref, cross_ref, out_ref):
    for head in range(self_ref.shape[0]):
        lanes = slice(head * HEAD_DIM, (head + 1) * HEAD_DIM)
        out_ref[:, lanes] = (self_ref[head].astype(jnp.float32) + cross_ref[:, lanes]).astype(
            out_ref.dtype
        )


def per_device(
    queries, self_keys, self_values, cross_queries, encoded, neighbour_weight, counts, sources
):
    position = lax.axis_index("ctx")
    count = lax.axis_size("ctx")
    groups = [list(range(first, first + HEADS)) for first in range(0, count, HEADS)]
    cross_part = cross_attention(
        cross_queries, encoded, neighbour_weight, counts, sources, position
    )
    by_head = self_attention(queries, self_keys, self_values, position // HEADS, groups)
    self_part = lax.all_to_all(by_head, "ctx", 0, 0, axis_index_groups=groups, tiled=True)
    return pl.pallas_call(
        sum_kernel,
        out_shape=jax.ShapeDtypeStruct(queries.shape, jnp.bfloat16),
        name="total",
    )(self_part, cross_part)


def solution(mesh):
    return jax.shard_map(
        per_device,
        mesh=mesh,
        in_specs=(
            P(("groups", "ctx"), None),
            P(("groups", "ctx"), None),
            P(("groups", "ctx"), None),
            P(("groups", "ctx"), None),
            P(("groups", "ctx"), None),
            P(),
            P(("groups", "ctx")),
            P(("groups", "ctx"), None),
        ),
        out_specs=P(("groups", "ctx"), None),
        check_vma=False,
    )
```

```python
import functools

import jax
import jax.numpy as jnp
from jax import lax
from jax.experimental import pallas as pl
from jax.experimental.pallas import tpu as pltpu
from jax.sharding import PartitionSpec as P


HEADS = 16
HEAD_DIM = 128
SPAN = 64
PLANE = 8
LEFT = 8

MASKED_SCORE = -1e30
LOG2E = 1.4426950408889634


def shifted(value, axis, steps):
    count = lax.axis_size(axis)
    first, last = (max(0, -steps), min(count, count - steps))
    return lax.ppermute(value, axis, [(source, source + steps) for source in range(first, last)])


def swapped(value, axis, bit):
    count = lax.axis_size(axis)
    return lax.ppermute(value, axis, [(source, source ^ bit) for source in range(count)])


def pack_kernel(*refs):
    *in_refs, out_ref = refs
    rows = in_refs[0].shape[0]
    for head in range(out_ref.shape[0]):
        columns = slice(head * HEAD_DIM, (head + 1) * HEAD_DIM)
        for n, ref in enumerate(in_refs):
            out_ref[head, n * rows : (n + 1) * rows, :] = ref[:, columns]


def packed(*arrays):
    rows, width = arrays[0].shape
    return pl.pallas_call(
        pack_kernel,
        out_shape=jax.ShapeDtypeStruct(
            (width // HEAD_DIM, len(arrays) * rows, HEAD_DIM), arrays[0].dtype
        ),
        cost_estimate=pl.CostEstimate(
            flops=0, bytes_accessed=4 * len(arrays) * rows * width, transcendentals=0
        ),
        name="pack",
    )(*arrays)


def scores_of(q, k):
    return lax.dot_general(q, k, (((1,), (1,)), ((), ())), preferred_element_type=jnp.float32)


def softmax_parts(q, pieces, scale):
    scores = []
    for k, _, mask in pieces:
        s = scores_of(q, k)
        scores.append(s if mask is None else jnp.where(mask, s, MASKED_SCORE))
    largest = functools.reduce(
        jnp.maximum, [jnp.max(s, axis=1, keepdims=True) for s in scores]
    )
    total, out = None, None
    for s, (_, v, _) in zip(scores, pieces):
        p = jnp.exp2((s - largest) * scale)
        t = jnp.sum(p, axis=1, keepdims=True)
        o = jnp.dot(p.astype(jnp.bfloat16), v, preferred_element_type=jnp.float32)
        total = t if total is None else total + t
        out = o if out is None else out + o
    return out, largest, total


def with_stats(largest, total):
    lane = lax.broadcasted_iota(jnp.int32, (largest.shape[0], 128), 1)
    return jnp.where(lane < 64, largest, total)


def halves(stat):
    return stat[:, 0:1], stat[:, 64:65]


def thirds(x):
    high = x.astype(jnp.bfloat16)
    rest = x - high.astype(jnp.float32)
    middle = rest.astype(jnp.bfloat16)
    low = (rest - middle.astype(jnp.float32)).astype(jnp.bfloat16)
    return high, middle, low


def taken(ref, first, count, start, rows):
    return ref[first : first + count, start : start + rows, :].reshape(count * rows, ref.shape[2])


def triangle(size, keep):
    row = lax.broadcasted_iota(jnp.int32, (size, size), 0)
    column = lax.broadcasted_iota(jnp.int32, (size, size), 1)
    return keep(column, row)


def own_kernel(scale, x_ref, out_ref, stat_ref):
    blocks, triple, dim = x_ref.shape
    rows = triple // 3
    causal = triangle(2 * rows, lambda column, row: column <= row)
    for i in range(0, blocks, 2):
        spans = [(i, 2, causal)] + ([(0, i, None)] if i else [])
        pieces = [
            (taken(x_ref, f, n, rows, rows), taken(x_ref, f, n, 2 * rows, rows), mask)
            for f, n, mask in spans
        ]
        out, largest, total = softmax_parts(taken(x_ref, i, 2, 0, rows), pieces, scale)
        out_ref[i : i + 2] = out.reshape(2, rows, dim)
        stat_ref[i : i + 2] = with_stats(largest, total).reshape(2, rows, 128)


def later_kernel(scale, q_ref, x_ref, out_ref):
    blocks, rows, dim = q_ref.shape
    later = triangle(2 * rows, lambda column, row: column > row)
    out_ref[blocks] = jnp.zeros((rows, dim), out_ref.dtype)
    for i in range(0, blocks, 2):
        spans = [(i, 2, later)] + ([(i + 2, blocks - i - 2, None)] if i + 2 < blocks else [])
        pieces = [
            (taken(x_ref, f, n, rows, rows), taken(x_ref, f, n, 2 * rows, rows), mask)
            for f, n, mask in spans
        ]
        out, largest, total = softmax_parts(taken(q_ref, i, 2, 0, rows), pieces, scale)
        out_ref[i : i + 2] = out.reshape(2, rows, dim).astype(out_ref.dtype)
        stat = with_stats(largest, total)
        for n in range(2):
            turned = stat[n * rows : (n + 1) * rows].T
            for m, row in enumerate((turned[0:1], turned[64:65])):
                for k, part in enumerate(thirds(row)):
                    place = ((i + n) * 2 + m) * 3 + k
                    out_ref[blocks, place : place + 1, :] = part


def sent_stats(ref, block, rows):
    values = []
    for m in range(2):
        place = (block * 2 + m) * 3
        three = ref[ref.shape[0] - 1, place : place + 3, :].astype(jnp.float32)
        values.append(three[0:1] + three[1:2] + three[2:3])
    sublane = lax.broadcasted_iota(jnp.int32, (rows, 128), 0)
    return jnp.where(sublane < 64, values[0], values[1]).T


def merged(parts, scale):
    top = functools.reduce(jnp.maximum, [largest for _, largest, _ in parts])
    weights = [jnp.exp2((largest - top) * scale) for _, largest, _ in parts]
    total = sum(w * t for w, (_, _, t) in zip(weights, parts))
    return sum(w * out for w, (out, _, _) in zip(weights, parts)), top, total


def previous_kernel(scale, flag_ref, q_ref, kv_ref, out1_ref, stat1_ref, out_ref, part_ref, stat_ref):
    blocks, rows, dim = q_ref.shape
    waiting = part_ref.shape[0]
    later = triangle(2 * rows, lambda column, row: column > row)

    def own_part(i):
        stat = stat1_ref[i : i + 2].reshape(2 * rows, 128)
        return (out1_ref[i : i + 2].reshape(2 * rows, dim), *halves(stat))

    def store(i, part):
        out, largest, total = part
        if i < waiting:
            part_ref[i : i + 2] = out.reshape(2, rows, dim)
            stat_ref[i : i + 2] = with_stats(largest, total).reshape(2, rows, 128)
        else:
            out = out * (1.0 / total)
            out_ref[i : i + 2] = out.reshape(2, rows, dim).astype(out_ref.dtype)

    @pl.when(flag_ref[0] > 0)
    def _():
        for i in range(0, blocks, 2):
            first = max(i - waiting, 0)
            spans = [(first, 2, later)] if i >= waiting else []
            first += 2 * len(spans)
            if first < kv_ref.shape[0]:
                spans.append((first, kv_ref.shape[0] - first, None))
            pieces = [
                (taken(kv_ref, f, n, 0, rows), taken(kv_ref, f, n, rows, rows), mask)
                for f, n, mask in spans
            ]
            part = softmax_parts(taken(q_ref, i, 2, 0, rows), pieces, scale)
            store(i, merged([part, own_part(i)], scale))

    @pl.when(flag_ref[0] == 0)
    def _():
        part_ref[...] = out1_ref[0:waiting]
        stat_ref[...] = stat1_ref[0:waiting]
        for i in range(waiting, blocks, 2):
            store(i, own_part(i))


def merge_kernel(scale, flag_ref, part_ref, stat_ref, back_ref, rest_ref, out_ref, done_ref, sem):
    del rest_ref
    blocks, rows, dim = part_ref.shape
    for i in range(0, blocks, 2):
        stat = stat_ref[i : i + 2].reshape(2 * rows, 128)
        parts = [(part_ref[i : i + 2].reshape(2 * rows, dim), *halves(stat))]
        stat = jnp.concatenate([sent_stats(back_ref, i + n, rows) for n in range(2)], axis=0)
        largest, total = halves(stat)
        largest = jnp.where(flag_ref[0] > 0, largest, MASKED_SCORE)
        parts.append((taken(back_ref, i, 2, 0, rows).astype(jnp.float32), largest, total))
        out, _, total = merged(parts, scale)
        done_ref[i : i + 2] = (out * (1.0 / total)).reshape(2, rows, dim).astype(done_ref.dtype)
    copy = pltpu.make_async_copy(done_ref, out_ref.at[0:blocks], sem)
    copy.start()
    copy.wait()


def estimate(area, arrays):
    return pl.CostEstimate(
        flops=4 * HEAD_DIM * area,
        bytes_accessed=sum(2 * a.size for a in arrays),
        transcendentals=area,
    )


def self_attention(queries, keys, values, chunk, groups):
    rows, width = queries.shape
    heads = width // HEAD_DIM
    scale = HEAD_DIM ** (-0.5) * LOG2E
    x = lax.all_to_all(
        packed(queries, keys, values), "ctx", 0, 0, axis_index_groups=groups, tiled=True
    )
    arriving = shifted(x[LEFT:, rows:], "ctx", heads)
    asked = shifted(x[:LEFT, :rows], "ctx", -heads)
    area = (heads * rows) ** 2 // 2
    small = (LEFT * rows) ** 2 // 2
    out1, stat = pl.pallas_call(
        functools.partial(own_kernel, scale),
        out_shape=(
            jax.ShapeDtypeStruct((heads, rows, HEAD_DIM), jnp.float32),
            jax.ShapeDtypeStruct((heads, rows, 128), jnp.float32),
        ),
        cost_estimate=estimate(area, (x,)),
        name="own",
    )(x)
    smem = pl.BlockSpec(memory_space=pltpu.SMEM)

    def first_blocks(count, height):
        return pl.BlockSpec((count, height, HEAD_DIM), lambda *_: (0, 0, 0))

    answer = pl.pallas_call(
        functools.partial(later_kernel, scale),
        out_shape=jax.ShapeDtypeStruct((LEFT + 1, rows, HEAD_DIM), jnp.bfloat16),
        grid=(1,),
        in_specs=[first_blocks(LEFT, rows), first_blocks(LEFT, 3 * rows)],
        out_specs=first_blocks(LEFT + 1, rows),
        cost_estimate=estimate(small, (asked,)),
        name="later",
    )(asked, x)
    back = shifted(answer, "ctx", heads)
    flag = chunk.reshape(1)
    all_blocks = first_blocks(heads, rows)
    rest, part, stat = pl.pallas_call(
        functools.partial(previous_kernel, scale),
        out_shape=(
            jax.ShapeDtypeStruct((heads, rows, HEAD_DIM), jnp.bfloat16),
            jax.ShapeDtypeStruct((LEFT, rows, HEAD_DIM), jnp.float32),
            jax.ShapeDtypeStruct((LEFT, rows, 128), jnp.float32),
        ),
        grid=(1,),
        in_specs=[smem, all_blocks, first_blocks(heads - LEFT, 2 * rows), all_blocks, all_blocks],
        out_specs=(all_blocks, first_blocks(LEFT, rows), first_blocks(LEFT, rows)),
        cost_estimate=estimate(area - small, (x, out1, stat)),
        name="previous",
    )(flag, x, arriving, out1, stat)
    vmem, anywhere = (pl.BlockSpec(memory_space=m) for m in (pltpu.VMEM, pl.ANY))
    return pl.pallas_call(
        functools.partial(merge_kernel, scale),
        out_shape=jax.ShapeDtypeStruct(rest.shape, rest.dtype),
        in_specs=[smem, vmem, vmem, vmem, anywhere],
        out_specs=anywhere,
        input_output_aliases={4: 0},
        scratch_shapes=[
            pltpu.VMEM((LEFT, rows, HEAD_DIM), rest.dtype),
            pltpu.SemaphoreType.DMA(()),
        ],
        cost_estimate=estimate(0, (part, stat, back)),
        name="merge",
    )(flag, part, stat, back, rest)


def wanted_pieces(table_ref, position, span_count):
    pieces = []
    place, plane = position % PLANE, position // PLANE
    for c in range(span_count):
        for slot in range(2):
            source = table_ref[c, slot] // 4
            for later in range(2):
                block = (source + later) // span_count
                relative = (block % PLANE) ^ place
                away = plane - block // PLANE
                column = relative // 2
                index = jnp.where(
                    column == 0, away, 1 + 2 * column + jnp.where(away == 1, 0, 1)
                )
                pieces.append((relative % 2 == 0, index, (source + later) % span_count))
    return pieces


def fetch(refs, rows, index, half, target, sem):
    size = target.shape[0]
    first = 0
    for ref in refs:
        count = ref.shape[0] // rows

        @pl.when((index >= first) & (index < first + count))
        def _(ref=ref, first=first):
            start = pl.multiple_of((index - first) * rows + half * size, size)
            pltpu.make_async_copy(ref.at[pl.ds(start, size), :], target, sem).start()

        first += count


def gather_kernel(span_count, position_ref, theirs_ref, *refs):
    *in_refs, out_ref, sems = refs
    rows = in_refs[0].shape[0]
    pieces = wanted_pieces(theirs_ref, position_ref[0], span_count)
    size = out_ref.shape[0] // len(pieces)
    targets = [out_ref.at[n * size : (n + 1) * size, :] for n in range(len(pieces))]
    for n, (here, index, half) in enumerate(pieces):
        fetch(in_refs, rows, jnp.where(here, index, -1), half, targets[n], sems.at[n])
    for n, (here, _, _) in enumerate(pieces):

        @pl.when(here)
        def _(n=n):
            pltpu.make_async_copy(in_refs[0].at[0:size, :], targets[n], sems.at[n]).wait()


def absorb_kernel(q_ref, weight_ref, out_ref, weights_ref, sems):
    rows, width = q_ref.shape
    span_count = out_ref.shape[0]
    span = rows // span_count
    steps, _, block = weights_ref.shape
    copies = [
        pltpu.make_async_copy(
            weight_ref.at[:, g * block : (g + 1) * block], weights_ref.at[g], sems.at[g]
        )
        for g in range(steps)
    ]
    for copy in copies:
        copy.start()
    for head in range(width // HEAD_DIM):
        g, first = divmod(head * HEAD_DIM, block)
        if first == 0:
            copies[g].wait()
        lanes = slice(head * HEAD_DIM, (head + 1) * HEAD_DIM)
        product = scores_of(q_ref[:, lanes], weights_ref[g, :, first : first + HEAD_DIM])
        product = product.astype(out_ref.dtype)
        for c in range(span_count):
            out_ref[c, head * span : (head + 1) * span, :] = product[c * span : (c + 1) * span]


def cross_kernel(scale, position_ref, table_ref, *refs):
    *in_refs, theirs_ref, asks_ref, weight_ref, out_ref = refs[:-6]
    rows_ref, all_asks_ref, weights_ref, sems, ask_sems, weight_sems = refs[-6:]
    rows, width = out_ref.shape
    steps, span_count, asked, _ = all_asks_ref.shape
    span = rows // span_count
    block = weights_ref.shape[2]
    pieces = wanted_pieces(table_ref, position_ref[0], span_count)
    targets = [rows_ref.at[n * span : (n + 1) * span, :] for n in range(len(pieces))]
    held = sum(ref.shape[0] for ref in in_refs) // rows
    for n, (here, index, half) in enumerate(pieces):
        fetch(in_refs, rows, jnp.where(here, index, held), half, targets[n], sems.at[n])

        @pl.when(jnp.logical_not(here))
        def _(n=n):
            source = theirs_ref.at[n * span : (n + 1) * span, :]
            pltpu.make_async_copy(source, targets[n], sems.at[n]).start()

    ask_copies = [
        pltpu.make_async_copy(
            asks_ref.at[:, g * asked : (g + 1) * asked, :], all_asks_ref.at[g], ask_sems.at[g]
        )
        for g in range(steps)
    ]
    weight_copies = [
        pltpu.make_async_copy(
            weight_ref.at[:, width + g * block : width + (g + 1) * block],
            weights_ref.at[g],
            weight_sems.at[g],
        )
        for g in range(steps)
    ]
    for g in range(steps):
        ask_copies[g].start()
        weight_copies[g].start()
    for n in range(len(pieces)):
        pltpu.make_async_copy(theirs_ref.at[0:span, :], targets[n], sems.at[n]).wait()

    keys_of_span = rows_ref.shape[0] // span_count
    slot = lax.broadcasted_iota(jnp.int32, (asked, keys_of_span), 1) // (2 * span)
    counts = [table_ref[c, 0] % 4 for c in range(span_count)]
    for g in range(steps):
        ask_copies[g].wait()
        means = []
        for c in range(span_count):
            keys = rows_ref[c * keys_of_span : (c + 1) * keys_of_span, :]
            s = jnp.where(slot < counts[c], scores_of(all_asks_ref[g, c], keys), MASKED_SCORE)
            p = jnp.exp2((s - jnp.max(s, axis=1, keepdims=True)) * scale)
            inverse = jnp.where(counts[c] > 0, 1.0 / jnp.sum(p, axis=1, keepdims=True), 0.0)
            mean = jnp.dot(p.astype(jnp.bfloat16), keys, preferred_element_type=jnp.float32)
            means.append((mean * inverse).astype(jnp.bfloat16))
        weight_copies[g].wait()
        for h in range(block // HEAD_DIM):
            mean = jnp.concatenate([m[h * span : (h + 1) * span] for m in means], axis=0)
            inner = slice(h * HEAD_DIM, (h + 1) * HEAD_DIM)
            lanes = slice(g * block + h * HEAD_DIM, g * block + (h + 1) * HEAD_DIM)
            out_ref[:, lanes] = jnp.dot(
                mean, weights_ref[g, :, inner], preferred_element_type=jnp.float32
            )


def cross_attention(cross_queries, encoded, weight, counts, sources, position):
    rows, width = cross_queries.shape
    span_count = counts.shape[0]
    depth = encoded.shape[1]
    place = position % PLANE
    one_back = shifted(encoded, "ctx", PLANE)
    table = sources * 4 + counts[:, None]
    before = shifted(table, "ctx", 1)
    table = jnp.concatenate([before[-1:], table[:-1]], axis=0)
    their_table = swapped(table, "ctx", 1)
    two_back = shifted(one_back, "ctx", PLANE)

    near = []
    for bit in (2, 4, 6):
        other = jnp.where(place < (place ^ bit), encoded, two_back)
        near.append(swapped(jnp.concatenate([one_back, other], axis=0), "ctx", bit))

    held = [encoded, one_back, two_back, *near]
    where = position.reshape(1)
    picked = span_count * 4 * SPAN
    pieces = picked // SPAN
    smem, anywhere = (pl.BlockSpec(memory_space=m) for m in (pltpu.SMEM, pl.ANY))
    vmem = pl.BlockSpec(memory_space=pltpu.VMEM)
    theirs = pl.pallas_call(
        functools.partial(gather_kernel, span_count),
        out_shape=jax.ShapeDtypeStruct((picked, depth), encoded.dtype),
        in_specs=[smem] * 2 + [anywhere] * len(held),
        out_specs=vmem,
        scratch_shapes=[pltpu.SemaphoreType.DMA((pieces,))],
        cost_estimate=pl.CostEstimate(
            flops=0, bytes_accessed=8 * picked * depth, transcendentals=0
        ),
        name="gather",
    )(where, their_table, *held)
    theirs = swapped(theirs, "ctx", 1)

    heads = width // HEAD_DIM
    block = 4 * HEAD_DIM
    steps = width // block
    asks = pl.pallas_call(
        absorb_kernel,
        out_shape=jax.ShapeDtypeStruct((span_count, heads * SPAN, depth), jnp.bfloat16),
        in_specs=[vmem, anywhere],
        out_specs=vmem,
        scratch_shapes=[
            pltpu.VMEM((steps, depth, block), weight.dtype),
            pltpu.SemaphoreType.DMA((steps,)),
        ],
        cost_estimate=pl.CostEstimate(
            flops=2 * rows * depth * width, bytes_accessed=2 * weight.size, transcendentals=0
        ),
        name="absorb",
    )(cross_queries, weight)
    block = 8 * HEAD_DIM
    steps = width // block
    cost = pl.CostEstimate(
        flops=4 * picked * depth * heads * SPAN + 2 * rows * depth * width,
        bytes_accessed=weight.size + asks.size * 2 + picked * depth * 4,
        transcendentals=picked * SPAN * heads,
    )
    return pl.pallas_call(
        functools.partial(cross_kernel, HEAD_DIM ** (-0.5) * LOG2E),
        out_shape=jax.ShapeDtypeStruct((rows, width), jnp.float32),
        in_specs=[smem] * 2 + [anywhere] * (len(held) + 3),
        out_specs=vmem,
        scratch_shapes=[
            pltpu.VMEM((picked, depth), encoded.dtype),
            pltpu.VMEM((steps, span_count, heads * SPAN // steps, depth), asks.dtype),
            pltpu.VMEM((steps, depth, block), weight.dtype),
            pltpu.SemaphoreType.DMA((pieces,)),
            pltpu.SemaphoreType.DMA((steps,)),
            pltpu.SemaphoreType.DMA((steps,)),
        ],
        cost_estimate=cost,
        name="cross",
    )(where, table, *held, theirs, asks, weight)


def sum_kernel(self_ref, cross_ref, out_ref):
    for head in range(self_ref.shape[0]):
        lanes = slice(head * HEAD_DIM, (head + 1) * HEAD_DIM)
        out_ref[:, lanes] = (self_ref[head].astype(jnp.float32) + cross_ref[:, lanes]).astype(
            out_ref.dtype
        )


def per_device(
    queries, self_keys, self_values, cross_queries, encoded, neighbour_weight, counts, sources
):
    position = lax.axis_index("ctx")
    count = lax.axis_size("ctx")
    groups = [list(range(first, first + HEADS)) for first in range(0, count, HEADS)]
    cross_part = cross_attention(
        cross_queries, encoded, neighbour_weight, counts, sources, position
    )
    by_head = self_attention(queries, self_keys, self_values, position // HEADS, groups)
    self_part = lax.all_to_all(by_head, "ctx", 0, 0, axis_index_groups=groups, tiled=True)
    return pl.pallas_call(
        sum_kernel,
        out_shape=jax.ShapeDtypeStruct(queries.shape, jnp.bfloat16),
        name="total",
    )(self_part, cross_part)


def solution(mesh):
    return jax.shard_map(
        per_device,
        mesh=mesh,
        in_specs=(
            P(("groups", "ctx"), None),
            P(("groups", "ctx"), None),
            P(("groups", "ctx"), None),
            P(("groups", "ctx"), None),
            P(("groups", "ctx"), None),
            P(),
            P(("groups", "ctx")),
            P(("groups", "ctx"), None),
        ),
        out_specs=P(("groups", "ctx"), None),
        check_vma=False,
    )
```

```python
import functools

import jax
import jax.numpy as jnp
from jax import lax
from jax.experimental import pallas as pl
from jax.experimental.pallas import tpu as pltpu
from jax.sharding import PartitionSpec as P


HEADS = 16
HEAD_DIM = 128
SPAN = 64
PLANE = 8

MASKED_SCORE = -1e30
LOG2E = 1.4426950408889634


def shifted(value, axis, steps):
    count = lax.axis_size(axis)
    first, last = (max(0, -steps), min(count, count - steps))
    return lax.ppermute(value, axis, [(source, source + steps) for source in range(first, last)])


def swapped(value, axis, bit):
    count = lax.axis_size(axis)
    return lax.ppermute(value, axis, [(source, source ^ bit) for source in range(count)])


def pack_kernel(*refs):
    *in_refs, out_ref = refs
    rows = in_refs[0].shape[0]
    for head in range(out_ref.shape[0]):
        columns = slice(head * HEAD_DIM, (head + 1) * HEAD_DIM)
        for n, ref in enumerate(in_refs):
            out_ref[head, n * rows : (n + 1) * rows, :] = ref[:, columns]


def packed(*arrays):
    rows, width = arrays[0].shape
    return pl.pallas_call(
        pack_kernel,
        out_shape=jax.ShapeDtypeStruct(
            (width // HEAD_DIM, len(arrays) * rows, HEAD_DIM), arrays[0].dtype
        ),
        cost_estimate=pl.CostEstimate(
            flops=0, bytes_accessed=4 * len(arrays) * rows * width, transcendentals=0
        ),
        name="pack",
    )(*arrays)


def scores_of(q, k):
    return lax.dot_general(q, k, (((1,), (1,)), ((), ())), preferred_element_type=jnp.float32)


def softmax_parts(q, pieces, scale, start=None):
    scores = []
    for k, _, mask in pieces:
        s = scores_of(q, k)
        scores.append(s if mask is None else jnp.where(mask, s, MASKED_SCORE))
    largest = functools.reduce(jnp.maximum, [jnp.max(s, axis=1, keepdims=True) for s in scores])
    total, out = None, None
    if start is not None:
        out, before, total = start
        largest = jnp.maximum(largest, before)
        weight = jnp.exp2((before - largest) * scale)
        out, total = out * weight, total * weight
    for s, (_, v, _) in zip(scores, pieces):
        p = jnp.exp2((s - largest) * scale)
        t = jnp.sum(p, axis=1, keepdims=True)
        o = jnp.dot(p.astype(jnp.bfloat16), v, preferred_element_type=jnp.float32)
        total = t if total is None else total + t
        out = o if out is None else out + o
    return out, largest, total


def with_stats(largest, total):
    lane = lax.broadcasted_iota(jnp.int32, (largest.shape[0], 128), 1)
    return jnp.where(lane < 64, largest, total)


def halves(stat):
    return stat[:, 0:1], stat[:, 64:65]


def thirds(x):
    high = x.astype(jnp.bfloat16)
    rest = x - high.astype(jnp.float32)
    middle = rest.astype(jnp.bfloat16)
    low = (rest - middle.astype(jnp.float32)).astype(jnp.bfloat16)
    return high, middle, low


def taken(ref, first, count, start, rows):
    return ref[first : first + count, start : start + rows, :].reshape(count * rows, ref.shape[2])


def triangle(size, keep):
    row = lax.broadcasted_iota(jnp.int32, (size, size), 0)
    column = lax.broadcasted_iota(jnp.int32, (size, size), 1)
    return keep(column, row)


def own_kernel(scale, x_ref, out_ref, stat_ref):
    blocks, triple, dim = x_ref.shape
    rows = triple // 3
    causal = triangle(2 * rows, lambda column, row: column <= row)
    for i in range(0, blocks, 2):
        spans = [(i, 2, causal)] + ([(0, i, None)] if i else [])
        pieces = [
            (taken(x_ref, f, n, rows, rows), taken(x_ref, f, n, 2 * rows, rows), mask)
            for f, n, mask in spans
        ]
        out, largest, total = softmax_parts(taken(x_ref, i, 2, 0, rows), pieces, scale)
        out_ref[i : i + 2] = out.reshape(2, rows, dim)
        stat_ref[i : i + 2] = with_stats(largest, total).reshape(2, rows, 128)


def later_kernel(scale, q_ref, x_ref, out_ref):
    blocks, rows, dim = q_ref.shape
    later = triangle(2 * rows, lambda column, row: column > row)
    out_ref[blocks] = jnp.zeros((rows, dim), out_ref.dtype)
    for i in range(0, blocks, 2):
        spans = [(i, 2, later)] + ([(i + 2, blocks - i - 2, None)] if i + 2 < blocks else [])
        pieces = [
            (taken(x_ref, f, n, rows, rows), taken(x_ref, f, n, 2 * rows, rows), mask)
            for f, n, mask in spans
        ]
        out, largest, total = softmax_parts(taken(q_ref, i, 2, 0, rows), pieces, scale)
        out_ref[i : i + 2] = out.reshape(2, rows, dim).astype(out_ref.dtype)
        stat = with_stats(largest, total)
        for n in range(2):
            turned = stat[n * rows : (n + 1) * rows].T
            for m, row in enumerate((turned[0:1], turned[64:65])):
                for k, part in enumerate(thirds(row)):
                    place = ((i + n) * 2 + m) * 3 + k
                    out_ref[blocks, place : place + 1, :] = part


def sent_stats(ref, block, rows):
    values = []
    for m in range(2):
        place = (block * 2 + m) * 3
        three = ref[ref.shape[0] - 1, place : place + 3, :].astype(jnp.float32)
        values.append(three[0:1] + three[1:2] + three[2:3])
    sublane = lax.broadcasted_iota(jnp.int32, (rows, 128), 0)
    return jnp.where(sublane < 64, values[0], values[1]).T


def previous_kernel(scale, flag_ref, q_ref, kv_ref, out1_ref, stat1_ref, out_ref, part_ref, stat_ref):
    blocks, rows, dim = q_ref.shape
    waiting = part_ref.shape[0]
    half = rows // 2
    later = triangle(2 * rows, lambda column, row: column > row)

    def arrived(first, count, start):
        return jnp.concatenate(
            [
                kv_ref[place, start : start + half, :]
                for block in range(first, first + count)
                for place in (block, waiting + block)
            ],
            axis=0,
        )

    def own_part(i):
        stat = stat1_ref[i : i + 2].reshape(2 * rows, 128)
        return (out1_ref[i : i + 2].reshape(2 * rows, dim), *halves(stat))

    def store(i, part):
        out, largest, total = part
        if i < waiting:
            part_ref[i : i + 2] = out.reshape(2, rows, dim)
            stat_ref[i : i + 2] = with_stats(largest, total).reshape(2, rows, 128)
        else:
            out = out * (1.0 / total)
            out_ref[i : i + 2] = out.reshape(2, rows, dim).astype(out_ref.dtype)

    @pl.when(flag_ref[0] > 0)
    def _():
        for i in range(0, blocks, 2):
            first = max(i - waiting, 0)
            spans = [(first, 2, later)] if i >= waiting else []
            first += 2 * len(spans)
            if first < waiting:
                spans.append((first, waiting - first, None))
            pieces = [(arrived(f, n, 0), arrived(f, n, half), mask) for f, n, mask in spans]
            store(i, softmax_parts(taken(q_ref, i, 2, 0, rows), pieces, scale, own_part(i)))

    @pl.when(flag_ref[0] == 0)
    def _():
        part_ref[...] = out1_ref[0:waiting]
        stat_ref[...] = stat1_ref[0:waiting]
        for i in range(waiting, blocks, 2):
            store(i, own_part(i))


def merge_kernel(scale, flag_ref, part_ref, stat_ref, back_ref, rest_ref, out_ref, done_ref, sem):
    del rest_ref
    blocks, rows, dim = part_ref.shape
    for i in range(0, blocks, 2):
        out1, largest1, total1 = (
            part_ref[i : i + 2].reshape(2 * rows, dim),
            *halves(stat_ref[i : i + 2].reshape(2 * rows, 128)),
        )
        stat = jnp.concatenate([sent_stats(back_ref, i + n, rows) for n in range(2)], axis=0)
        largest2, total2 = halves(stat)
        largest2 = jnp.where(flag_ref[0] > 0, largest2, MASKED_SCORE)
        top = jnp.maximum(largest1, largest2)
        a, b = jnp.exp2((largest1 - top) * scale), jnp.exp2((largest2 - top) * scale)
        inverse = 1.0 / (a * total1 + b * total2)
        out2 = taken(back_ref, i, 2, 0, rows).astype(jnp.float32)
        out = out1 * (a * inverse) + out2 * (b * inverse)
        done_ref[i : i + 2] = out.reshape(2, rows, dim).astype(done_ref.dtype)
    copy = pltpu.make_async_copy(done_ref, out_ref.at[0:blocks], sem)
    copy.start()
    copy.wait()


def estimate(area, arrays):
    return pl.CostEstimate(
        flops=4 * HEAD_DIM * area,
        bytes_accessed=sum(2 * a.size for a in arrays),
        transcendentals=area,
    )


def self_attention(queries, keys, values, chunk, chunk_place, groups):
    rows, width = queries.shape
    heads = width // HEAD_DIM
    scale = HEAD_DIM ** (-0.5) * LOG2E
    x = lax.all_to_all(
        packed(queries, keys, values), "ctx", 0, 0, axis_index_groups=groups, tiled=True
    )
    count, half, left = lax.axis_size("ctx"), rows // 2, heads // 2
    pieces = []
    for n in range(2):
        steps = left * (n + 1)
        pairs = [(i, i + steps) for i in range(count - steps) if i % heads >= left]
        part = slice(n * half, (n + 1) * half)
        pieces.append(
            lax.ppermute(jnp.concatenate([keys[part], values[part]], axis=0), "ctx", pairs)
        )
    raw = jnp.where(chunk_place < left, pieces[0], pieces[1])
    arriving = lax.all_to_all(
        packed(raw), "ctx", 0, 0, axis_index_groups=groups, tiled=True
    )
    asked = shifted(x[:left, :rows], "ctx", -heads)
    area = (heads * rows) ** 2 // 2
    small = (left * rows) ** 2 // 2
    out1, stat = pl.pallas_call(
        functools.partial(own_kernel, scale),
        out_shape=(
            jax.ShapeDtypeStruct((heads, rows, HEAD_DIM), jnp.float32),
            jax.ShapeDtypeStruct((heads, rows, 128), jnp.float32),
        ),
        cost_estimate=estimate(area, (x,)),
        name="own",
    )(x)
    smem = pl.BlockSpec(memory_space=pltpu.SMEM)

    def first_blocks(count, height):
        return pl.BlockSpec((count, height, HEAD_DIM), lambda *_: (0, 0, 0))

    answer = pl.pallas_call(
        functools.partial(later_kernel, scale),
        out_shape=jax.ShapeDtypeStruct((left + 1, rows, HEAD_DIM), jnp.bfloat16),
        grid=(1,),
        in_specs=[first_blocks(left, rows), first_blocks(left, 3 * rows)],
        out_specs=first_blocks(left + 1, rows),
        cost_estimate=estimate(small, (asked,)),
        name="later",
    )(asked, x)
    back = shifted(answer, "ctx", heads)
    flag = chunk.reshape(1)
    all_blocks = first_blocks(heads, rows)
    rest, part, stat = pl.pallas_call(
        functools.partial(previous_kernel, scale),
        out_shape=(
            jax.ShapeDtypeStruct((heads, rows, HEAD_DIM), jnp.bfloat16),
            jax.ShapeDtypeStruct((left, rows, HEAD_DIM), jnp.float32),
            jax.ShapeDtypeStruct((left, rows, 128), jnp.float32),
        ),
        grid=(1,),
        in_specs=[
            smem,
            all_blocks,
            all_blocks,
            all_blocks,
            all_blocks,
        ],
        out_specs=(all_blocks, first_blocks(left, rows), first_blocks(left, rows)),
        cost_estimate=estimate(area - small, (x, out1, stat)),
        name="previous",
    )(flag, x, arriving, out1, stat)
    vmem, anywhere = (pl.BlockSpec(memory_space=m) for m in (pltpu.VMEM, pl.ANY))
    return pl.pallas_call(
        functools.partial(merge_kernel, scale),
        out_shape=jax.ShapeDtypeStruct(rest.shape, rest.dtype),
        in_specs=[smem, vmem, vmem, vmem, anywhere],
        out_specs=anywhere,
        input_output_aliases={4: 0},
        scratch_shapes=[
            pltpu.VMEM((left, rows, HEAD_DIM), rest.dtype),
            pltpu.SemaphoreType.DMA(()),
        ],
        cost_estimate=estimate(0, (part, stat, back)),
        name="merge",
    )(flag, part, stat, back, rest)


def wanted_pieces(table_ref, position, span_count):
    pieces = []
    place, plane = position % PLANE, position // PLANE
    for c in range(span_count):
        for slot in range(2):
            source = table_ref[c, slot] // 4
            for later in range(2):
                block = (source + later) // span_count
                relative = (block % PLANE) ^ place
                away = plane - block // PLANE
                column = relative // 2
                index = jnp.where(
                    column == 0, away, 1 + 2 * column + jnp.where(away == 1, 0, 1)
                )
                pieces.append((relative % 2 == 0, index, (source + later) % span_count))
    return pieces


def fetch(refs, rows, index, half, target, sem):
    size = target.shape[0]
    first = 0
    for ref in refs:
        count = ref.shape[0] // rows

        @pl.when((index >= first) & (index < first + count))
        def _(ref=ref, first=first):
            start = pl.multiple_of((index - first) * rows + half * size, size)
            pltpu.make_async_copy(ref.at[pl.ds(start, size), :], target, sem).start()

        first += count


def gather_kernel(span_count, position_ref, theirs_ref, *refs):
    *in_refs, out_ref, sems = refs
    rows = in_refs[0].shape[0]
    pieces = wanted_pieces(theirs_ref, position_ref[0], span_count)
    size = out_ref.shape[0] // len(pieces)
    targets = [out_ref.at[n * size : (n + 1) * size, :] for n in range(len(pieces))]
    for n, (here, index, half) in enumerate(pieces):
        fetch(in_refs, rows, jnp.where(here, index, -1), half, targets[n], sems.at[n])
    for n, (here, _, _) in enumerate(pieces):

        @pl.when(here)
        def _(n=n):
            pltpu.make_async_copy(in_refs[0].at[0:size, :], targets[n], sems.at[n]).wait()


def absorb_kernel(q_ref, weight_ref, out_ref, weights_ref, sems):
    rows, width = q_ref.shape
    span_count = out_ref.shape[0]
    span = rows // span_count
    steps, _, block = weights_ref.shape
    copies = [
        pltpu.make_async_copy(
            weight_ref.at[:, g * block : (g + 1) * block], weights_ref.at[g], sems.at[g]
        )
        for g in range(steps)
    ]
    for copy in copies:
        copy.start()
    for head in range(width // HEAD_DIM):
        g, first = divmod(head * HEAD_DIM, block)
        if first == 0:
            copies[g].wait()
        lanes = slice(head * HEAD_DIM, (head + 1) * HEAD_DIM)
        product = scores_of(q_ref[:, lanes], weights_ref[g, :, first : first + HEAD_DIM])
        product = product.astype(out_ref.dtype)
        for c in range(span_count):
            out_ref[c, head * span : (head + 1) * span, :] = product[c * span : (c + 1) * span]


def cross_kernel(scale, position_ref, table_ref, *refs):
    *in_refs, theirs_ref, asks_ref, weight_ref, out_ref = refs[:-6]
    rows_ref, all_asks_ref, weights_ref, sems, ask_sems, weight_sems = refs[-6:]
    rows, width = out_ref.shape
    steps, span_count, asked, _ = all_asks_ref.shape
    span = rows // span_count
    block = weights_ref.shape[2]
    pieces = wanted_pieces(table_ref, position_ref[0], span_count)
    targets = [rows_ref.at[n * span : (n + 1) * span, :] for n in range(len(pieces))]
    held = sum(ref.shape[0] for ref in in_refs) // rows
    for n, (here, index, half) in enumerate(pieces):
        fetch(in_refs, rows, jnp.where(here, index, held), half, targets[n], sems.at[n])

        @pl.when(jnp.logical_not(here))
        def _(n=n):
            source = theirs_ref.at[n * span : (n + 1) * span, :]
            pltpu.make_async_copy(source, targets[n], sems.at[n]).start()

    ask_copies = [
        pltpu.make_async_copy(
            asks_ref.at[:, g * asked : (g + 1) * asked, :], all_asks_ref.at[g], ask_sems.at[g]
        )
        for g in range(steps)
    ]
    weight_copies = [
        pltpu.make_async_copy(
            weight_ref.at[:, width + g * block : width + (g + 1) * block],
            weights_ref.at[g],
            weight_sems.at[g],
        )
        for g in range(steps)
    ]
    for g in range(steps):
        ask_copies[g].start()
        weight_copies[g].start()
    for n in range(len(pieces)):
        pltpu.make_async_copy(theirs_ref.at[0:span, :], targets[n], sems.at[n]).wait()

    keys_of_span = rows_ref.shape[0] // span_count
    slot = lax.broadcasted_iota(jnp.int32, (asked, keys_of_span), 1) // (2 * span)
    counts = [table_ref[c, 0] % 4 for c in range(span_count)]
    for g in range(steps):
        ask_copies[g].wait()
        means = []
        for c in range(span_count):
            keys = rows_ref[c * keys_of_span : (c + 1) * keys_of_span, :]
            s = jnp.where(slot < counts[c], scores_of(all_asks_ref[g, c], keys), MASKED_SCORE)
            p = jnp.exp2((s - jnp.max(s, axis=1, keepdims=True)) * scale)
            inverse = jnp.where(counts[c] > 0, 1.0 / jnp.sum(p, axis=1, keepdims=True), 0.0)
            mean = jnp.dot(p.astype(jnp.bfloat16), keys, preferred_element_type=jnp.float32)
            means.append((mean * inverse).astype(jnp.bfloat16))
        weight_copies[g].wait()
        for h in range(block // HEAD_DIM):
            mean = jnp.concatenate([m[h * span : (h + 1) * span] for m in means], axis=0)
            inner = slice(h * HEAD_DIM, (h + 1) * HEAD_DIM)
            lanes = slice(g * block + h * HEAD_DIM, g * block + (h + 1) * HEAD_DIM)
            out_ref[:, lanes] = jnp.dot(
                mean, weights_ref[g, :, inner], preferred_element_type=jnp.float32
            )


def cross_attention(cross_queries, encoded, weight, counts, sources, position):
    rows, width = cross_queries.shape
    span_count = counts.shape[0]
    depth = encoded.shape[1]
    place = position % PLANE
    one_back = shifted(encoded, "ctx", PLANE)
    table = sources * 4 + counts[:, None]
    before = shifted(table, "ctx", 1)
    table = jnp.concatenate([before[-1:], table[:-1]], axis=0)
    their_table = swapped(table, "ctx", 1)
    two_back = shifted(one_back, "ctx", PLANE)

    near = []
    for bit in (2, 4, 6):
        other = jnp.where(place < (place ^ bit), encoded, two_back)
        near.append(swapped(jnp.concatenate([one_back, other], axis=0), "ctx", bit))

    held = [encoded, one_back, two_back, *near]
    where = position.reshape(1)
    picked = span_count * 4 * SPAN
    pieces = picked // SPAN
    smem, anywhere = (pl.BlockSpec(memory_space=m) for m in (pltpu.SMEM, pl.ANY))
    vmem = pl.BlockSpec(memory_space=pltpu.VMEM)
    theirs = pl.pallas_call(
        functools.partial(gather_kernel, span_count),
        out_shape=jax.ShapeDtypeStruct((picked, depth), encoded.dtype),
        in_specs=[smem] * 2 + [anywhere] * len(held),
        out_specs=vmem,
        scratch_shapes=[pltpu.SemaphoreType.DMA((pieces,))],
        cost_estimate=pl.CostEstimate(
            flops=0, bytes_accessed=8 * picked * depth, transcendentals=0
        ),
        name="gather",
    )(where, their_table, *held)
    theirs = swapped(theirs, "ctx", 1)

    heads = width // HEAD_DIM
    block = 4 * HEAD_DIM
    steps = width // block
    asks = pl.pallas_call(
        absorb_kernel,
        out_shape=jax.ShapeDtypeStruct((span_count, heads * SPAN, depth), jnp.bfloat16),
        in_specs=[vmem, anywhere],
        out_specs=vmem,
        scratch_shapes=[
            pltpu.VMEM((steps, depth, block), weight.dtype),
            pltpu.SemaphoreType.DMA((steps,)),
        ],
        cost_estimate=pl.CostEstimate(
            flops=2 * rows * depth * width, bytes_accessed=2 * weight.size, transcendentals=0
        ),
        name="absorb",
    )(cross_queries, weight)
    block = 8 * HEAD_DIM
    steps = width // block
    cost = pl.CostEstimate(
        flops=4 * picked * depth * heads * SPAN + 2 * rows * depth * width,
        bytes_accessed=weight.size + asks.size * 2 + picked * depth * 4,
        transcendentals=picked * SPAN * heads,
    )
    return pl.pallas_call(
        functools.partial(cross_kernel, HEAD_DIM ** (-0.5) * LOG2E),
        out_shape=jax.ShapeDtypeStruct((rows, width), jnp.float32),
        in_specs=[smem] * 2 + [anywhere] * (len(held) + 3),
        out_specs=vmem,
        scratch_shapes=[
            pltpu.VMEM((picked, depth), encoded.dtype),
            pltpu.VMEM((steps, span_count, heads * SPAN // steps, depth), asks.dtype),
            pltpu.VMEM((steps, depth, block), weight.dtype),
            pltpu.SemaphoreType.DMA((pieces,)),
            pltpu.SemaphoreType.DMA((steps,)),
            pltpu.SemaphoreType.DMA((steps,)),
        ],
        cost_estimate=cost,
        name="cross",
    )(where, table, *held, theirs, asks, weight)


def sum_kernel(self_ref, cross_ref, out_ref):
    for head in range(self_ref.shape[0]):
        lanes = slice(head * HEAD_DIM, (head + 1) * HEAD_DIM)
        out_ref[:, lanes] = (self_ref[head].astype(jnp.float32) + cross_ref[:, lanes]).astype(
            out_ref.dtype
        )


def per_device(
    queries, self_keys, self_values, cross_queries, encoded, neighbour_weight, counts, sources
):
    position = lax.axis_index("ctx")
    count = lax.axis_size("ctx")
    groups = [list(range(first, first + HEADS)) for first in range(0, count, HEADS)]
    cross_part = cross_attention(
        cross_queries, encoded, neighbour_weight, counts, sources, position
    )
    by_head = self_attention(
        queries, self_keys, self_values, position // HEADS, position % HEADS, groups
    )
    self_part = lax.all_to_all(by_head, "ctx", 0, 0, axis_index_groups=groups, tiled=True)
    return pl.pallas_call(
        sum_kernel,
        out_shape=jax.ShapeDtypeStruct(queries.shape, jnp.bfloat16),
        name="total",
    )(self_part, cross_part)


def solution(mesh):
    return jax.shard_map(
        per_device,
        mesh=mesh,
        in_specs=(
            P(("groups", "ctx"), None),
            P(("groups", "ctx"), None),
            P(("groups", "ctx"), None),
            P(("groups", "ctx"), None),
            P(("groups", "ctx"), None),
            P(),
            P(("groups", "ctx")),
            P(("groups", "ctx"), None),
        ),
        out_specs=P(("groups", "ctx"), None),
        check_vma=False,
    )
```

```python
import functools

import jax
import jax.numpy as jnp
from jax import lax
from jax.experimental import pallas as pl
from jax.experimental.pallas import tpu as pltpu
from jax.sharding import PartitionSpec as P


HEADS = 16
HEAD_DIM = 128
SPAN = 64
PLANE = 8
LEFT = 8

MASKED_SCORE = -1e30
LOG2E = 1.4426950408889634


def shifted(value, axis, steps):
    count = lax.axis_size(axis)
    first, last = (max(0, -steps), min(count, count - steps))
    return lax.ppermute(value, axis, [(source, source + steps) for source in range(first, last)])


def swapped(value, axis, bit):
    count = lax.axis_size(axis)
    return lax.ppermute(value, axis, [(source, source ^ bit) for source in range(count)])


def pack_kernel(*refs):
    *in_refs, out_ref = refs
    rows = in_refs[0].shape[0]
    for head in range(out_ref.shape[0]):
        columns = slice(head * HEAD_DIM, (head + 1) * HEAD_DIM)
        for n, ref in enumerate(in_refs):
            out_ref[head, n * rows : (n + 1) * rows, :] = ref[:, columns]


def packed(*arrays):
    rows, width = arrays[0].shape
    return pl.pallas_call(
        pack_kernel,
        out_shape=jax.ShapeDtypeStruct(
            (width // HEAD_DIM, len(arrays) * rows, HEAD_DIM), arrays[0].dtype
        ),
        cost_estimate=pl.CostEstimate(
            flops=0, bytes_accessed=4 * len(arrays) * rows * width, transcendentals=0
        ),
        name="pack",
    )(*arrays)


def scores_of(q, k):
    return lax.dot_general(q, k, (((1,), (1,)), ((), ())), preferred_element_type=jnp.float32)


def softmax_parts(q, pieces, scale, start=None):
    scores = []
    for k, _, mask in pieces:
        s = scores_of(q, k)
        scores.append(s if mask is None else jnp.where(mask, s, MASKED_SCORE))
    largest = functools.reduce(jnp.maximum, [jnp.max(s, axis=1, keepdims=True) for s in scores])
    total, out = None, None
    if start is not None:
        out, before, total = start
        largest = jnp.maximum(largest, before)
        weight = jnp.exp2((before - largest) * scale)
        out, total = out * weight, total * weight
    for s, (_, v, _) in zip(scores, pieces):
        p = jnp.exp2((s - largest) * scale)
        t = jnp.sum(p, axis=1, keepdims=True)
        o = jnp.dot(p.astype(jnp.bfloat16), v, preferred_element_type=jnp.float32)
        total = t if total is None else total + t
        out = o if out is None else out + o
    return out, largest, total


def with_stats(largest, total):
    lane = lax.broadcasted_iota(jnp.int32, (largest.shape[0], 128), 1)
    return jnp.where(lane < 64, largest, total)


def halves(stat):
    return stat[:, 0:1], stat[:, 64:65]


def thirds(x):
    high = x.astype(jnp.bfloat16)
    rest = x - high.astype(jnp.float32)
    middle = rest.astype(jnp.bfloat16)
    low = (rest - middle.astype(jnp.float32)).astype(jnp.bfloat16)
    return high, middle, low


def taken(ref, first, count, start, rows):
    return ref[first : first + count, start : start + rows, :].reshape(count * rows, ref.shape[2])


def triangle(size, keep):
    row = lax.broadcasted_iota(jnp.int32, (size, size), 0)
    column = lax.broadcasted_iota(jnp.int32, (size, size), 1)
    return keep(column, row)


def own_kernel(scale, q_ref, kv_ref, out_ref, stat_ref):
    blocks, rows, dim = q_ref.shape
    causal = triangle(2 * rows, lambda column, row: column <= row)
    for i in range(0, blocks, 2):
        spans = [(i, 2, causal)] + ([(0, i, None)] if i else [])
        pieces = [
            (taken(kv_ref, f, n, 0, rows), taken(kv_ref, f, n, rows, rows), mask)
            for f, n, mask in spans
        ]
        out, largest, total = softmax_parts(taken(q_ref, i, 2, 0, rows), pieces, scale)
        out_ref[i : i + 2] = out.reshape(2, rows, dim)
        stat_ref[i : i + 2] = with_stats(largest, total).reshape(2, rows, 128)


def later_kernel(scale, q_ref, kv_ref, out_ref):
    blocks, rows, dim = q_ref.shape
    later = triangle(2 * rows, lambda column, row: column > row)
    out_ref[blocks] = jnp.zeros((rows, dim), out_ref.dtype)
    for i in range(0, blocks, 2):
        spans = [(i, 2, later)] + ([(i + 2, blocks - i - 2, None)] if i + 2 < blocks else [])
        pieces = [
            (taken(kv_ref, f, n, 0, rows), taken(kv_ref, f, n, rows, rows), mask)
            for f, n, mask in spans
        ]
        out, largest, total = softmax_parts(taken(q_ref, i, 2, 0, rows), pieces, scale)
        out_ref[i : i + 2] = out.reshape(2, rows, dim).astype(out_ref.dtype)
        stat = with_stats(largest, total)
        for n in range(2):
            turned = stat[n * rows : (n + 1) * rows].T
            for m, row in enumerate((turned[0:1], turned[64:65])):
                for k, part in enumerate(thirds(row)):
                    place = ((i + n) * 2 + m) * 3 + k
                    out_ref[blocks, place : place + 1, :] = part


def sent_stats(ref, block, rows):
    values = []
    for m in range(2):
        place = (block * 2 + m) * 3
        three = ref[ref.shape[0] - 1, place : place + 3, :].astype(jnp.float32)
        values.append(three[0:1] + three[1:2] + three[2:3])
    sublane = lax.broadcasted_iota(jnp.int32, (rows, 128), 0)
    return jnp.where(sublane < 64, values[0], values[1]).T


def previous_kernel(scale, flag_ref, q_ref, kv_ref, out1_ref, stat1_ref, out_ref, part_ref, stat_ref):
    blocks, rows, dim = q_ref.shape
    waiting = part_ref.shape[0]
    later = triangle(2 * rows, lambda column, row: column > row)

    def own_part(i):
        stat = stat1_ref[i : i + 2].reshape(2 * rows, 128)
        return (out1_ref[i : i + 2].reshape(2 * rows, dim), *halves(stat))

    def store(i, part):
        out, largest, total = part
        if i < waiting:
            part_ref[i : i + 2] = out.reshape(2, rows, dim)
            stat_ref[i : i + 2] = with_stats(largest, total).reshape(2, rows, 128)
        else:
            out = out * (1.0 / total)
            out_ref[i : i + 2] = out.reshape(2, rows, dim).astype(out_ref.dtype)

    @pl.when(flag_ref[0] > 0)
    def _():
        for i in range(0, blocks, 2):
            first = max(i - waiting, 0)
            spans = [(first, 2, later)] if i >= waiting else []
            first += 2 * len(spans)
            if first < kv_ref.shape[0]:
                spans.append((first, kv_ref.shape[0] - first, None))
            pieces = [
                (taken(kv_ref, f, n, 0, rows), taken(kv_ref, f, n, rows, rows), mask)
                for f, n, mask in spans
            ]
            store(i, softmax_parts(taken(q_ref, i, 2, 0, rows), pieces, scale, own_part(i)))

    @pl.when(flag_ref[0] == 0)
    def _():
        part_ref[...] = out1_ref[0:waiting]
        stat_ref[...] = stat1_ref[0:waiting]
        for i in range(waiting, blocks, 2):
            store(i, own_part(i))


def merge_kernel(scale, flag_ref, part_ref, stat_ref, back_ref, rest_ref, out_ref, done_ref, sem):
    del rest_ref
    blocks, rows, dim = part_ref.shape
    for i in range(0, blocks, 2):
        out1, largest1, total1 = (
            part_ref[i : i + 2].reshape(2 * rows, dim),
            *halves(stat_ref[i : i + 2].reshape(2 * rows, 128)),
        )
        stat = jnp.concatenate([sent_stats(back_ref, i + n, rows) for n in range(2)], axis=0)
        largest2, total2 = halves(stat)
        largest2 = jnp.where(flag_ref[0] > 0, largest2, MASKED_SCORE)
        top = jnp.maximum(largest1, largest2)
        a, b = jnp.exp2((largest1 - top) * scale), jnp.exp2((largest2 - top) * scale)
        inverse = 1.0 / (a * total1 + b * total2)
        out2 = taken(back_ref, i, 2, 0, rows).astype(jnp.float32)
        out = out1 * (a * inverse) + out2 * (b * inverse)
        done_ref[i : i + 2] = out.reshape(2, rows, dim).astype(done_ref.dtype)
    copy = pltpu.make_async_copy(done_ref, out_ref.at[0:blocks], sem)
    copy.start()
    copy.wait()


def estimate(area, arrays):
    return pl.CostEstimate(
        flops=4 * HEAD_DIM * area,
        bytes_accessed=sum(2 * a.size for a in arrays),
        transcendentals=area,
    )


def self_attention(queries, keys, values, chunk, groups):
    rows, width = queries.shape
    heads = width // HEAD_DIM
    scale = HEAD_DIM ** (-0.5) * LOG2E
    kv = lax.all_to_all(
        packed(keys, values), "ctx", 0, 0, axis_index_groups=groups, tiled=True
    )
    arriving = shifted(kv[LEFT:], "ctx", heads)
    q = lax.all_to_all(packed(queries), "ctx", 0, 0, axis_index_groups=groups, tiled=True)
    asked = shifted(q[:LEFT], "ctx", -heads)
    area = (heads * rows) ** 2 // 2
    small = (LEFT * rows) ** 2 // 2
    out1, stat = pl.pallas_call(
        functools.partial(own_kernel, scale),
        out_shape=(
            jax.ShapeDtypeStruct((heads, rows, HEAD_DIM), jnp.float32),
            jax.ShapeDtypeStruct((heads, rows, 128), jnp.float32),
        ),
        cost_estimate=estimate(area, (q, kv)),
        name="own",
    )(q, kv)
    smem = pl.BlockSpec(memory_space=pltpu.SMEM)

    def first_blocks(count, height):
        return pl.BlockSpec((count, height, HEAD_DIM), lambda *_: (0, 0, 0))

    answer = pl.pallas_call(
        functools.partial(later_kernel, scale),
        out_shape=jax.ShapeDtypeStruct((LEFT + 1, rows, HEAD_DIM), jnp.bfloat16),
        grid=(1,),
        in_specs=[first_blocks(LEFT, rows), first_blocks(LEFT, 2 * rows)],
        out_specs=first_blocks(LEFT + 1, rows),
        cost_estimate=estimate(small, (asked,)),
        name="later",
    )(asked, kv)
    back = shifted(answer, "ctx", heads)
    flag = chunk.reshape(1)
    all_blocks = first_blocks(heads, rows)
    rest, part, stat = pl.pallas_call(
        functools.partial(previous_kernel, scale),
        out_shape=(
            jax.ShapeDtypeStruct((heads, rows, HEAD_DIM), jnp.bfloat16),
            jax.ShapeDtypeStruct((LEFT, rows, HEAD_DIM), jnp.float32),
            jax.ShapeDtypeStruct((LEFT, rows, 128), jnp.float32),
        ),
        grid=(1,),
        in_specs=[smem, all_blocks, first_blocks(heads - LEFT, 2 * rows), all_blocks, all_blocks],
        out_specs=(all_blocks, first_blocks(LEFT, rows), first_blocks(LEFT, rows)),
        cost_estimate=estimate(area - small, (q, kv, out1, stat)),
        name="previous",
    )(flag, q, arriving, out1, stat)
    vmem, anywhere = (pl.BlockSpec(memory_space=m) for m in (pltpu.VMEM, pl.ANY))
    return pl.pallas_call(
        functools.partial(merge_kernel, scale),
        out_shape=jax.ShapeDtypeStruct(rest.shape, rest.dtype),
        in_specs=[smem, vmem, vmem, vmem, anywhere],
        out_specs=anywhere,
        input_output_aliases={4: 0},
        scratch_shapes=[
            pltpu.VMEM((LEFT, rows, HEAD_DIM), rest.dtype),
            pltpu.SemaphoreType.DMA(()),
        ],
        cost_estimate=estimate(0, (part, stat, back)),
        name="merge",
    )(flag, part, stat, back, rest)


def wanted_pieces(table_ref, position, span_count):
    pieces = []
    place, plane = position % PLANE, position // PLANE
    for c in range(span_count):
        for slot in range(2):
            source = table_ref[c, slot] // 4
            for later in range(2):
                block = (source + later) // span_count
                relative = (block % PLANE) ^ place
                away = plane - block // PLANE
                column = relative // 2
                index = jnp.where(
                    column == 0, away, 1 + 2 * column + jnp.where(away == 1, 0, 1)
                )
                pieces.append((relative % 2 == 0, index, (source + later) % span_count))
    return pieces


def fetch(refs, rows, index, half, target, sem):
    size = target.shape[0]
    first = 0
    for ref in refs:
        count = ref.shape[0] // rows

        @pl.when((index >= first) & (index < first + count))
        def _(ref=ref, first=first):
            start = pl.multiple_of((index - first) * rows + half * size, size)
            pltpu.make_async_copy(ref.at[pl.ds(start, size), :], target, sem).start()

        first += count


def gather_kernel(span_count, position_ref, theirs_ref, *refs):
    *in_refs, out_ref, sems = refs
    rows = in_refs[0].shape[0]
    pieces = wanted_pieces(theirs_ref, position_ref[0], span_count)
    size = out_ref.shape[0] // len(pieces)
    targets = [out_ref.at[n * size : (n + 1) * size, :] for n in range(len(pieces))]
    for n, (here, index, half) in enumerate(pieces):
        fetch(in_refs, rows, jnp.where(here, index, -1), half, targets[n], sems.at[n])
    for n, (here, _, _) in enumerate(pieces):

        @pl.when(here)
        def _(n=n):
            pltpu.make_async_copy(in_refs[0].at[0:size, :], targets[n], sems.at[n]).wait()


def absorb_kernel(q_ref, weight_ref, out_ref, weights_ref, sems):
    rows, width = q_ref.shape
    span_count = out_ref.shape[0]
    span = rows // span_count
    steps, _, block = weights_ref.shape
    copies = [
        pltpu.make_async_copy(
            weight_ref.at[:, g * block : (g + 1) * block], weights_ref.at[g], sems.at[g]
        )
        for g in range(steps)
    ]
    for copy in copies:
        copy.start()
    for head in range(width // HEAD_DIM):
        g, first = divmod(head * HEAD_DIM, block)
        if first == 0:
            copies[g].wait()
        lanes = slice(head * HEAD_DIM, (head + 1) * HEAD_DIM)
        product = scores_of(q_ref[:, lanes], weights_ref[g, :, first : first + HEAD_DIM])
        product = product.astype(out_ref.dtype)
        for c in range(span_count):
            out_ref[c, head * span : (head + 1) * span, :] = product[c * span : (c + 1) * span]


def cross_kernel(scale, position_ref, table_ref, *refs):
    *in_refs, theirs_ref, asks_ref, weight_ref, out_ref = refs[:-6]
    rows_ref, all_asks_ref, weights_ref, sems, ask_sems, weight_sems = refs[-6:]
    rows, width = out_ref.shape
    steps, span_count, asked, _ = all_asks_ref.shape
    span = rows // span_count
    block = weights_ref.shape[2]
    pieces = wanted_pieces(table_ref, position_ref[0], span_count)
    targets = [rows_ref.at[n * span : (n + 1) * span, :] for n in range(len(pieces))]
    held = sum(ref.shape[0] for ref in in_refs) // rows
    for n, (here, index, half) in enumerate(pieces):
        fetch(in_refs, rows, jnp.where(here, index, held), half, targets[n], sems.at[n])

        @pl.when(jnp.logical_not(here))
        def _(n=n):
            source = theirs_ref.at[n * span : (n + 1) * span, :]
            pltpu.make_async_copy(source, targets[n], sems.at[n]).start()

    ask_copies = [
        pltpu.make_async_copy(
            asks_ref.at[:, g * asked : (g + 1) * asked, :], all_asks_ref.at[g], ask_sems.at[g]
        )
        for g in range(steps)
    ]
    weight_copies = [
        pltpu.make_async_copy(
            weight_ref.at[:, width + g * block : width + (g + 1) * block],
            weights_ref.at[g],
            weight_sems.at[g],
        )
        for g in range(steps)
    ]
    for g in range(steps):
        ask_copies[g].start()
        weight_copies[g].start()
    for n in range(len(pieces)):
        pltpu.make_async_copy(theirs_ref.at[0:span, :], targets[n], sems.at[n]).wait()

    keys_of_span = rows_ref.shape[0] // span_count
    slot = lax.broadcasted_iota(jnp.int32, (asked, keys_of_span), 1) // (2 * span)
    counts = [table_ref[c, 0] % 4 for c in range(span_count)]
    for g in range(steps):
        ask_copies[g].wait()
        means = []
        for c in range(span_count):
            keys = rows_ref[c * keys_of_span : (c + 1) * keys_of_span, :]
            s = jnp.where(slot < counts[c], scores_of(all_asks_ref[g, c], keys), MASKED_SCORE)
            p = jnp.exp2((s - jnp.max(s, axis=1, keepdims=True)) * scale)
            inverse = jnp.where(counts[c] > 0, 1.0 / jnp.sum(p, axis=1, keepdims=True), 0.0)
            mean = jnp.dot(p.astype(jnp.bfloat16), keys, preferred_element_type=jnp.float32)
            means.append((mean * inverse).astype(jnp.bfloat16))
        weight_copies[g].wait()
        for h in range(block // HEAD_DIM):
            mean = jnp.concatenate([m[h * span : (h + 1) * span] for m in means], axis=0)
            inner = slice(h * HEAD_DIM, (h + 1) * HEAD_DIM)
            lanes = slice(g * block + h * HEAD_DIM, g * block + (h + 1) * HEAD_DIM)
            out_ref[:, lanes] = jnp.dot(
                mean, weights_ref[g, :, inner], preferred_element_type=jnp.float32
            )


def cross_attention(cross_queries, encoded, weight, counts, sources, position):
    rows, width = cross_queries.shape
    span_count = counts.shape[0]
    depth = encoded.shape[1]
    place = position % PLANE
    one_back = shifted(encoded, "ctx", PLANE)
    table = sources * 4 + counts[:, None]
    before = shifted(table, "ctx", 1)
    table = jnp.concatenate([before[-1:], table[:-1]], axis=0)
    their_table = swapped(table, "ctx", 1)
    two_back = shifted(one_back, "ctx", PLANE)

    near = []
    for bit in (2, 4, 6):
        other = jnp.where(place < (place ^ bit), encoded, two_back)
        near.append(swapped(jnp.concatenate([one_back, other], axis=0), "ctx", bit))

    held = [encoded, one_back, two_back, *near]
    where = position.reshape(1)
    picked = span_count * 4 * SPAN
    pieces = picked // SPAN
    smem, anywhere = (pl.BlockSpec(memory_space=m) for m in (pltpu.SMEM, pl.ANY))
    vmem = pl.BlockSpec(memory_space=pltpu.VMEM)
    theirs = pl.pallas_call(
        functools.partial(gather_kernel, span_count),
        out_shape=jax.ShapeDtypeStruct((picked, depth), encoded.dtype),
        in_specs=[smem] * 2 + [anywhere] * len(held),
        out_specs=vmem,
        scratch_shapes=[pltpu.SemaphoreType.DMA((pieces,))],
        cost_estimate=pl.CostEstimate(
            flops=0, bytes_accessed=8 * picked * depth, transcendentals=0
        ),
        name="gather",
    )(where, their_table, *held)
    theirs = swapped(theirs, "ctx", 1)

    heads = width // HEAD_DIM
    block = 4 * HEAD_DIM
    steps = width // block
    asks = pl.pallas_call(
        absorb_kernel,
        out_shape=jax.ShapeDtypeStruct((span_count, heads * SPAN, depth), jnp.bfloat16),
        in_specs=[vmem, anywhere],
        out_specs=vmem,
        scratch_shapes=[
            pltpu.VMEM((steps, depth, block), weight.dtype),
            pltpu.SemaphoreType.DMA((steps,)),
        ],
        cost_estimate=pl.CostEstimate(
            flops=2 * rows * depth * width, bytes_accessed=2 * weight.size, transcendentals=0
        ),
        name="absorb",
    )(cross_queries, weight)
    block = 8 * HEAD_DIM
    steps = width // block
    cost = pl.CostEstimate(
        flops=4 * picked * depth * heads * SPAN + 2 * rows * depth * width,
        bytes_accessed=weight.size + asks.size * 2 + picked * depth * 4,
        transcendentals=picked * SPAN * heads,
    )
    return pl.pallas_call(
        functools.partial(cross_kernel, HEAD_DIM ** (-0.5) * LOG2E),
        out_shape=jax.ShapeDtypeStruct((rows, width), jnp.float32),
        in_specs=[smem] * 2 + [anywhere] * (len(held) + 3),
        out_specs=vmem,
        scratch_shapes=[
            pltpu.VMEM((picked, depth), encoded.dtype),
            pltpu.VMEM((steps, span_count, heads * SPAN // steps, depth), asks.dtype),
            pltpu.VMEM((steps, depth, block), weight.dtype),
            pltpu.SemaphoreType.DMA((pieces,)),
            pltpu.SemaphoreType.DMA((steps,)),
            pltpu.SemaphoreType.DMA((steps,)),
        ],
        cost_estimate=cost,
        name="cross",
    )(where, table, *held, theirs, asks, weight)


def sum_kernel(self_ref, cross_ref, out_ref):
    for head in range(self_ref.shape[0]):
        lanes = slice(head * HEAD_DIM, (head + 1) * HEAD_DIM)
        out_ref[:, lanes] = (self_ref[head].astype(jnp.float32) + cross_ref[:, lanes]).astype(
            out_ref.dtype
        )


def per_device(
    queries, self_keys, self_values, cross_queries, encoded, neighbour_weight, counts, sources
):
    position = lax.axis_index("ctx")
    count = lax.axis_size("ctx")
    groups = [list(range(first, first + HEADS)) for first in range(0, count, HEADS)]
    cross_part = cross_attention(
        cross_queries, encoded, neighbour_weight, counts, sources, position
    )
    by_head = self_attention(queries, self_keys, self_values, position // HEADS, groups)
    self_part = lax.all_to_all(by_head, "ctx", 0, 0, axis_index_groups=groups, tiled=True)
    return pl.pallas_call(
        sum_kernel,
        out_shape=jax.ShapeDtypeStruct(queries.shape, jnp.bfloat16),
        name="total",
    )(self_part, cross_part)


def solution(mesh):
    return jax.shard_map(
        per_device,
        mesh=mesh,
        in_specs=(
            P(("groups", "ctx"), None),
            P(("groups", "ctx"), None),
            P(("groups", "ctx"), None),
            P(("groups", "ctx"), None),
            P(("groups", "ctx"), None),
            P(),
            P(("groups", "ctx")),
            P(("groups", "ctx"), None),
        ),
        out_specs=P(("groups", "ctx"), None),
        check_vma=False,
    )
```

```python
import functools

import jax
import jax.numpy as jnp
from jax import lax
from jax.experimental import pallas as pl
from jax.experimental.pallas import tpu as pltpu
from jax.sharding import PartitionSpec as P


HEADS = 16
HEAD_DIM = 128
SPAN = 64
PLANE = 8
LEFT = 12

MASKED_SCORE = -1e30
LOG2E = 1.4426950408889634


def shifted(value, axis, steps):
    count = lax.axis_size(axis)
    first, last = (max(0, -steps), min(count, count - steps))
    return lax.ppermute(value, axis, [(source, source + steps) for source in range(first, last)])


def swapped(value, axis, bit):
    count = lax.axis_size(axis)
    return lax.ppermute(value, axis, [(source, source ^ bit) for source in range(count)])


def pack_kernel(*refs):
    *in_refs, out_ref = refs
    rows = in_refs[0].shape[0]
    for head in range(out_ref.shape[0]):
        columns = slice(head * HEAD_DIM, (head + 1) * HEAD_DIM)
        for n, ref in enumerate(in_refs):
            out_ref[head, n * rows : (n + 1) * rows, :] = ref[:, columns]


def packed(*arrays):
    rows, width = arrays[0].shape
    return pl.pallas_call(
        pack_kernel,
        out_shape=jax.ShapeDtypeStruct(
            (width // HEAD_DIM, len(arrays) * rows, HEAD_DIM), arrays[0].dtype
        ),
        cost_estimate=pl.CostEstimate(
            flops=0, bytes_accessed=4 * len(arrays) * rows * width, transcendentals=0
        ),
        name="pack",
    )(*arrays)


def scores_of(q, k):
    return lax.dot_general(q, k, (((1,), (1,)), ((), ())), preferred_element_type=jnp.float32)


def softmax_parts(q, pieces, scale, start=None):
    scores = []
    for k, _, mask in pieces:
        s = scores_of(q, k)
        scores.append(s if mask is None else jnp.where(mask, s, MASKED_SCORE))
    largest = functools.reduce(jnp.maximum, [jnp.max(s, axis=1, keepdims=True) for s in scores])
    total, out = None, None
    if start is not None:
        out, before, total = start
        largest = jnp.maximum(largest, before)
        weight = jnp.exp2((before - largest) * scale)
        out, total = out * weight, total * weight
    for s, (_, v, _) in zip(scores, pieces):
        p = jnp.exp2((s - largest) * scale)
        t = jnp.sum(p, axis=1, keepdims=True)
        o = jnp.dot(p.astype(jnp.bfloat16), v, preferred_element_type=jnp.float32)
        total = t if total is None else total + t
        out = o if out is None else out + o
    return out, largest, total


def with_stats(largest, total):
    lane = lax.broadcasted_iota(jnp.int32, (largest.shape[0], 128), 1)
    return jnp.where(lane < 64, largest, total)


def halves(stat):
    return stat[:, 0:1], stat[:, 64:65]


def thirds(x):
    high = x.astype(jnp.bfloat16)
    rest = x - high.astype(jnp.float32)
    middle = rest.astype(jnp.bfloat16)
    low = (rest - middle.astype(jnp.float32)).astype(jnp.bfloat16)
    return high, middle, low


def taken(ref, first, count, start, rows):
    return ref[first : first + count, start : start + rows, :].reshape(count * rows, ref.shape[2])


def triangle(size, keep):
    row = lax.broadcasted_iota(jnp.int32, (size, size), 0)
    column = lax.broadcasted_iota(jnp.int32, (size, size), 1)
    return keep(column, row)


def own_kernel(scale, q_ref, kv_ref, out_ref, stat_ref):
    blocks, rows, dim = q_ref.shape
    causal = triangle(2 * rows, lambda column, row: column <= row)
    for i in range(0, blocks, 2):
        spans = [(i, 2, causal)] + ([(0, i, None)] if i else [])
        pieces = [
            (taken(kv_ref, f, n, 0, rows), taken(kv_ref, f, n, rows, rows), mask)
            for f, n, mask in spans
        ]
        out, largest, total = softmax_parts(taken(q_ref, i, 2, 0, rows), pieces, scale)
        out_ref[i : i + 2] = out.reshape(2, rows, dim)
        stat_ref[i : i + 2] = with_stats(largest, total).reshape(2, rows, 128)


def later_kernel(scale, q_ref, kv_ref, out_ref):
    blocks, rows, dim = q_ref.shape
    later = triangle(2 * rows, lambda column, row: column > row)
    out_ref[blocks] = jnp.zeros((rows, dim), out_ref.dtype)
    for i in range(0, blocks, 2):
        spans = [(i, 2, later)] + ([(i + 2, blocks - i - 2, None)] if i + 2 < blocks else [])
        pieces = [
            (taken(kv_ref, f, n, 0, rows), taken(kv_ref, f, n, rows, rows), mask)
            for f, n, mask in spans
        ]
        out, largest, total = softmax_parts(taken(q_ref, i, 2, 0, rows), pieces, scale)
        out_ref[i : i + 2] = out.reshape(2, rows, dim).astype(out_ref.dtype)
        stat = with_stats(largest, total)
        for n in range(2):
            turned = stat[n * rows : (n + 1) * rows].T
            for m, row in enumerate((turned[0:1], turned[64:65])):
                for k, part in enumerate(thirds(row)):
                    place = ((i + n) * 2 + m) * 3 + k
                    out_ref[blocks, place : place + 1, :] = part


def sent_stats(ref, block, rows):
    values = []
    for m in range(2):
        place = (block * 2 + m) * 3
        three = ref[ref.shape[0] - 1, place : place + 3, :].astype(jnp.float32)
        values.append(three[0:1] + three[1:2] + three[2:3])
    sublane = lax.broadcasted_iota(jnp.int32, (rows, 128), 0)
    return jnp.where(sublane < 64, values[0], values[1]).T


def previous_kernel(scale, flag_ref, q_ref, kv_ref, out1_ref, stat1_ref, out_ref, part_ref, stat_ref):
    blocks, rows, dim = q_ref.shape
    waiting = part_ref.shape[0]
    later = triangle(2 * rows, lambda column, row: column > row)

    def own_part(i):
        stat = stat1_ref[i : i + 2].reshape(2 * rows, 128)
        return (out1_ref[i : i + 2].reshape(2 * rows, dim), *halves(stat))

    def store(i, part):
        out, largest, total = part
        if i < waiting:
            part_ref[i : i + 2] = out.reshape(2, rows, dim)
            stat_ref[i : i + 2] = with_stats(largest, total).reshape(2, rows, 128)
        else:
            out = out * (1.0 / total)
            out_ref[i : i + 2] = out.reshape(2, rows, dim).astype(out_ref.dtype)

    @pl.when(flag_ref[0] > 0)
    def _():
        for i in range(0, blocks, 2):
            first = max(i - waiting, 0)
            spans = [(first, 2, later)] if i >= waiting else []
            first += 2 * len(spans)
            if first < kv_ref.shape[0]:
                spans.append((first, kv_ref.shape[0] - first, None))
            pieces = [
                (taken(kv_ref, f, n, 0, rows), taken(kv_ref, f, n, rows, rows), mask)
                for f, n, mask in spans
            ]
            store(i, softmax_parts(taken(q_ref, i, 2, 0, rows), pieces, scale, own_part(i)))

    @pl.when(flag_ref[0] == 0)
    def _():
        part_ref[...] = out1_ref[0:waiting]
        stat_ref[...] = stat1_ref[0:waiting]
        for i in range(waiting, blocks, 2):
            store(i, own_part(i))


def merge_kernel(scale, flag_ref, part_ref, stat_ref, back_ref, rest_ref, out_ref, done_ref, sem):
    del rest_ref
    blocks, rows, dim = part_ref.shape
    for i in range(0, blocks, 2):
        out1, largest1, total1 = (
            part_ref[i : i + 2].reshape(2 * rows, dim),
            *halves(stat_ref[i : i + 2].reshape(2 * rows, 128)),
        )
        stat = jnp.concatenate([sent_stats(back_ref, i + n, rows) for n in range(2)], axis=0)
        largest2, total2 = halves(stat)
        largest2 = jnp.where(flag_ref[0] > 0, largest2, MASKED_SCORE)
        top = jnp.maximum(largest1, largest2)
        a, b = jnp.exp2((largest1 - top) * scale), jnp.exp2((largest2 - top) * scale)
        inverse = 1.0 / (a * total1 + b * total2)
        out2 = taken(back_ref, i, 2, 0, rows).astype(jnp.float32)
        out = out1 * (a * inverse) + out2 * (b * inverse)
        done_ref[i : i + 2] = out.reshape(2, rows, dim).astype(done_ref.dtype)
    copy = pltpu.make_async_copy(done_ref, out_ref.at[0:blocks], sem)
    copy.start()
    copy.wait()


def estimate(area, arrays):
    return pl.CostEstimate(
        flops=4 * HEAD_DIM * area,
        bytes_accessed=sum(2 * a.size for a in arrays),
        transcendentals=area,
    )


def self_attention(queries, keys, values, chunk, groups):
    rows, width = queries.shape
    heads = width // HEAD_DIM
    scale = HEAD_DIM ** (-0.5) * LOG2E
    kv = lax.all_to_all(
        packed(keys, values), "ctx", 0, 0, axis_index_groups=groups, tiled=True
    )
    arriving = shifted(kv[LEFT:], "ctx", heads)
    q = lax.all_to_all(packed(queries), "ctx", 0, 0, axis_index_groups=groups, tiled=True)
    asked = shifted(q[:LEFT], "ctx", -heads)
    area = (heads * rows) ** 2 // 2
    small = (LEFT * rows) ** 2 // 2
    out1, stat = pl.pallas_call(
        functools.partial(own_kernel, scale),
        out_shape=(
            jax.ShapeDtypeStruct((heads, rows, HEAD_DIM), jnp.float32),
            jax.ShapeDtypeStruct((heads, rows, 128), jnp.float32),
        ),
        cost_estimate=estimate(area, (q, kv)),
        name="own",
    )(q, kv)
    smem = pl.BlockSpec(memory_space=pltpu.SMEM)

    def first_blocks(count, height):
        return pl.BlockSpec((count, height, HEAD_DIM), lambda *_: (0, 0, 0))

    answer = pl.pallas_call(
        functools.partial(later_kernel, scale),
        out_shape=jax.ShapeDtypeStruct((LEFT + 1, rows, HEAD_DIM), jnp.bfloat16),
        grid=(1,),
        in_specs=[first_blocks(LEFT, rows), first_blocks(LEFT, 2 * rows)],
        out_specs=first_blocks(LEFT + 1, rows),
        cost_estimate=estimate(small, (asked,)),
        name="later",
    )(asked, kv)
    back = shifted(answer, "ctx", heads)
    flag = chunk.reshape(1)
    all_blocks = first_blocks(heads, rows)
    rest, part, stat = pl.pallas_call(
        functools.partial(previous_kernel, scale),
        out_shape=(
            jax.ShapeDtypeStruct((heads, rows, HEAD_DIM), jnp.bfloat16),
            jax.ShapeDtypeStruct((LEFT, rows, HEAD_DIM), jnp.float32),
            jax.ShapeDtypeStruct((LEFT, rows, 128), jnp.float32),
        ),
        grid=(1,),
        in_specs=[smem, all_blocks, first_blocks(heads - LEFT, 2 * rows), all_blocks, all_blocks],
        out_specs=(all_blocks, first_blocks(LEFT, rows), first_blocks(LEFT, rows)),
        cost_estimate=estimate(area - small, (q, kv, out1, stat)),
        name="previous",
    )(flag, q, arriving, out1, stat)
    vmem, anywhere = (pl.BlockSpec(memory_space=m) for m in (pltpu.VMEM, pl.ANY))
    return pl.pallas_call(
        functools.partial(merge_kernel, scale),
        out_shape=jax.ShapeDtypeStruct(rest.shape, rest.dtype),
        in_specs=[smem, vmem, vmem, vmem, anywhere],
        out_specs=anywhere,
        input_output_aliases={4: 0},
        scratch_shapes=[
            pltpu.VMEM((LEFT, rows, HEAD_DIM), rest.dtype),
            pltpu.SemaphoreType.DMA(()),
        ],
        cost_estimate=estimate(0, (part, stat, back)),
        name="merge",
    )(flag, part, stat, back, rest)


def wanted_pieces(table_ref, position, span_count, held):
    pieces = []
    place, plane = position % PLANE, position // PLANE
    for c in range(span_count):
        for slot in range(2):
            source = table_ref[c, slot] // 4
            for later in range(2):
                block = (source + later) // span_count
                relative = (block % PLANE) ^ place
                away = plane - block // PLANE
                column = relative // 2
                index = jnp.where(column == 0, away, 1 + 2 * column + jnp.where(away == 1, 0, 1))
                index = jnp.clip(index, 0, held - 1) + held * (relative % 2)
                pieces.append((index, (source + later) % span_count))
    return pieces


def fetch(refs, rows, index, half, target, sem):
    size = target.shape[0]
    first = 0
    for ref in refs:
        count = ref.shape[0] // rows

        @pl.when((index >= first) & (index < first + count))
        def _(ref=ref, first=first):
            start = pl.multiple_of((index - first) * rows + half * size, size)
            pltpu.make_async_copy(ref.at[pl.ds(start, size), :], target, sem).start()

        first += count


def absorb_kernel(q_ref, weight_ref, out_ref, weights_ref, sems):
    rows, width = q_ref.shape
    span_count = out_ref.shape[0]
    span = rows // span_count
    steps, _, block = weights_ref.shape
    copies = [
        pltpu.make_async_copy(
            weight_ref.at[:, g * block : (g + 1) * block], weights_ref.at[g], sems.at[g]
        )
        for g in range(steps)
    ]
    for copy in copies:
        copy.start()
    for head in range(width // HEAD_DIM):
        g, first = divmod(head * HEAD_DIM, block)
        if first == 0:
            copies[g].wait()
        lanes = slice(head * HEAD_DIM, (head + 1) * HEAD_DIM)
        product = scores_of(q_ref[:, lanes], weights_ref[g, :, first : first + HEAD_DIM])
        product = product.astype(out_ref.dtype)
        for c in range(span_count):
            out_ref[c, head * span : (head + 1) * span, :] = product[c * span : (c + 1) * span]


def cross_kernel(scale, position_ref, table_ref, *refs):
    *in_refs, asks_ref, out_ref = refs[:-6]
    rows_ref, all_asks_ref, means_ref, sems, ask_sems, mean_sems = refs[-6:]
    steps, span_count, asked, _ = all_asks_ref.shape
    rows = in_refs[0].shape[0]
    span = rows // span_count
    held = sum(ref.shape[0] for ref in in_refs) // rows // 2
    pieces = wanted_pieces(table_ref, position_ref[0], span_count, held)
    targets = [rows_ref.at[n * span : (n + 1) * span, :] for n in range(len(pieces))]
    for n, (index, half) in enumerate(pieces):
        fetch(in_refs, rows, index, half, targets[n], sems.at[n])
    ask_copies = [
        pltpu.make_async_copy(
            asks_ref.at[:, g * asked : (g + 1) * asked, :], all_asks_ref.at[g], ask_sems.at[g]
        )
        for g in range(steps)
    ]
    height = means_ref.shape[1]
    mean_copies = [
        pltpu.make_async_copy(
            means_ref.at[g], out_ref.at[g * height : (g + 1) * height, :], mean_sems.at[g]
        )
        for g in range(steps)
    ]
    for copy in ask_copies:
        copy.start()
    for n in range(len(pieces)):
        pltpu.make_async_copy(in_refs[0].at[0:span, :], targets[n], sems.at[n]).wait()

    keys_of_span = rows_ref.shape[0] // span_count
    slot = lax.broadcasted_iota(jnp.int32, (asked, keys_of_span), 1) // (2 * span)
    for g in range(steps):
        ask_copies[g].wait()
        for c in range(span_count):
            count = table_ref[c, 0] % 4
            keys = rows_ref[c * keys_of_span : (c + 1) * keys_of_span, :]
            s = jnp.where(slot < count, scores_of(all_asks_ref[g, c], keys), MASKED_SCORE)
            p = jnp.exp2((s - jnp.max(s, axis=1, keepdims=True)) * scale)
            inverse = jnp.where(count > 0, 1.0 / jnp.sum(p, axis=1, keepdims=True), 0.0)
            mean = jnp.dot(p.astype(jnp.bfloat16), keys, preferred_element_type=jnp.float32)
            mean = (mean * inverse).astype(jnp.bfloat16)
            for h in range(asked // span):
                place = h * rows + c * span
                means_ref[g, place : place + span, :] = mean[h * span : (h + 1) * span]
        mean_copies[g].start()
    for copy in mean_copies:
        copy.wait()


def values_kernel(means_ref, weight_ref, out_ref, all_means_ref, weights_ref, sems):
    rows, width = out_ref.shape
    steps, _, block = weights_ref.shape
    height = all_means_ref.shape[1]
    copies = [
        (
            pltpu.make_async_copy(
                means_ref.at[g * height : (g + 1) * height, :], all_means_ref.at[g], sems.at[0, g]
            ),
            pltpu.make_async_copy(
                weight_ref.at[:, width + g * block : width + (g + 1) * block],
                weights_ref.at[g],
                sems.at[1, g],
            ),
        )
        for g in range(steps)
    ]
    for pair in copies:
        for copy in pair:
            copy.start()
    for g in range(steps):
        for copy in copies[g]:
            copy.wait()
        for h in range(block // HEAD_DIM):
            inner = slice(h * HEAD_DIM, (h + 1) * HEAD_DIM)
            lanes = slice(g * block + h * HEAD_DIM, g * block + (h + 1) * HEAD_DIM)
            out_ref[:, lanes] = jnp.dot(
                all_means_ref[g, h * rows : (h + 1) * rows, :],
                weights_ref[g, :, inner],
                preferred_element_type=jnp.float32,
            )


def cross_attention(cross_queries, encoded, weight, counts, sources, position):
    rows, width = cross_queries.shape
    span_count = counts.shape[0]
    depth = encoded.shape[1]
    heads = width // HEAD_DIM
    place = position % PLANE
    one_back = shifted(encoded, "ctx", PLANE)
    table = sources * 4 + counts[:, None]
    before = shifted(table, "ctx", 1)
    table = jnp.concatenate([before[-1:], table[:-1]], axis=0)
    two_back = shifted(one_back, "ctx", PLANE)
    far = [swapped(jnp.concatenate([encoded, one_back, two_back], axis=0), "ctx", 1)]
    near = []
    for bit in (2, 4, 6):
        other = jnp.where(place < (place ^ bit), encoded, two_back)
        near.append(swapped(jnp.concatenate([one_back, other], axis=0), "ctx", bit))
        far.append(swapped(near[-1], "ctx", 1))

    held = [encoded, one_back, two_back, *near, *far]
    picked = span_count * 4 * SPAN
    pieces = picked // SPAN
    smem, anywhere = (pl.BlockSpec(memory_space=m) for m in (pltpu.SMEM, pl.ANY))
    vmem = pl.BlockSpec(memory_space=pltpu.VMEM)
    block = 4 * HEAD_DIM
    steps = width // block
    asks = pl.pallas_call(
        absorb_kernel,
        out_shape=jax.ShapeDtypeStruct((span_count, heads * SPAN, depth), jnp.bfloat16),
        in_specs=[vmem, anywhere],
        out_specs=vmem,
        scratch_shapes=[
            pltpu.VMEM((steps, depth, block), weight.dtype),
            pltpu.SemaphoreType.DMA((steps,)),
        ],
        cost_estimate=pl.CostEstimate(
            flops=2 * rows * depth * width, bytes_accessed=2 * weight.size, transcendentals=0
        ),
        name="absorb",
    )(cross_queries, weight)
    halves_of_heads = 2
    means = pl.pallas_call(
        functools.partial(cross_kernel, HEAD_DIM ** (-0.5) * LOG2E),
        out_shape=jax.ShapeDtypeStruct((heads * rows, depth), jnp.bfloat16),
        in_specs=[smem] * 2 + [anywhere] * (len(held) + 1),
        out_specs=anywhere,
        scratch_shapes=[
            pltpu.VMEM((picked, depth), encoded.dtype),
            pltpu.VMEM(
                (halves_of_heads, span_count, heads * SPAN // halves_of_heads, depth), asks.dtype
            ),
            pltpu.VMEM((halves_of_heads, heads * rows // halves_of_heads, depth), jnp.bfloat16),
            pltpu.SemaphoreType.DMA((pieces,)),
            pltpu.SemaphoreType.DMA((halves_of_heads,)),
            pltpu.SemaphoreType.DMA((halves_of_heads,)),
        ],
        cost_estimate=pl.CostEstimate(
            flops=4 * picked * depth * heads * SPAN,
            bytes_accessed=asks.size * 4 + picked * depth * 2,
            transcendentals=picked * SPAN * heads,
        ),
        name="cross",
    )(position.reshape(1), table, *held, asks)
    return pl.pallas_call(
        values_kernel,
        out_shape=jax.ShapeDtypeStruct((rows, width), jnp.float32),
        in_specs=[anywhere] * 2,
        out_specs=vmem,
        scratch_shapes=[
            pltpu.VMEM((steps, heads * rows // steps, depth), jnp.bfloat16),
            pltpu.VMEM((steps, depth, block), weight.dtype),
            pltpu.SemaphoreType.DMA((2, steps)),
        ],
        cost_estimate=pl.CostEstimate(
            flops=2 * rows * depth * width,
            bytes_accessed=weight.size + means.size * 2,
            transcendentals=0,
        ),
        name="values",
    )(means, weight)


def sum_kernel(self_ref, cross_ref, out_ref):
    for head in range(self_ref.shape[0]):
        lanes = slice(head * HEAD_DIM, (head + 1) * HEAD_DIM)
        out_ref[:, lanes] = (self_ref[head].astype(jnp.float32) + cross_ref[:, lanes]).astype(
            out_ref.dtype
        )


def per_device(
    queries, self_keys, self_values, cross_queries, encoded, neighbour_weight, counts, sources
):
    position = lax.axis_index("ctx")
    count = lax.axis_size("ctx")
    groups = [list(range(first, first + HEADS)) for first in range(0, count, HEADS)]
    cross_part = cross_attention(
        cross_queries, encoded, neighbour_weight, counts, sources, position
    )
    by_head = self_attention(queries, self_keys, self_values, position // HEADS, groups)
    self_part = lax.all_to_all(by_head, "ctx", 0, 0, axis_index_groups=groups, tiled=True)
    return pl.pallas_call(
        sum_kernel,
        out_shape=jax.ShapeDtypeStruct(queries.shape, jnp.bfloat16),
        name="total",
    )(self_part, cross_part)


def solution(mesh):
    return jax.shard_map(
        per_device,
        mesh=mesh,
        in_specs=(
            P(("groups", "ctx"), None),
            P(("groups", "ctx"), None),
            P(("groups", "ctx"), None),
            P(("groups", "ctx"), None),
            P(("groups", "ctx"), None),
            P(),
            P(("groups", "ctx")),
            P(("groups", "ctx"), None),
        ),
        out_specs=P(("groups", "ctx"), None),
        check_vma=False,
    )
```

```python
import functools

import jax
import jax.numpy as jnp
from jax import lax
from jax.experimental import pallas as pl
from jax.experimental.pallas import tpu as pltpu
from jax.sharding import PartitionSpec as P


HEADS = 16
HEAD_DIM = 128
SPAN = 64
PLANE = 8
LEFT = 8

MASKED_SCORE = -1e30
LOG2E = 1.4426950408889634


def shifted(value, axis, steps):
    count = lax.axis_size(axis)
    first, last = (max(0, -steps), min(count, count - steps))
    return lax.ppermute(value, axis, [(source, source + steps) for source in range(first, last)])


def swapped(value, axis, bit):
    count = lax.axis_size(axis)
    return lax.ppermute(value, axis, [(source, source ^ bit) for source in range(count)])


def pack_kernel(*refs):
    *in_refs, out_ref = refs
    rows = in_refs[0].shape[0]
    for head in range(out_ref.shape[0]):
        columns = slice(head * HEAD_DIM, (head + 1) * HEAD_DIM)
        for n, ref in enumerate(in_refs):
            out_ref[head, n * rows : (n + 1) * rows, :] = ref[:, columns]


def packed(*arrays):
    rows, width = arrays[0].shape
    return pl.pallas_call(
        pack_kernel,
        out_shape=jax.ShapeDtypeStruct(
            (width // HEAD_DIM, len(arrays) * rows, HEAD_DIM), arrays[0].dtype
        ),
        cost_estimate=pl.CostEstimate(
            flops=0, bytes_accessed=4 * len(arrays) * rows * width, transcendentals=0
        ),
        name="pack",
    )(*arrays)


def scores_of(q, k):
    return lax.dot_general(q, k, (((1,), (1,)), ((), ())), preferred_element_type=jnp.float32)


def softmax_parts(q, pieces, scale, start=None):
    scores = []
    for k, _, mask in pieces:
        s = scores_of(q, k)
        scores.append(s if mask is None else jnp.where(mask, s, MASKED_SCORE))
    largest = functools.reduce(jnp.maximum, [jnp.max(s, axis=1, keepdims=True) for s in scores])
    total, out = None, None
    if start is not None:
        out, before, total = start
        largest = jnp.maximum(largest, before)
        weight = jnp.exp2((before - largest) * scale)
        out, total = out * weight, total * weight
    for s, (_, v, _) in zip(scores, pieces):
        p = jnp.exp2((s - largest) * scale)
        t = jnp.sum(p, axis=1, keepdims=True)
        o = jnp.dot(p.astype(jnp.bfloat16), v, preferred_element_type=jnp.float32)
        total = t if total is None else total + t
        out = o if out is None else out + o
    return out, largest, total


def with_stats(largest, total):
    lane = lax.broadcasted_iota(jnp.int32, (largest.shape[0], 128), 1)
    return jnp.where(lane < 64, largest, total)


def halves(stat):
    return stat[:, 0:1], stat[:, 64:65]


def thirds(x):
    high = x.astype(jnp.bfloat16)
    rest = x - high.astype(jnp.float32)
    middle = rest.astype(jnp.bfloat16)
    low = (rest - middle.astype(jnp.float32)).astype(jnp.bfloat16)
    return high, middle, low


def taken(ref, first, count, start, rows):
    return ref[first : first + count, start : start + rows, :].reshape(count * rows, ref.shape[2])


def triangle(size, keep):
    row = lax.broadcasted_iota(jnp.int32, (size, size), 0)
    column = lax.broadcasted_iota(jnp.int32, (size, size), 1)
    return keep(column, row)


def own_kernel(scale, q_ref, kv_ref, out_ref, stat_ref):
    blocks, rows, dim = q_ref.shape
    causal = triangle(2 * rows, lambda column, row: column <= row)
    for i in range(0, blocks, 2):
        spans = [(i, 2, causal)] + ([(0, i, None)] if i else [])
        pieces = [
            (taken(kv_ref, f, n, 0, rows), taken(kv_ref, f, n, rows, rows), mask)
            for f, n, mask in spans
        ]
        out, largest, total = softmax_parts(taken(q_ref, i, 2, 0, rows), pieces, scale)
        out_ref[i : i + 2] = out.reshape(2, rows, dim)
        stat_ref[i : i + 2] = with_stats(largest, total).reshape(2, rows, 128)


def later_kernel(scale, q_ref, kv_ref, out_ref):
    blocks, rows, dim = q_ref.shape
    later = triangle(2 * rows, lambda column, row: column > row)
    out_ref[blocks] = jnp.zeros((rows, dim), out_ref.dtype)
    for i in range(0, blocks, 2):
        spans = [(i, 2, later)] + ([(i + 2, blocks - i - 2, None)] if i + 2 < blocks else [])
        pieces = [
            (taken(kv_ref, f, n, 0, rows), taken(kv_ref, f, n, rows, rows), mask)
            for f, n, mask in spans
        ]
        out, largest, total = softmax_parts(taken(q_ref, i, 2, 0, rows), pieces, scale)
        out_ref[i : i + 2] = out.reshape(2, rows, dim).astype(out_ref.dtype)
        stat = with_stats(largest, total)
        for n in range(2):
            turned = stat[n * rows : (n + 1) * rows].T
            for m, row in enumerate((turned[0:1], turned[64:65])):
                for k, part in enumerate(thirds(row)):
                    place = ((i + n) * 2 + m) * 3 + k
                    out_ref[blocks, place : place + 1, :] = part


def sent_stats(ref, block, rows):
    values = []
    for m in range(2):
        place = (block * 2 + m) * 3
        three = ref[ref.shape[0] - 1, place : place + 3, :].astype(jnp.float32)
        values.append(three[0:1] + three[1:2] + three[2:3])
    sublane = lax.broadcasted_iota(jnp.int32, (rows, 128), 0)
    return jnp.where(sublane < 64, values[0], values[1]).T


def previous_kernel(scale, flag_ref, q_ref, kv_ref, back_ref, out1_ref, stat1_ref, out_ref):
    blocks, rows, dim = q_ref.shape
    sent = back_ref.shape[0] - 1
    later = triangle(2 * rows, lambda column, row: column > row)

    def own_part(i):
        stat = stat1_ref[i : i + 2].reshape(2 * rows, 128)
        return (out1_ref[i : i + 2].reshape(2 * rows, dim), *halves(stat))

    def with_sent(i):
        out1, largest1, total1 = own_part(i)
        stat = jnp.concatenate([sent_stats(back_ref, i + n, rows) for n in range(2)], axis=0)
        largest2, total2 = halves(stat)
        top = jnp.maximum(largest1, largest2)
        a, b = jnp.exp2((largest1 - top) * scale), jnp.exp2((largest2 - top) * scale)
        out2 = taken(back_ref, i, 2, 0, rows).astype(jnp.float32)
        return out1 * a + out2 * b, top, total1 * a + total2 * b

    def store(i, part):
        out, _, total = part
        out = out * (1.0 / total)
        out_ref[i : i + 2] = out.reshape(2, rows, dim).astype(out_ref.dtype)

    @pl.when(flag_ref[0] > 0)
    def _():
        for i in range(0, blocks, 2):
            first = max(i - sent, 0)
            spans = [(first, 2, later)] if i >= sent else []
            first += 2 * len(spans)
            if first < kv_ref.shape[0]:
                spans.append((first, kv_ref.shape[0] - first, None))
            pieces = [
                (taken(kv_ref, f, n, 0, rows), taken(kv_ref, f, n, rows, rows), mask)
                for f, n, mask in spans
            ]
            start = with_sent(i) if i < sent else own_part(i)
            store(i, softmax_parts(taken(q_ref, i, 2, 0, rows), pieces, scale, start))

    @pl.when(flag_ref[0] == 0)
    def _():
        for i in range(0, blocks, 2):
            store(i, own_part(i))


def estimate(area, arrays):
    return pl.CostEstimate(
        flops=4 * HEAD_DIM * area,
        bytes_accessed=sum(2 * a.size for a in arrays),
        transcendentals=area,
    )


def self_attention(queries, keys, values, chunk, groups):
    rows, width = queries.shape
    heads = width // HEAD_DIM
    scale = HEAD_DIM ** (-0.5) * LOG2E
    kv = lax.all_to_all(
        packed(keys, values), "ctx", 0, 0, axis_index_groups=groups, tiled=True
    )
    arriving = shifted(kv[LEFT:], "ctx", heads)
    q = lax.all_to_all(packed(queries), "ctx", 0, 0, axis_index_groups=groups, tiled=True)
    asked = shifted(q[:LEFT], "ctx", -heads)
    area = (heads * rows) ** 2 // 2
    small = (LEFT * rows) ** 2 // 2
    out1, stat = pl.pallas_call(
        functools.partial(own_kernel, scale),
        out_shape=(
            jax.ShapeDtypeStruct((heads, rows, HEAD_DIM), jnp.float32),
            jax.ShapeDtypeStruct((heads, rows, 128), jnp.float32),
        ),
        cost_estimate=estimate(area, (q, kv)),
        name="own",
    )(q, kv)
    smem = pl.BlockSpec(memory_space=pltpu.SMEM)

    def first_blocks(count, height):
        return pl.BlockSpec((count, height, HEAD_DIM), lambda *_: (0, 0, 0))

    answer = pl.pallas_call(
        functools.partial(later_kernel, scale),
        out_shape=jax.ShapeDtypeStruct((LEFT + 1, rows, HEAD_DIM), jnp.bfloat16),
        grid=(1,),
        in_specs=[first_blocks(LEFT, rows), first_blocks(LEFT, 2 * rows)],
        out_specs=first_blocks(LEFT + 1, rows),
        cost_estimate=estimate(small, (asked,)),
        name="later",
    )(asked, kv)
    back = shifted(answer, "ctx", heads)
    flag = chunk.reshape(1)
    vmem = pl.BlockSpec(memory_space=pltpu.VMEM)
    return pl.pallas_call(
        functools.partial(previous_kernel, scale),
        out_shape=jax.ShapeDtypeStruct((heads, rows, HEAD_DIM), jnp.bfloat16),
        in_specs=[smem] + [vmem] * 5,
        cost_estimate=estimate(area - small, (q, kv, out1, stat)),
        name="previous",
    )(flag, q, arriving, back, out1, stat)


def wanted_pieces(table_ref, position, span_count, held):
    pieces = []
    place, plane = position % PLANE, position // PLANE
    for c in range(span_count):
        for slot in range(2):
            source = table_ref[c, slot] // 4
            for later in range(2):
                block = (source + later) // span_count
                relative = (block % PLANE) ^ place
                away = plane - block // PLANE
                column = relative // 2
                index = jnp.where(column == 0, away, 1 + 2 * column + jnp.where(away == 1, 0, 1))
                index = jnp.clip(index, 0, held - 1) + held * (relative % 2)
                pieces.append((index, (source + later) % span_count))
    return pieces


def fetch(refs, rows, index, half, target, sem):
    size = target.shape[0]
    first = 0
    for ref in refs:
        count = ref.shape[0] // rows

        @pl.when((index >= first) & (index < first + count))
        def _(ref=ref, first=first):
            start = pl.multiple_of((index - first) * rows + half * size, size)
            pltpu.make_async_copy(ref.at[pl.ds(start, size), :], target, sem).start()

        first += count


def absorb_kernel(q_ref, weight_ref, out_ref, weights_ref, sems):
    rows, width = q_ref.shape
    span_count = out_ref.shape[0]
    span = rows // span_count
    steps, _, block = weights_ref.shape
    copies = [
        pltpu.make_async_copy(
            weight_ref.at[:, g * block : (g + 1) * block], weights_ref.at[g], sems.at[g]
        )
        for g in range(steps)
    ]
    for copy in copies:
        copy.start()
    for head in range(width // HEAD_DIM):
        g, first = divmod(head * HEAD_DIM, block)
        if first == 0:
            copies[g].wait()
        lanes = slice(head * HEAD_DIM, (head + 1) * HEAD_DIM)
        product = scores_of(q_ref[:, lanes], weights_ref[g, :, first : first + HEAD_DIM])
        product = product.astype(out_ref.dtype)
        for c in range(span_count):
            out_ref[c, head * span : (head + 1) * span, :] = product[c * span : (c + 1) * span]


def cross_kernel(scale, position_ref, table_ref, *refs):
    *in_refs, asks_ref, out_ref = refs[:-6]
    rows_ref, all_asks_ref, means_ref, sems, ask_sems, mean_sems = refs[-6:]
    steps, span_count, asked, _ = all_asks_ref.shape
    rows = in_refs[0].shape[0]
    span = rows // span_count
    held = sum(ref.shape[0] for ref in in_refs) // rows // 2
    pieces = wanted_pieces(table_ref, position_ref[0], span_count, held)
    targets = [rows_ref.at[n * span : (n + 1) * span, :] for n in range(len(pieces))]
    for n, (index, half) in enumerate(pieces):
        fetch(in_refs, rows, index, half, targets[n], sems.at[n])
    ask_copies = [
        pltpu.make_async_copy(
            asks_ref.at[:, g * asked : (g + 1) * asked, :], all_asks_ref.at[g], ask_sems.at[g]
        )
        for g in range(steps)
    ]
    height = means_ref.shape[1]
    mean_copies = [
        pltpu.make_async_copy(
            means_ref.at[g], out_ref.at[g * height : (g + 1) * height, :], mean_sems.at[g]
        )
        for g in range(steps)
    ]
    for copy in ask_copies:
        copy.start()
    for n in range(len(pieces)):
        pltpu.make_async_copy(in_refs[0].at[0:span, :], targets[n], sems.at[n]).wait()

    keys_of_span = rows_ref.shape[0] // span_count
    slot = lax.broadcasted_iota(jnp.int32, (asked, keys_of_span), 1) // (2 * span)
    for g in range(steps):
        ask_copies[g].wait()
        for c in range(span_count):
            count = table_ref[c, 0] % 4
            keys = rows_ref[c * keys_of_span : (c + 1) * keys_of_span, :]
            s = jnp.where(slot < count, scores_of(all_asks_ref[g, c], keys), MASKED_SCORE)
            p = jnp.exp2((s - jnp.max(s, axis=1, keepdims=True)) * scale)
            inverse = jnp.where(count > 0, 1.0 / jnp.sum(p, axis=1, keepdims=True), 0.0)
            mean = jnp.dot(p.astype(jnp.bfloat16), keys, preferred_element_type=jnp.float32)
            mean = (mean * inverse).astype(jnp.bfloat16)
            for h in range(asked // span):
                place = h * rows + c * span
                means_ref[g, place : place + span, :] = mean[h * span : (h + 1) * span]
        mean_copies[g].start()
    for copy in mean_copies:
        copy.wait()


def values_kernel(means_ref, weight_ref, out_ref, all_means_ref, weights_ref, sems):
    rows, width = out_ref.shape
    steps, _, block = weights_ref.shape
    height = all_means_ref.shape[1]
    copies = [
        (
            pltpu.make_async_copy(
                means_ref.at[g * height : (g + 1) * height, :], all_means_ref.at[g], sems.at[0, g]
            ),
            pltpu.make_async_copy(
                weight_ref.at[:, width + g * block : width + (g + 1) * block],
                weights_ref.at[g],
                sems.at[1, g],
            ),
        )
        for g in range(steps)
    ]
    for pair in copies:
        for copy in pair:
            copy.start()
    for g in range(steps):
        for copy in copies[g]:
            copy.wait()
        for h in range(block // HEAD_DIM):
            inner = slice(h * HEAD_DIM, (h + 1) * HEAD_DIM)
            lanes = slice(g * block + h * HEAD_DIM, g * block + (h + 1) * HEAD_DIM)
            out_ref[:, lanes] = jnp.dot(
                all_means_ref[g, h * rows : (h + 1) * rows, :],
                weights_ref[g, :, inner],
                preferred_element_type=jnp.float32,
            )


def cross_attention(cross_queries, encoded, weight, counts, sources, position):
    rows, width = cross_queries.shape
    span_count = counts.shape[0]
    depth = encoded.shape[1]
    heads = width // HEAD_DIM
    place = position % PLANE
    one_back = shifted(encoded, "ctx", PLANE)
    table = sources * 4 + counts[:, None]
    before = shifted(table, "ctx", 1)
    table = jnp.concatenate([before[-1:], table[:-1]], axis=0)
    two_back = shifted(one_back, "ctx", PLANE)
    far = [swapped(jnp.concatenate([encoded, one_back, two_back], axis=0), "ctx", 1)]
    near = []
    for bit in (2, 4, 6):
        other = jnp.where(place < (place ^ bit), encoded, two_back)
        near.append(swapped(jnp.concatenate([one_back, other], axis=0), "ctx", bit))
        far.append(swapped(near[-1], "ctx", 1))

    held = [encoded, one_back, two_back, *near, *far]
    picked = span_count * 4 * SPAN
    pieces = picked // SPAN
    smem, anywhere = (pl.BlockSpec(memory_space=m) for m in (pltpu.SMEM, pl.ANY))
    vmem = pl.BlockSpec(memory_space=pltpu.VMEM)
    block = 4 * HEAD_DIM
    steps = width // block
    asks = pl.pallas_call(
        absorb_kernel,
        out_shape=jax.ShapeDtypeStruct((span_count, heads * SPAN, depth), jnp.bfloat16),
        in_specs=[vmem, anywhere],
        out_specs=vmem,
        scratch_shapes=[
            pltpu.VMEM((steps, depth, block), weight.dtype),
            pltpu.SemaphoreType.DMA((steps,)),
        ],
        cost_estimate=pl.CostEstimate(
            flops=2 * rows * depth * width, bytes_accessed=2 * weight.size, transcendentals=0
        ),
        name="absorb",
    )(cross_queries, weight)
    halves_of_heads = 2
    means = pl.pallas_call(
        functools.partial(cross_kernel, HEAD_DIM ** (-0.5) * LOG2E),
        out_shape=jax.ShapeDtypeStruct((heads * rows, depth), jnp.bfloat16),
        in_specs=[smem] * 2 + [anywhere] * (len(held) + 1),
        out_specs=anywhere,
        scratch_shapes=[
            pltpu.VMEM((picked, depth), encoded.dtype),
            pltpu.VMEM(
                (halves_of_heads, span_count, heads * SPAN // halves_of_heads, depth), asks.dtype
            ),
            pltpu.VMEM((halves_of_heads, heads * rows // halves_of_heads, depth), jnp.bfloat16),
            pltpu.SemaphoreType.DMA((pieces,)),
            pltpu.SemaphoreType.DMA((halves_of_heads,)),
            pltpu.SemaphoreType.DMA((halves_of_heads,)),
        ],
        cost_estimate=pl.CostEstimate(
            flops=4 * picked * depth * heads * SPAN,
            bytes_accessed=asks.size * 4 + picked * depth * 2,
            transcendentals=picked * SPAN * heads,
        ),
        name="cross",
    )(position.reshape(1), table, *held, asks)
    return pl.pallas_call(
        values_kernel,
        out_shape=jax.ShapeDtypeStruct((rows, width), jnp.float32),
        in_specs=[anywhere] * 2,
        out_specs=vmem,
        scratch_shapes=[
            pltpu.VMEM((steps, heads * rows // steps, depth), jnp.bfloat16),
            pltpu.VMEM((steps, depth, block), weight.dtype),
            pltpu.SemaphoreType.DMA((2, steps)),
        ],
        cost_estimate=pl.CostEstimate(
            flops=2 * rows * depth * width,
            bytes_accessed=weight.size + means.size * 2,
            transcendentals=0,
        ),
        name="values",
    )(means, weight)


def per_device(
    queries, self_keys, self_values, cross_queries, encoded, neighbour_weight, counts, sources
):
    position = lax.axis_index("ctx")
    count = lax.axis_size("ctx")
    groups = [list(range(first, first + HEADS)) for first in range(0, count, HEADS)]
    cross_part = cross_attention(
        cross_queries, encoded, neighbour_weight, counts, sources, position
    )
    by_head = self_attention(queries, self_keys, self_values, position // HEADS, groups)
    self_part = lax.all_to_all(by_head, "ctx", 0, 0, axis_index_groups=groups, tiled=True)
    self_part = jnp.moveaxis(self_part.astype(jnp.float32), 0, 1).reshape(queries.shape)
    return (self_part + cross_part).astype(jnp.bfloat16)


def solution(mesh):
    return jax.shard_map(
        per_device,
        mesh=mesh,
        in_specs=(
            P(("groups", "ctx"), None),
            P(("groups", "ctx"), None),
            P(("groups", "ctx"), None),
            P(("groups", "ctx"), None),
            P(("groups", "ctx"), None),
            P(),
            P(("groups", "ctx")),
            P(("groups", "ctx"), None),
        ),
        out_specs=P(("groups", "ctx"), None),
        check_vma=False,
    )
```

```python
import functools

import jax
import jax.numpy as jnp
from jax import lax
from jax.experimental import pallas as pl
from jax.experimental.pallas import tpu as pltpu
from jax.sharding import PartitionSpec as P


HEADS = 16
HEAD_DIM = 128
SPAN = 64
PLANE = 8
LEFT = 8

MASKED_SCORE = -1e30
LOG2E = 1.4426950408889634


def shifted(value, axis, steps):
    count = lax.axis_size(axis)
    first, last = (max(0, -steps), min(count, count - steps))
    return lax.ppermute(value, axis, [(source, source + steps) for source in range(first, last)])


def swapped(value, axis, bit):
    count = lax.axis_size(axis)
    return lax.ppermute(value, axis, [(source, source ^ bit) for source in range(count)])


def pack_kernel(*refs):
    *in_refs, out_ref = refs
    rows = in_refs[0].shape[0]
    for head in range(out_ref.shape[0]):
        columns = slice(head * HEAD_DIM, (head + 1) * HEAD_DIM)
        for n, ref in enumerate(in_refs):
            out_ref[head, n * rows : (n + 1) * rows, :] = ref[:, columns]


def packed(*arrays):
    rows, width = arrays[0].shape
    return pl.pallas_call(
        pack_kernel,
        out_shape=jax.ShapeDtypeStruct(
            (width // HEAD_DIM, len(arrays) * rows, HEAD_DIM), arrays[0].dtype
        ),
        cost_estimate=pl.CostEstimate(
            flops=0, bytes_accessed=4 * len(arrays) * rows * width, transcendentals=0
        ),
        name="pack",
    )(*arrays)


def scores_of(q, k):
    return lax.dot_general(q, k, (((1,), (1,)), ((), ())), preferred_element_type=jnp.float32)


def softmax_parts(q, pieces, scale, start=None):
    scores = []
    for k, _, mask in pieces:
        s = scores_of(q, k)
        scores.append(s if mask is None else jnp.where(mask, s, MASKED_SCORE))
    largest = functools.reduce(jnp.maximum, [jnp.max(s, axis=1, keepdims=True) for s in scores])
    total, out = None, None
    if start is not None:
        out, before, total = start
        largest = jnp.maximum(largest, before)
        weight = jnp.exp2((before - largest) * scale)
        out, total = out * weight, total * weight
    for s, (_, v, _) in zip(scores, pieces):
        p = jnp.exp2((s - largest) * scale)
        t = jnp.sum(p, axis=1, keepdims=True)
        o = jnp.dot(p.astype(jnp.bfloat16), v, preferred_element_type=jnp.float32)
        total = t if total is None else total + t
        out = o if out is None else out + o
    return out, largest, total


def with_stats(largest, total):
    lane = lax.broadcasted_iota(jnp.int32, (largest.shape[0], 128), 1)
    return jnp.where(lane < 64, largest, total)


def halves(stat):
    return stat[:, 0:1], stat[:, 64:65]


def thirds(x):
    high = x.astype(jnp.bfloat16)
    rest = x - high.astype(jnp.float32)
    middle = rest.astype(jnp.bfloat16)
    low = (rest - middle.astype(jnp.float32)).astype(jnp.bfloat16)
    return high, middle, low


def taken(ref, first, count, start, rows):
    return ref[first : first + count, start : start + rows, :].reshape(count * rows, ref.shape[2])


def triangle(size, keep):
    row = lax.broadcasted_iota(jnp.int32, (size, size), 0)
    column = lax.broadcasted_iota(jnp.int32, (size, size), 1)
    return keep(column, row)


def own_kernel(scale, q_ref, kv_ref, out_ref, stat_ref):
    blocks, rows, dim = q_ref.shape
    causal = triangle(2 * rows, lambda column, row: column <= row)
    for i in range(0, blocks, 2):
        spans = [(i, 2, causal)] + ([(0, i, None)] if i else [])
        pieces = [
            (taken(kv_ref, f, n, 0, rows), taken(kv_ref, f, n, rows, rows), mask)
            for f, n, mask in spans
        ]
        out, largest, total = softmax_parts(taken(q_ref, i, 2, 0, rows), pieces, scale)
        out_ref[i : i + 2] = out.reshape(2, rows, dim)
        stat_ref[i : i + 2] = with_stats(largest, total).reshape(2, rows, 128)


def later_kernel(scale, q_ref, kv_ref, out_ref):
    blocks, rows, dim = q_ref.shape
    later = triangle(2 * rows, lambda column, row: column > row)
    out_ref[blocks] = jnp.zeros((rows, dim), out_ref.dtype)
    for i in range(0, blocks, 2):
        spans = [(i, 2, later)] + ([(i + 2, blocks - i - 2, None)] if i + 2 < blocks else [])
        pieces = [
            (taken(kv_ref, f, n, 0, rows), taken(kv_ref, f, n, rows, rows), mask)
            for f, n, mask in spans
        ]
        out, largest, total = softmax_parts(taken(q_ref, i, 2, 0, rows), pieces, scale)
        out_ref[i : i + 2] = out.reshape(2, rows, dim).astype(out_ref.dtype)
        stat = with_stats(largest, total)
        for n in range(2):
            turned = stat[n * rows : (n + 1) * rows].T
            for m, row in enumerate((turned[0:1], turned[64:65])):
                for k, part in enumerate(thirds(row)):
                    place = ((i + n) * 2 + m) * 3 + k
                    out_ref[blocks, place : place + 1, :] = part


def sent_stats(ref, block, rows):
    values = []
    for m in range(2):
        place = (block * 2 + m) * 3
        three = ref[ref.shape[0] - 1, place : place + 3, :].astype(jnp.float32)
        values.append(three[0:1] + three[1:2] + three[2:3])
    sublane = lax.broadcasted_iota(jnp.int32, (rows, 128), 0)
    return jnp.where(sublane < 64, values[0], values[1]).T


def previous_kernel(scale, flag_ref, q_ref, kv_ref, out1_ref, stat1_ref, out_ref, part_ref, stat_ref):
    blocks, rows, dim = q_ref.shape
    waiting = part_ref.shape[0]
    later = triangle(2 * rows, lambda column, row: column > row)

    def own_part(i):
        stat = stat1_ref[i : i + 2].reshape(2 * rows, 128)
        return (out1_ref[i : i + 2].reshape(2 * rows, dim), *halves(stat))

    def store(i, part):
        out, largest, total = part
        if i < waiting:
            part_ref[i : i + 2] = out.reshape(2, rows, dim)
            stat_ref[i : i + 2] = with_stats(largest, total).reshape(2, rows, 128)
        else:
            out = out * (1.0 / total)
            out_ref[i : i + 2] = out.reshape(2, rows, dim).astype(out_ref.dtype)

    @pl.when(flag_ref[0] > 0)
    def _():
        for i in range(0, blocks, 2):
            first = max(i - waiting, 0)
            spans = [(first, 2, later)] if i >= waiting else []
            first += 2 * len(spans)
            if first < kv_ref.shape[0]:
                spans.append((first, kv_ref.shape[0] - first, None))
            pieces = [
                (taken(kv_ref, f, n, 0, rows), taken(kv_ref, f, n, rows, rows), mask)
                for f, n, mask in spans
            ]
            store(i, softmax_parts(taken(q_ref, i, 2, 0, rows), pieces, scale, own_part(i)))

    @pl.when(flag_ref[0] == 0)
    def _():
        part_ref[...] = out1_ref[0:waiting]
        stat_ref[...] = stat1_ref[0:waiting]
        for i in range(waiting, blocks, 2):
            store(i, own_part(i))


def merge_kernel(scale, flag_ref, part_ref, stat_ref, back_ref, rest_ref, out_ref, done_ref, sem):
    del rest_ref
    blocks, rows, dim = part_ref.shape
    for i in range(0, blocks, 2):
        out1, largest1, total1 = (
            part_ref[i : i + 2].reshape(2 * rows, dim),
            *halves(stat_ref[i : i + 2].reshape(2 * rows, 128)),
        )
        stat = jnp.concatenate([sent_stats(back_ref, i + n, rows) for n in range(2)], axis=0)
        largest2, total2 = halves(stat)
        largest2 = jnp.where(flag_ref[0] > 0, largest2, MASKED_SCORE)
        top = jnp.maximum(largest1, largest2)
        a, b = jnp.exp2((largest1 - top) * scale), jnp.exp2((largest2 - top) * scale)
        inverse = 1.0 / (a * total1 + b * total2)
        out2 = taken(back_ref, i, 2, 0, rows).astype(jnp.float32)
        out = out1 * (a * inverse) + out2 * (b * inverse)
        done_ref[i : i + 2] = out.reshape(2, rows, dim).astype(done_ref.dtype)
    copy = pltpu.make_async_copy(done_ref, out_ref.at[0:blocks], sem)
    copy.start()
    copy.wait()


def estimate(area, arrays):
    return pl.CostEstimate(
        flops=4 * HEAD_DIM * area,
        bytes_accessed=sum(2 * a.size for a in arrays),
        transcendentals=area,
    )


def self_attention(queries, keys, values, chunk, groups):
    rows, width = queries.shape
    heads = width // HEAD_DIM
    scale = HEAD_DIM ** (-0.5) * LOG2E
    kv = lax.all_to_all(
        packed(keys, values), "ctx", 0, 0, axis_index_groups=groups, tiled=True
    )
    arriving = shifted(kv[LEFT:], "ctx", heads)
    q = lax.all_to_all(packed(queries), "ctx", 0, 0, axis_index_groups=groups, tiled=True)
    asked = shifted(q[:LEFT], "ctx", -heads)
    area = (heads * rows) ** 2 // 2
    small = (LEFT * rows) ** 2 // 2
    out1, stat = pl.pallas_call(
        functools.partial(own_kernel, scale),
        out_shape=(
            jax.ShapeDtypeStruct((heads, rows, HEAD_DIM), jnp.float32),
            jax.ShapeDtypeStruct((heads, rows, 128), jnp.float32),
        ),
        cost_estimate=estimate(area, (q, kv)),
        name="own",
    )(q, kv)
    smem = pl.BlockSpec(memory_space=pltpu.SMEM)

    def first_blocks(count, height):
        return pl.BlockSpec((count, height, HEAD_DIM), lambda *_: (0, 0, 0))

    answer = pl.pallas_call(
        functools.partial(later_kernel, scale),
        out_shape=jax.ShapeDtypeStruct((LEFT + 1, rows, HEAD_DIM), jnp.bfloat16),
        grid=(1,),
        in_specs=[first_blocks(LEFT, rows), first_blocks(LEFT, 2 * rows)],
        out_specs=first_blocks(LEFT + 1, rows),
        cost_estimate=estimate(small, (asked,)),
        name="later",
    )(asked, kv)
    back = shifted(answer, "ctx", heads)
    flag = chunk.reshape(1)
    all_blocks = first_blocks(heads, rows)
    rest, part, stat = pl.pallas_call(
        functools.partial(previous_kernel, scale),
        out_shape=(
            jax.ShapeDtypeStruct((heads, rows, HEAD_DIM), jnp.bfloat16),
            jax.ShapeDtypeStruct((LEFT, rows, HEAD_DIM), jnp.float32),
            jax.ShapeDtypeStruct((LEFT, rows, 128), jnp.float32),
        ),
        grid=(1,),
        in_specs=[smem, all_blocks, first_blocks(heads - LEFT, 2 * rows), all_blocks, all_blocks],
        out_specs=(all_blocks, first_blocks(LEFT, rows), first_blocks(LEFT, rows)),
        cost_estimate=estimate(area - small, (q, kv, out1, stat)),
        name="previous",
    )(flag, q, arriving, out1, stat)
    vmem, anywhere = (pl.BlockSpec(memory_space=m) for m in (pltpu.VMEM, pl.ANY))
    return pl.pallas_call(
        functools.partial(merge_kernel, scale),
        out_shape=jax.ShapeDtypeStruct(rest.shape, rest.dtype),
        in_specs=[smem, vmem, vmem, vmem, anywhere],
        out_specs=anywhere,
        input_output_aliases={4: 0},
        scratch_shapes=[
            pltpu.VMEM((LEFT, rows, HEAD_DIM), rest.dtype),
            pltpu.SemaphoreType.DMA(()),
        ],
        cost_estimate=estimate(0, (part, stat, back)),
        name="merge",
    )(flag, part, stat, back, rest)


def wanted_pieces(table_ref, position, span_count, held):
    pieces = []
    place, plane = position % PLANE, position // PLANE
    for c in range(span_count):
        for slot in range(2):
            source = table_ref[c, slot] // 4
            for later in range(2):
                block = (source + later) // span_count
                relative = (block % PLANE) ^ place
                away = plane - block // PLANE
                column = relative // 2
                index = jnp.where(column == 0, away, 1 + 2 * column + jnp.where(away == 1, 0, 1))
                index = jnp.clip(index, 0, held - 1) + held * (relative % 2)
                pieces.append((index, (source + later) % span_count))
    return pieces


def fetch(refs, rows, index, half, target, sem):
    size = target.shape[0]
    first = 0
    for ref in refs:
        count = ref.shape[0] // rows

        @pl.when((index >= first) & (index < first + count))
        def _(ref=ref, first=first):
            start = pl.multiple_of((index - first) * rows + half * size, size)
            pltpu.make_async_copy(ref.at[pl.ds(start, size), :], target, sem).start()

        first += count


def absorb_kernel(q_ref, weight_ref, out_ref, weights_ref, sems):
    rows, width = q_ref.shape
    span_count = out_ref.shape[0]
    span = rows // span_count
    steps, _, block = weights_ref.shape
    copies = [
        pltpu.make_async_copy(
            weight_ref.at[:, g * block : (g + 1) * block], weights_ref.at[g], sems.at[g]
        )
        for g in range(steps)
    ]
    for copy in copies:
        copy.start()
    for head in range(width // HEAD_DIM):
        g, first = divmod(head * HEAD_DIM, block)
        if first == 0:
            copies[g].wait()
        lanes = slice(head * HEAD_DIM, (head + 1) * HEAD_DIM)
        product = scores_of(q_ref[:, lanes], weights_ref[g, :, first : first + HEAD_DIM])
        product = product.astype(out_ref.dtype)
        for c in range(span_count):
            out_ref[c, head * span : (head + 1) * span, :] = product[c * span : (c + 1) * span]


def cross_kernel(scale, position_ref, table_ref, *refs):
    *in_refs, asks_ref, out_ref = refs[:-6]
    rows_ref, all_asks_ref, means_ref, sems, ask_sems, mean_sems = refs[-6:]
    steps, span_count, asked, _ = all_asks_ref.shape
    rows = in_refs[0].shape[0]
    span = rows // span_count
    held = sum(ref.shape[0] for ref in in_refs) // rows // 2
    pieces = wanted_pieces(table_ref, position_ref[0], span_count, held)
    targets = [rows_ref.at[n * span : (n + 1) * span, :] for n in range(len(pieces))]
    for n, (index, half) in enumerate(pieces):
        fetch(in_refs, rows, index, half, targets[n], sems.at[n])
    ask_copies = [
        pltpu.make_async_copy(
            asks_ref.at[:, g * asked : (g + 1) * asked, :], all_asks_ref.at[g], ask_sems.at[g]
        )
        for g in range(steps)
    ]
    height = means_ref.shape[1]
    mean_copies = [
        pltpu.make_async_copy(
            means_ref.at[g], out_ref.at[g * height : (g + 1) * height, :], mean_sems.at[g]
        )
        for g in range(steps)
    ]
    for copy in ask_copies:
        copy.start()
    for n in range(len(pieces)):
        pltpu.make_async_copy(in_refs[0].at[0:span, :], targets[n], sems.at[n]).wait()

    keys_of_span = rows_ref.shape[0] // span_count
    slot = lax.broadcasted_iota(jnp.int32, (asked, keys_of_span), 1) // (2 * span)
    for g in range(steps):
        ask_copies[g].wait()
        for c in range(span_count):
            count = table_ref[c, 0] % 4
            keys = rows_ref[c * keys_of_span : (c + 1) * keys_of_span, :]
            s = jnp.where(slot < count, scores_of(all_asks_ref[g, c], keys), MASKED_SCORE)
            p = jnp.exp2((s - jnp.max(s, axis=1, keepdims=True)) * scale)
            inverse = jnp.where(count > 0, 1.0 / jnp.sum(p, axis=1, keepdims=True), 0.0)
            mean = jnp.dot(p.astype(jnp.bfloat16), keys, preferred_element_type=jnp.float32)
            mean = (mean * inverse).astype(jnp.bfloat16)
            for h in range(asked // span):
                place = h * rows + c * span
                means_ref[g, place : place + span, :] = mean[h * span : (h + 1) * span]
        mean_copies[g].start()
    for copy in mean_copies:
        copy.wait()


def values_kernel(means_ref, weight_ref, out_ref, all_means_ref, weights_ref, sems):
    rows, width = out_ref.shape
    steps, _, block = weights_ref.shape
    height = all_means_ref.shape[1]
    copies = [
        (
            pltpu.make_async_copy(
                means_ref.at[g * height : (g + 1) * height, :], all_means_ref.at[g], sems.at[0, g]
            ),
            pltpu.make_async_copy(
                weight_ref.at[:, width + g * block : width + (g + 1) * block],
                weights_ref.at[g],
                sems.at[1, g],
            ),
        )
        for g in range(steps)
    ]
    for pair in copies:
        for copy in pair:
            copy.start()
    for g in range(steps):
        for copy in copies[g]:
            copy.wait()
        for h in range(block // HEAD_DIM):
            inner = slice(h * HEAD_DIM, (h + 1) * HEAD_DIM)
            lanes = slice(g * block + h * HEAD_DIM, g * block + (h + 1) * HEAD_DIM)
            out_ref[:, lanes] = jnp.dot(
                all_means_ref[g, h * rows : (h + 1) * rows, :],
                weights_ref[g, :, inner],
                preferred_element_type=jnp.float32,
            )


def cross_attention(cross_queries, encoded, weight, counts, sources, position):
    rows, width = cross_queries.shape
    span_count = counts.shape[0]
    depth = encoded.shape[1]
    heads = width // HEAD_DIM
    place = position % PLANE
    one_back = shifted(encoded, "ctx", PLANE)
    table = sources * 4 + counts[:, None]
    before = shifted(table, "ctx", 1)
    table = jnp.concatenate([before[-1:], table[:-1]], axis=0)
    two_back = shifted(one_back, "ctx", PLANE)
    far = [swapped(jnp.concatenate([encoded, one_back, two_back], axis=0), "ctx", 1)]
    near = []
    for bit in (2, 4, 6):
        other = jnp.where(place < (place ^ bit), encoded, two_back)
        near.append(swapped(jnp.concatenate([one_back, other], axis=0), "ctx", bit))
        far.append(swapped(near[-1], "ctx", 1))

    held = [encoded, one_back, two_back, *near, *far]
    picked = span_count * 4 * SPAN
    pieces = picked // SPAN
    smem, anywhere = (pl.BlockSpec(memory_space=m) for m in (pltpu.SMEM, pl.ANY))
    vmem = pl.BlockSpec(memory_space=pltpu.VMEM)
    block = 4 * HEAD_DIM
    steps = width // block
    asks = pl.pallas_call(
        absorb_kernel,
        out_shape=jax.ShapeDtypeStruct((span_count, heads * SPAN, depth), jnp.bfloat16),
        in_specs=[vmem, anywhere],
        out_specs=vmem,
        scratch_shapes=[
            pltpu.VMEM((steps, depth, block), weight.dtype),
            pltpu.SemaphoreType.DMA((steps,)),
        ],
        cost_estimate=pl.CostEstimate(
            flops=2 * rows * depth * width, bytes_accessed=2 * weight.size, transcendentals=0
        ),
        name="absorb",
    )(cross_queries, weight)
    halves_of_heads = 2
    means = pl.pallas_call(
        functools.partial(cross_kernel, HEAD_DIM ** (-0.5) * LOG2E),
        out_shape=jax.ShapeDtypeStruct((heads * rows, depth), jnp.bfloat16),
        in_specs=[smem] * 2 + [anywhere] * (len(held) + 1),
        out_specs=anywhere,
        scratch_shapes=[
            pltpu.VMEM((picked, depth), encoded.dtype),
            pltpu.VMEM(
                (halves_of_heads, span_count, heads * SPAN // halves_of_heads, depth), asks.dtype
            ),
            pltpu.VMEM((halves_of_heads, heads * rows // halves_of_heads, depth), jnp.bfloat16),
            pltpu.SemaphoreType.DMA((pieces,)),
            pltpu.SemaphoreType.DMA((halves_of_heads,)),
            pltpu.SemaphoreType.DMA((halves_of_heads,)),
        ],
        cost_estimate=pl.CostEstimate(
            flops=4 * picked * depth * heads * SPAN,
            bytes_accessed=asks.size * 4 + picked * depth * 2,
            transcendentals=picked * SPAN * heads,
        ),
        name="cross",
    )(position.reshape(1), table, *held, asks)
    return pl.pallas_call(
        values_kernel,
        out_shape=jax.ShapeDtypeStruct((rows, width), jnp.float32),
        in_specs=[anywhere] * 2,
        out_specs=vmem,
        scratch_shapes=[
            pltpu.VMEM((steps, heads * rows // steps, depth), jnp.bfloat16),
            pltpu.VMEM((steps, depth, block), weight.dtype),
            pltpu.SemaphoreType.DMA((2, steps)),
        ],
        cost_estimate=pl.CostEstimate(
            flops=2 * rows * depth * width,
            bytes_accessed=weight.size + means.size * 2,
            transcendentals=0,
        ),
        name="values",
    )(means, weight)


def per_device(
    queries, self_keys, self_values, cross_queries, encoded, neighbour_weight, counts, sources
):
    position = lax.axis_index("ctx")
    count = lax.axis_size("ctx")
    groups = [list(range(first, first + HEADS)) for first in range(0, count, HEADS)]
    cross_part = cross_attention(
        cross_queries, encoded, neighbour_weight, counts, sources, position
    )
    by_head = self_attention(queries, self_keys, self_values, position // HEADS, groups)
    self_part = lax.all_to_all(by_head, "ctx", 0, 0, axis_index_groups=groups, tiled=True)
    self_part = jnp.moveaxis(self_part.astype(jnp.float32), 0, 1).reshape(queries.shape)
    return (self_part + cross_part).astype(jnp.bfloat16)


def solution(mesh):
    return jax.shard_map(
        per_device,
        mesh=mesh,
        in_specs=(
            P(("groups", "ctx"), None),
            P(("groups", "ctx"), None),
            P(("groups", "ctx"), None),
            P(("groups", "ctx"), None),
            P(("groups", "ctx"), None),
            P(),
            P(("groups", "ctx")),
            P(("groups", "ctx"), None),
        ),
        out_specs=P(("groups", "ctx"), None),
        check_vma=False,
    )
```

```python
import functools

import jax
import jax.numpy as jnp
from jax import lax
from jax.experimental import pallas as pl
from jax.experimental.pallas import tpu as pltpu
from jax.sharding import PartitionSpec as P


HEADS = 16
HEAD_DIM = 128
SPAN = 64
PLANE = 8
LEFT = 8

MASKED_SCORE = -1e30
LOG2E = 1.4426950408889634


def shifted(value, axis, steps):
    count = lax.axis_size(axis)
    first, last = (max(0, -steps), min(count, count - steps))
    return lax.ppermute(value, axis, [(source, source + steps) for source in range(first, last)])


def swapped(value, axis, bit):
    count = lax.axis_size(axis)
    return lax.ppermute(value, axis, [(source, source ^ bit) for source in range(count)])


def pack_kernel(*refs):
    *in_refs, out_ref = refs
    rows = in_refs[0].shape[0]
    for head in range(out_ref.shape[0]):
        columns = slice(head * HEAD_DIM, (head + 1) * HEAD_DIM)
        for n, ref in enumerate(in_refs):
            out_ref[head, n * rows : (n + 1) * rows, :] = ref[:, columns]


def packed(*arrays):
    rows, width = arrays[0].shape
    return pl.pallas_call(
        pack_kernel,
        out_shape=jax.ShapeDtypeStruct(
            (width // HEAD_DIM, len(arrays) * rows, HEAD_DIM), arrays[0].dtype
        ),
        cost_estimate=pl.CostEstimate(
            flops=0, bytes_accessed=4 * len(arrays) * rows * width, transcendentals=0
        ),
        name="pack",
    )(*arrays)


def scores_of(q, k):
    return lax.dot_general(q, k, (((1,), (1,)), ((), ())), preferred_element_type=jnp.float32)


def softmax_parts(q, pieces, scale, start=None):
    scores = []
    for k, _, mask in pieces:
        s = scores_of(q, k)
        scores.append(s if mask is None else jnp.where(mask, s, MASKED_SCORE))
    largest = functools.reduce(jnp.maximum, [jnp.max(s, axis=1, keepdims=True) for s in scores])
    total, out = None, None
    if start is not None:
        out, before, total = start
        largest = jnp.maximum(largest, before)
        weight = jnp.exp2((before - largest) * scale)
        out, total = out * weight, total * weight
    for s, (_, v, _) in zip(scores, pieces):
        p = jnp.exp2((s - largest) * scale)
        t = jnp.sum(p, axis=1, keepdims=True)
        o = jnp.dot(p.astype(jnp.bfloat16), v, preferred_element_type=jnp.float32)
        total = t if total is None else total + t
        out = o if out is None else out + o
    return out, largest, total


def with_stats(largest, total):
    lane = lax.broadcasted_iota(jnp.int32, (largest.shape[0], 128), 1)
    return jnp.where(lane < 64, largest, total)


def halves(stat):
    return stat[:, 0:1], stat[:, 64:65]


def thirds(x):
    high = x.astype(jnp.bfloat16)
    rest = x - high.astype(jnp.float32)
    middle = rest.astype(jnp.bfloat16)
    low = (rest - middle.astype(jnp.float32)).astype(jnp.bfloat16)
    return high, middle, low


def taken(ref, first, count, start, rows):
    return ref[first : first + count, start : start + rows, :].reshape(count * rows, ref.shape[2])


def triangle(size, keep):
    row = lax.broadcasted_iota(jnp.int32, (size, size), 0)
    column = lax.broadcasted_iota(jnp.int32, (size, size), 1)
    return keep(column, row)


def own_kernel(scale, q_ref, kv_ref, out_ref, stat_ref):
    blocks, rows, dim = q_ref.shape
    causal = triangle(2 * rows, lambda column, row: column <= row)
    for i in range(0, blocks, 2):
        spans = [(i, 2, causal)] + ([(0, i, None)] if i else [])
        pieces = [
            (taken(kv_ref, f, n, 0, rows), taken(kv_ref, f, n, rows, rows), mask)
            for f, n, mask in spans
        ]
        out, largest, total = softmax_parts(taken(q_ref, i, 2, 0, rows), pieces, scale)
        out_ref[i : i + 2] = out.reshape(2, rows, dim)
        stat_ref[i : i + 2] = with_stats(largest, total).reshape(2, rows, 128)


def later_kernel(scale, q_ref, kv_ref, out_ref):
    blocks, rows, dim = q_ref.shape
    later = triangle(2 * rows, lambda column, row: column > row)
    out_ref[blocks] = jnp.zeros((rows, dim), out_ref.dtype)
    for i in range(0, blocks, 2):
        spans = [(i, 2, later)] + ([(i + 2, blocks - i - 2, None)] if i + 2 < blocks else [])
        pieces = [
            (taken(kv_ref, f, n, 0, rows), taken(kv_ref, f, n, rows, rows), mask)
            for f, n, mask in spans
        ]
        out, largest, total = softmax_parts(taken(q_ref, i, 2, 0, rows), pieces, scale)
        out_ref[i : i + 2] = out.reshape(2, rows, dim).astype(out_ref.dtype)
        stat = with_stats(largest, total)
        for n in range(2):
            turned = stat[n * rows : (n + 1) * rows].T
            for m, row in enumerate((turned[0:1], turned[64:65])):
                for k, part in enumerate(thirds(row)):
                    place = ((i + n) * 2 + m) * 3 + k
                    out_ref[blocks, place : place + 1, :] = part


def sent_stats(ref, block, rows):
    values = []
    for m in range(2):
        place = (block * 2 + m) * 3
        three = ref[ref.shape[0] - 1, place : place + 3, :].astype(jnp.float32)
        values.append(three[0:1] + three[1:2] + three[2:3])
    sublane = lax.broadcasted_iota(jnp.int32, (rows, 128), 0)
    return jnp.where(sublane < 64, values[0], values[1]).T


def previous_kernel(scale, flag_ref, q_ref, kv_ref, out1_ref, stat1_ref, out_ref, part_ref, stat_ref):
    blocks, rows, dim = q_ref.shape
    waiting = part_ref.shape[0]
    later = triangle(2 * rows, lambda column, row: column > row)

    def own_part(i):
        stat = stat1_ref[i : i + 2].reshape(2 * rows, 128)
        return (out1_ref[i : i + 2].reshape(2 * rows, dim), *halves(stat))

    def finish(i, part):
        out, _, total = part
        out = out * (1.0 / total)
        out_ref[i : i + 2] = out.reshape(2, rows, dim).astype(out_ref.dtype)

    def store(i, part):
        if i >= waiting:
            return finish(i, part)
        out, largest, total = part
        part_ref[i : i + 2] = out.reshape(2, rows, dim)
        stat_ref[i : i + 2] = with_stats(largest, total).reshape(2, rows, 128)

    @pl.when(flag_ref[0] > 0)
    def _():
        for i in range(0, blocks, 2):
            first = max(i - waiting, 0)
            spans = [(first, 2, later)] if i >= waiting else []
            first += 2 * len(spans)
            if first < kv_ref.shape[0]:
                spans.append((first, kv_ref.shape[0] - first, None))
            pieces = [
                (taken(kv_ref, f, n, 0, rows), taken(kv_ref, f, n, rows, rows), mask)
                for f, n, mask in spans
            ]
            store(i, softmax_parts(taken(q_ref, i, 2, 0, rows), pieces, scale, own_part(i)))

    @pl.when(flag_ref[0] == 0)
    def _():
        for i in range(0, blocks, 2):
            finish(i, own_part(i))


def merge_kernel(scale, flag_ref, part_ref, stat_ref, back_ref, rest_ref, out_ref, done_ref, sem):
    del rest_ref
    blocks, rows, dim = part_ref.shape

    @pl.when(flag_ref[0] > 0)
    def _():
        for i in range(0, blocks, 2):
            out1, largest1, total1 = (
                part_ref[i : i + 2].reshape(2 * rows, dim),
                *halves(stat_ref[i : i + 2].reshape(2 * rows, 128)),
            )
            stat = jnp.concatenate([sent_stats(back_ref, i + n, rows) for n in range(2)], axis=0)
            largest2, total2 = halves(stat)
            top = jnp.maximum(largest1, largest2)
            a, b = jnp.exp2((largest1 - top) * scale), jnp.exp2((largest2 - top) * scale)
            inverse = 1.0 / (a * total1 + b * total2)
            out2 = taken(back_ref, i, 2, 0, rows).astype(jnp.float32)
            out = out1 * (a * inverse) + out2 * (b * inverse)
            done_ref[i : i + 2] = out.reshape(2, rows, dim).astype(done_ref.dtype)
        copy = pltpu.make_async_copy(done_ref, out_ref.at[0:blocks], sem)
        copy.start()
        copy.wait()


def estimate(area, arrays):
    return pl.CostEstimate(
        flops=4 * HEAD_DIM * area,
        bytes_accessed=sum(2 * a.size for a in arrays),
        transcendentals=area,
    )


def self_attention(queries, keys, values, chunk, groups):
    rows, width = queries.shape
    heads = width // HEAD_DIM
    scale = HEAD_DIM ** (-0.5) * LOG2E
    kv = lax.all_to_all(
        packed(keys, values), "ctx", 0, 0, axis_index_groups=groups, tiled=True
    )
    arriving = shifted(kv[LEFT:], "ctx", heads)
    q = lax.all_to_all(packed(queries), "ctx", 0, 0, axis_index_groups=groups, tiled=True)
    asked = shifted(q[:LEFT], "ctx", -heads)
    area = (heads * rows) ** 2 // 2
    small = (LEFT * rows) ** 2 // 2
    out1, stat = pl.pallas_call(
        functools.partial(own_kernel, scale),
        out_shape=(
            jax.ShapeDtypeStruct((heads, rows, HEAD_DIM), jnp.float32),
            jax.ShapeDtypeStruct((heads, rows, 128), jnp.float32),
        ),
        cost_estimate=estimate(area, (q, kv)),
        name="own",
    )(q, kv)
    smem = pl.BlockSpec(memory_space=pltpu.SMEM)

    def first_blocks(count, height):
        return pl.BlockSpec((count, height, HEAD_DIM), lambda *_: (0, 0, 0))

    answer = pl.pallas_call(
        functools.partial(later_kernel, scale),
        out_shape=jax.ShapeDtypeStruct((LEFT + 1, rows, HEAD_DIM), jnp.bfloat16),
        grid=(1,),
        in_specs=[first_blocks(LEFT, rows), first_blocks(LEFT, 2 * rows)],
        out_specs=first_blocks(LEFT + 1, rows),
        cost_estimate=estimate(small, (asked,)),
        name="later",
    )(asked, kv)
    back = shifted(answer, "ctx", heads)
    flag = chunk.reshape(1)
    all_blocks = first_blocks(heads, rows)
    rest, part, stat = pl.pallas_call(
        functools.partial(previous_kernel, scale),
        out_shape=(
            jax.ShapeDtypeStruct((heads, rows, HEAD_DIM), jnp.bfloat16),
            jax.ShapeDtypeStruct((LEFT, rows, HEAD_DIM), jnp.float32),
            jax.ShapeDtypeStruct((LEFT, rows, 128), jnp.float32),
        ),
        grid=(1,),
        in_specs=[smem, all_blocks, first_blocks(heads - LEFT, 2 * rows), all_blocks, all_blocks],
        out_specs=(all_blocks, first_blocks(LEFT, rows), first_blocks(LEFT, rows)),
        cost_estimate=estimate(area - small, (q, kv, out1, stat)),
        name="previous",
    )(flag, q, arriving, out1, stat)
    vmem, anywhere = (pl.BlockSpec(memory_space=m) for m in (pltpu.VMEM, pl.ANY))
    return pl.pallas_call(
        functools.partial(merge_kernel, scale),
        out_shape=jax.ShapeDtypeStruct(rest.shape, rest.dtype),
        in_specs=[smem, vmem, vmem, vmem, anywhere],
        out_specs=anywhere,
        input_output_aliases={4: 0},
        scratch_shapes=[
            pltpu.VMEM((LEFT, rows, HEAD_DIM), rest.dtype),
            pltpu.SemaphoreType.DMA(()),
        ],
        cost_estimate=estimate(0, (part, stat, back)),
        name="merge",
    )(flag, part, stat, back, rest)


def wanted_pieces(table_ref, position, span_count, held):
    pieces = []
    place, plane = position % PLANE, position // PLANE
    for c in range(span_count):
        for slot in range(2):
            source = table_ref[c, slot] // 4
            for later in range(2):
                block = (source + later) // span_count
                relative = (block % PLANE) ^ place
                away = plane - block // PLANE
                column = relative // 2
                index = jnp.where(column == 0, away, 1 + 2 * column + jnp.where(away == 1, 0, 1))
                index = jnp.clip(index, 0, held - 1) + held * (relative % 2)
                pieces.append((index, (source + later) % span_count))
    return pieces


def fetch(refs, rows, index, half, target, sem):
    size = target.shape[0]
    first = 0
    for ref in refs:
        count = ref.shape[0] // rows

        @pl.when((index >= first) & (index < first + count))
        def _(ref=ref, first=first):
            start = pl.multiple_of((index - first) * rows + half * size, size)
            pltpu.make_async_copy(ref.at[pl.ds(start, size), :], target, sem).start()

        first += count


def absorb_kernel(q_ref, weight_ref, out_ref, weights_ref, sems):
    rows, width = q_ref.shape
    span_count = out_ref.shape[0]
    span = rows // span_count
    steps, _, block = weights_ref.shape
    copies = [
        pltpu.make_async_copy(
            weight_ref.at[:, g * block : (g + 1) * block], weights_ref.at[g], sems.at[g]
        )
        for g in range(steps)
    ]
    for copy in copies:
        copy.start()
    for head in range(width // HEAD_DIM):
        g, first = divmod(head * HEAD_DIM, block)
        if first == 0:
            copies[g].wait()
        lanes = slice(head * HEAD_DIM, (head + 1) * HEAD_DIM)
        product = scores_of(q_ref[:, lanes], weights_ref[g, :, first : first + HEAD_DIM])
        product = product.astype(out_ref.dtype)
        for c in range(span_count):
            out_ref[c, head * span : (head + 1) * span, :] = product[c * span : (c + 1) * span]


def cross_kernel(scale, position_ref, table_ref, *refs):
    *in_refs, asks_ref, out_ref = refs[:-6]
    rows_ref, all_asks_ref, means_ref, sems, ask_sems, mean_sems = refs[-6:]
    steps, span_count, asked, _ = all_asks_ref.shape
    rows = in_refs[0].shape[0]
    span = rows // span_count
    held = sum(ref.shape[0] for ref in in_refs) // rows // 2
    pieces = wanted_pieces(table_ref, position_ref[0], span_count, held)
    targets = [rows_ref.at[n * span : (n + 1) * span, :] for n in range(len(pieces))]
    for n, (index, half) in enumerate(pieces):
        fetch(in_refs, rows, index, half, targets[n], sems.at[n])
    ask_copies = [
        pltpu.make_async_copy(
            asks_ref.at[:, g * asked : (g + 1) * asked, :], all_asks_ref.at[g], ask_sems.at[g]
        )
        for g in range(steps)
    ]
    height = means_ref.shape[1]
    mean_copies = [
        pltpu.make_async_copy(
            means_ref.at[g], out_ref.at[g * height : (g + 1) * height, :], mean_sems.at[g]
        )
        for g in range(steps)
    ]
    for copy in ask_copies:
        copy.start()
    for n in range(len(pieces)):
        pltpu.make_async_copy(in_refs[0].at[0:span, :], targets[n], sems.at[n]).wait()

    keys_of_span = rows_ref.shape[0] // span_count
    slot = lax.broadcasted_iota(jnp.int32, (asked, keys_of_span), 1) // (2 * span)
    for g in range(steps):
        ask_copies[g].wait()
        for c in range(span_count):
            count = table_ref[c, 0] % 4
            keys = rows_ref[c * keys_of_span : (c + 1) * keys_of_span, :]
            s = jnp.where(slot < count, scores_of(all_asks_ref[g, c], keys), MASKED_SCORE)
            p = jnp.exp2((s - jnp.max(s, axis=1, keepdims=True)) * scale)
            inverse = jnp.where(count > 0, 1.0 / jnp.sum(p, axis=1, keepdims=True), 0.0)
            mean = jnp.dot(p.astype(jnp.bfloat16), keys, preferred_element_type=jnp.float32)
            mean = (mean * inverse).astype(jnp.bfloat16)
            for h in range(asked // span):
                place = h * rows + c * span
                means_ref[g, place : place + span, :] = mean[h * span : (h + 1) * span]
        mean_copies[g].start()
    for copy in mean_copies:
        copy.wait()


def values_kernel(means_ref, weight_ref, out_ref, all_means_ref, weights_ref, sems):
    rows, width = out_ref.shape
    steps, _, block = weights_ref.shape
    height = all_means_ref.shape[1]
    copies = [
        (
            pltpu.make_async_copy(
                means_ref.at[g * height : (g + 1) * height, :], all_means_ref.at[g], sems.at[0, g]
            ),
            pltpu.make_async_copy(
                weight_ref.at[:, width + g * block : width + (g + 1) * block],
                weights_ref.at[g],
                sems.at[1, g],
            ),
        )
        for g in range(steps)
    ]
    for pair in copies:
        for copy in pair:
            copy.start()
    for g in range(steps):
        for copy in copies[g]:
            copy.wait()
        for h in range(block // HEAD_DIM):
            inner = slice(h * HEAD_DIM, (h + 1) * HEAD_DIM)
            lanes = slice(g * block + h * HEAD_DIM, g * block + (h + 1) * HEAD_DIM)
            out_ref[:, lanes] = jnp.dot(
                all_means_ref[g, h * rows : (h + 1) * rows, :],
                weights_ref[g, :, inner],
                preferred_element_type=jnp.float32,
            )


def cross_attention(cross_queries, encoded, weight, counts, sources, position):
    rows, width = cross_queries.shape
    span_count = counts.shape[0]
    depth = encoded.shape[1]
    heads = width // HEAD_DIM
    place = position % PLANE
    one_back = shifted(encoded, "ctx", PLANE)
    table = sources * 4 + counts[:, None]
    before = shifted(table, "ctx", 1)
    table = jnp.concatenate([before[-1:], table[:-1]], axis=0)
    two_back = shifted(one_back, "ctx", PLANE)
    far = [swapped(jnp.concatenate([encoded, one_back, two_back], axis=0), "ctx", 1)]
    near = []
    for bit in (2, 4, 6):
        other = jnp.where(place < (place ^ bit), encoded, two_back)
        near.append(swapped(jnp.concatenate([one_back, other], axis=0), "ctx", bit))
        far.append(swapped(near[-1], "ctx", 1))

    held = [encoded, one_back, two_back, *near, *far]
    picked = span_count * 4 * SPAN
    pieces = picked // SPAN
    smem, anywhere = (pl.BlockSpec(memory_space=m) for m in (pltpu.SMEM, pl.ANY))
    vmem = pl.BlockSpec(memory_space=pltpu.VMEM)
    block = 4 * HEAD_DIM
    steps = width // block
    asks = pl.pallas_call(
        absorb_kernel,
        out_shape=jax.ShapeDtypeStruct((span_count, heads * SPAN, depth), jnp.bfloat16),
        in_specs=[vmem, anywhere],
        out_specs=vmem,
        scratch_shapes=[
            pltpu.VMEM((steps, depth, block), weight.dtype),
            pltpu.SemaphoreType.DMA((steps,)),
        ],
        cost_estimate=pl.CostEstimate(
            flops=2 * rows * depth * width, bytes_accessed=2 * weight.size, transcendentals=0
        ),
        name="absorb",
    )(cross_queries, weight)
    halves_of_heads = 2
    means = pl.pallas_call(
        functools.partial(cross_kernel, HEAD_DIM ** (-0.5) * LOG2E),
        out_shape=jax.ShapeDtypeStruct((heads * rows, depth), jnp.bfloat16),
        in_specs=[smem] * 2 + [anywhere] * (len(held) + 1),
        out_specs=anywhere,
        scratch_shapes=[
            pltpu.VMEM((picked, depth), encoded.dtype),
            pltpu.VMEM(
                (halves_of_heads, span_count, heads * SPAN // halves_of_heads, depth), asks.dtype
            ),
            pltpu.VMEM((halves_of_heads, heads * rows // halves_of_heads, depth), jnp.bfloat16),
            pltpu.SemaphoreType.DMA((pieces,)),
            pltpu.SemaphoreType.DMA((halves_of_heads,)),
            pltpu.SemaphoreType.DMA((halves_of_heads,)),
        ],
        cost_estimate=pl.CostEstimate(
            flops=4 * picked * depth * heads * SPAN,
            bytes_accessed=asks.size * 4 + picked * depth * 2,
            transcendentals=picked * SPAN * heads,
        ),
        name="cross",
    )(position.reshape(1), table, *held, asks)
    return pl.pallas_call(
        values_kernel,
        out_shape=jax.ShapeDtypeStruct((rows, width), jnp.float32),
        in_specs=[anywhere] * 2,
        out_specs=vmem,
        scratch_shapes=[
            pltpu.VMEM((steps, heads * rows // steps, depth), jnp.bfloat16),
            pltpu.VMEM((steps, depth, block), weight.dtype),
            pltpu.SemaphoreType.DMA((2, steps)),
        ],
        cost_estimate=pl.CostEstimate(
            flops=2 * rows * depth * width,
            bytes_accessed=weight.size + means.size * 2,
            transcendentals=0,
        ),
        name="values",
    )(means, weight)


def per_device(
    queries, self_keys, self_values, cross_queries, encoded, neighbour_weight, counts, sources
):
    position = lax.axis_index("ctx")
    count = lax.axis_size("ctx")
    groups = [list(range(first, first + HEADS)) for first in range(0, count, HEADS)]
    cross_part = cross_attention(
        cross_queries, encoded, neighbour_weight, counts, sources, position
    )
    by_head = self_attention(queries, self_keys, self_values, position // HEADS, groups)
    self_part = lax.all_to_all(by_head, "ctx", 0, 0, axis_index_groups=groups, tiled=True)
    self_part = jnp.moveaxis(self_part.astype(jnp.float32), 0, 1).reshape(queries.shape)
    return (self_part + cross_part).astype(jnp.bfloat16)


def solution(mesh):
    return jax.shard_map(
        per_device,
        mesh=mesh,
        in_specs=(
            P(("groups", "ctx"), None),
            P(("groups", "ctx"), None),
            P(("groups", "ctx"), None),
            P(("groups", "ctx"), None),
            P(("groups", "ctx"), None),
            P(),
            P(("groups", "ctx")),
            P(("groups", "ctx"), None),
        ),
        out_specs=P(("groups", "ctx"), None),
        check_vma=False,
    )
```
